512 devices in a mesh: view: 64 (over y, z), chord: 8 (over x, core).
Axes of the slice: x: 4, y: 8, z: 8, core: 2. Of those that a mesh axis runs over, the one named last changes fastest.
Arguments:
- proj: bfloat16 [768, 4096, 128], P('view', 'chord'), may hold values from -16 to 16
- tiles: bfloat16 [384, 256, 1024], P('view'), may hold values from -0.01953125 to 0.01953125
- owner: int32 [8, 512], replicated, may hold values from 0 to 511, as said below
- lengths: int32 [8, 512], replicated, may hold values from 1 to 1024, as said below
Outputs:
- recon: float32 [8, 512, 1024], P('chord', 'view')
The draws below stay inside these ranges and needn't reach their ends.
Inputs may be any that keep to these rules, and one draw needn't show every extreme that they name: `owner`: each row is an ordering of the 512 chords of one group. In each group, the lengths of the chords at owner positions k * 8 to k * 8 + 7 sum to at most 4608, exactly 4608 for some k; the largest entry of each row is 1024.
All inputs are finite; a program needn't handle non-finite values.
Results may differ from the reference program's by a relative error of at most 0.0003.
Values sent between devices are 32-bit elements; how exact they have to be, the bound alone decides.
A program may use at most 64 MiB of HBM per device.

```python
import math
import jax
import jax.numpy as jnp
from jax import lax

S = 1024
DW = 128
VB = 2
CHD = 8
PACK = 4608
VIEWS = 768
CH_GRP = 512
GROUPS = 8
CHORDS = 4096


def chord_layout(key):
    base = jax.random.fold_in(key, 11)
    perm_keys = jax.random.split(jax.random.fold_in(base, 1), GROUPS)
    owner = jax.vmap(lambda k: jax.random.permutation(k, CH_GRP))(perm_keys).astype(jnp.int32)
    first = jax.random.randint(jax.random.fold_in(base, 2), (GROUPS, CH_GRP), 0, S, dtype=jnp.int32)
    second = jax.random.randint(jax.random.fold_in(base, 3), (GROUPS, CH_GRP), 0, S, dtype=jnp.int32)
    raw = 1 + first * second // S
    owners = CH_GRP // CHD
    blocks = raw.reshape(GROUPS, owners, CHD)
    total = jnp.sum(blocks, axis=2, keepdims=True)
    room = PACK - CHD
    scaled = 1 + (blocks - 1) * room // jnp.maximum(total - CHD, room)
    pick = jax.random.randint(jax.random.fold_in(base, 4), (GROUPS, 1, 1), 0, owners, dtype=jnp.int32)
    full = jnp.where(jnp.arange(CHD, dtype=jnp.int32) == 0, S, S // 2).astype(jnp.int32)[None, None, :]
    chosen = jnp.arange(owners, dtype=jnp.int32)[None, :, None] == pick
    ordered = jnp.where(chosen, full, scaled).astype(jnp.int32).reshape(GROUPS, CH_GRP)
    rows = jnp.arange(GROUPS, dtype=jnp.int32)[:, None]
    lengths = jnp.zeros((GROUPS, CH_GRP), jnp.int32).at[rows, owner].set(ordered)
    return (owner, lengths)


def draw_owner(key, part):
    return chord_layout(key)[0]


def draw_lengths(key, part):
    return chord_layout(key)[1]


def with_spikes(drawn, key, source, target, shards_of, factor):
    owner, partner = [(jnp.arange(drawn.shape[axis_at]) // (drawn.shape[axis_at] // shards_of)).reshape([-1 if axis == axis_at else 1 for axis in range(drawn.ndim)]) for axis_at in (source, target)]
    chosen = jax.random.permutation(key, shards_of)[partner]
    strong = (owner == chosen) | (owner == (partner + shards_of // 2) % shards_of)
    return jnp.where(strong, factor * drawn, drawn)


def block_levels(key, shape, cuts, low, high):
    def one(dim, shards_of):
        steps = jax.random.uniform(jax.random.fold_in(jax.random.fold_in(key, 6), dim), (shards_of,), jnp.float32, low / len(cuts), high / len(cuts))
        return jnp.repeat(jnp.exp(steps), shape[dim] // shards_of).reshape((-1,) + (1,) * (len(shape) - dim - 1))

    gain = one(*cuts[0])
    for cut in cuts[1:]:
        gain = gain * one(*cut)
    return gain


def gaussian(key, dims, spread, bound, shards=(), kind=jnp.bfloat16):
    level = block_levels(key, dims, shards, -0.22, 0.18) if shards else 1.0
    values = jax.random.normal(key, dims, jnp.float32) * spread * level
    return jnp.minimum(jnp.maximum(values, -bound), bound).astype(kind)


def noise_with(rng, shape, deviation, most, shards, heavy, held_as=jnp.bfloat16):
    result = deviation * jax.random.normal(rng, shape, jnp.float32)
    if shards:
        result = result * block_levels(rng, shape, shards, -0.22, 0.18)
    return jnp.clip(with_spikes(result, jax.random.fold_in(rng, 3), *heavy), -most, most).astype(held_as)


def setup_inputs(seed: int = 0) -> dict:
    splits = jax.random.split(jax.random.key(seed), 5)
    return {
        "proj": noise_with(splits[0], (VIEWS, CHORDS, DW), 1.0, 16.0, ((0, 64), (1, 8)), (0, 1, 64, 4.0)),
        "tiles": gaussian(splits[1], (VIEWS // VB, VB * DW, S), (VIEWS * DW) ** -0.5, 0.01953125, ((0, 64),)),
        "owner": draw_owner(jax.random.fold_in(splits[4], 71), 0),
        "lengths": draw_lengths(jax.random.fold_in(splits[4], 71), 0),
    }


def kernel_table(rows, start, cols):
    row_pos = start + jnp.arange(rows, dtype=jnp.float32)[:, None]
    col_pos = jnp.arange(cols, dtype=jnp.float32)[None, :]
    return 1.0 / (row_pos - col_pos + 0.5)

def weigh(length, count, start):
    position = start + jnp.arange(count, dtype=jnp.float32)[None, :] + 0.5
    inside = position < length
    return (inside, jnp.sqrt(jnp.where(inside, position * (length - position), 1.0)))

def invert_block(sums, length, table, start):
    length = length.astype(jnp.float32)[:, None]
    col_in, col_w = weigh(length, sums.shape[1], 0.0)
    row_in, row_w = weigh(length, table.shape[0], start)
    scaled = jnp.where(col_in, col_w * sums, 0.0)
    image = jnp.dot(scaled, table.T, precision=lax.Precision.HIGHEST, preferred_element_type=jnp.float32)
    return jnp.where(row_in, image / (math.pi * row_w), 0.0)

def reference(proj, tiles, owner, lengths):
    block_data = proj.reshape(VIEWS // VB, VB, CHORDS, DW)
    tile_stack = tiles.reshape(VIEWS // VB, VB, DW, S)

    def step(total, inputs):
        views_now, tile = inputs
        term = jnp.einsum('vkd,vds->ks', views_now.astype(jnp.float32), tile.astype(jnp.float32), precision=lax.Precision.HIGHEST)
        return (total + term, None)
    sums, _ = lax.scan(step, jnp.zeros((CHORDS, S), jnp.float32), (block_data, tile_stack))
    grouped = sums.reshape(GROUPS, CH_GRP, S)
    ordered = jnp.take_along_axis(grouped, owner[:, :, None], axis=1)
    ordered_len = jnp.take_along_axis(lengths, owner, axis=1)
    table = kernel_table(S, 0.0, S)
    recon = invert_block(ordered.reshape(CHORDS, S), ordered_len.reshape(CHORDS), table, 0.0)
    return recon.reshape(GROUPS, CH_GRP, S)
```

```python
import math

import jax
import jax.numpy as jnp
from jax import lax
from jax.sharding import PartitionSpec as P

LANES = 128
PACK = 4608


def kernel_table(rows, start, cols):
    row_pos = start + jnp.arange(rows, dtype=jnp.float32)[:, None]
    col_pos = jnp.arange(cols, dtype=jnp.float32)[None, :]
    return 1.0 / (row_pos - col_pos + 0.5)


def weigh(length, count, start):
    position = start + jnp.arange(count, dtype=jnp.float32)[None, :] + 0.5
    inside = position < length
    return (inside, jnp.sqrt(jnp.where(inside, position * (length - position), 1.0)))


def invert_block(sums, length, table, start):
    length = length.astype(jnp.float32)[:, None]
    col_in, col_w = weigh(length, sums.shape[1], 0.0)
    row_in, row_w = weigh(length, table.shape[0], start)
    scaled = jnp.where(col_in, col_w * sums, 0.0)
    image = jnp.dot(
        scaled, table.T, precision=lax.Precision.HIGHEST, preferred_element_type=jnp.float32
    )
    return jnp.where(row_in, image / (math.pi * row_w), 0.0)


def chunk_plan(order_len, per_owner, chunks_per_row, slots):
    counts = (order_len + LANES - 1) // LANES
    ends = jnp.cumsum(counts, axis=1)
    starts = ends - counts
    slot = jnp.arange(slots, dtype=jnp.int32)
    member = jnp.sum(ends[:, None, :] <= slot[None, :, None], axis=2)
    member = jnp.minimum(member, per_owner - 1)
    first = jnp.take_along_axis(starts, member, axis=1)
    within = jnp.clip(slot[None, :] - first, 0, chunks_per_row - 1)
    return starts, member, within


def per_device(proj, tiles, owner, lengths):
    view_count, group_rows, footprint = proj.shape
    samples = tiles.shape[2]
    group = lax.axis_index("chord")
    view_place = lax.axis_index("view")
    view_devices = lax.axis_size("view")
    owned = group_rows // view_devices
    chunks_per_row = samples // LANES
    slots = min(chunks_per_row * owned, (PACK + owned * (LANES - 1)) // LANES)

    tile_rows = tiles.reshape(view_count, footprint, samples)
    sums = jnp.einsum("vkd,vds->ks", proj, tile_rows, preferred_element_type=jnp.float32)

    my_order = lax.dynamic_index_in_dim(owner, group, 0, keepdims=False)
    my_lengths = lax.dynamic_index_in_dim(lengths, group, 0, keepdims=False)
    order_len = jnp.take(my_lengths, my_order).reshape(view_devices, owned)
    order_rows = my_order.reshape(view_devices, owned)
    starts, member, within = chunk_plan(order_len, owned, chunks_per_row, slots)
    src_row = jnp.take_along_axis(order_rows, member, axis=1)
    src = src_row * chunks_per_row + within
    flat = sums.reshape(group_rows * chunks_per_row, LANES)
    packed = jnp.take(flat, src.reshape(-1), axis=0).reshape(view_devices, slots, LANES)

    mine = lax.psum_scatter(packed, "view", scatter_dimension=0, tiled=True)[0]

    my_starts = lax.dynamic_index_in_dim(starts, view_place, 0, keepdims=False)
    my_len = lax.dynamic_index_in_dim(order_len, view_place, 0, keepdims=False)
    back = my_starts[:, None] + jnp.arange(chunks_per_row, dtype=jnp.int32)[None, :]
    back = jnp.minimum(back, slots - 1)
    rows = jnp.take(mine, back.reshape(-1), axis=0).reshape(owned, samples)

    table = kernel_table(samples, 0.0, samples)
    recon = invert_block(rows, my_len, table, 0.0)
    return recon[None]


def solution(mesh):
    placed = (P("view", "chord", None), P("view", None, None), P(), P())
    return jax.shard_map(
        per_device, mesh=mesh, in_specs=placed, out_specs=P("chord", "view", None), check_vma=False
    )
```

```python
import functools
import math

import jax
import jax.numpy as jnp
from jax import lax
from jax.experimental import pallas as pl
from jax.experimental.pallas import tpu as pltpu
from jax.sharding import PartitionSpec as P

LANES = 128
PACK = 4608
MESH = pl.DeviceIdType.MESH


def kernel_table(rows, start, cols):
    row_pos = start + jnp.arange(rows, dtype=jnp.float32)[:, None]
    col_pos = jnp.arange(cols, dtype=jnp.float32)[None, :]
    return 1.0 / (row_pos - col_pos + 0.5)


def weigh(length, count, start):
    position = start + jnp.arange(count, dtype=jnp.float32)[None, :] + 0.5
    inside = position < length
    return (inside, jnp.sqrt(jnp.where(inside, position * (length - position), 1.0)))


def invert_block(sums, length, table, start):
    length = length.astype(jnp.float32)[:, None]
    col_in, col_w = weigh(length, sums.shape[1], 0.0)
    row_in, row_w = weigh(length, table.shape[0], start)
    scaled = jnp.where(col_in, col_w * sums, 0.0)
    image = jnp.dot(
        scaled, table.T, precision=lax.Precision.HIGHEST, preferred_element_type=jnp.float32
    )
    return jnp.where(row_in, image / (math.pi * row_w), 0.0)


def pick(table, index):
    hit = index[:, :, None] == jnp.arange(table.shape[1], dtype=jnp.int32)
    return jnp.sum(jnp.where(hit, table[:, None, :], 0), axis=-1)


def ring_phase(n, me, send_right, send_left, chunk, own, recv_r, recv_l, send_r, send_l, ssem, rsem, base):
    nr = n // 2
    nl = n - 1 - nr
    for s in range(max(nr, nl)):
        copies = []
        for go, steps, to, recv, send, sem in (
            (1, nr, send_right, recv_r, send_r, base + s),
            (-1, nl, send_left, recv_l, send_l, base + nr + s),
        ):
            if s >= steps:
                continue
            dest = lax.rem(me + go * (steps - s) + 2 * n, n)
            if s == 0:
                src = chunk(dest)
            else:
                send[s] = recv[s - 1] + own(dest)
                src = send.at[s]
            copy = pltpu.make_async_remote_copy(
                src_ref=src,
                dst_ref=recv.at[s],
                send_sem=ssem.at[sem],
                recv_sem=rsem.at[sem],
                device_id=to,
                device_id_type=MESH,
            )
            copy.start()
            copies.append(copy)
        for copy in copies:
            copy.wait()
    return recv_r.at[nr - 1], recv_l.at[nl - 1]


def rs_kernel(ny, nz, x_ref, o_ref, s1, rr1, rl1, sr1, sl1, rr2, rl2, sr2, sl2, ssem, rsem):
    view = lax.axis_index("view")
    group = lax.axis_index("chord")
    y = view // nz
    z = lax.rem(view, nz)

    def dev(yy, zz):
        return (yy * nz + zz, group)

    z_right = dev(y, lax.rem(z + 1, nz))
    z_left = dev(y, lax.rem(z + nz - 1, nz))
    y_right = dev(lax.rem(y + 1, ny), z)
    y_left = dev(lax.rem(y + ny - 1, ny), z)

    barrier = pltpu.get_barrier_semaphore()
    for peer in (z_right, z_left, y_right, y_left):
        pl.semaphore_signal(barrier, inc=1, device_id=peer, device_id_type=MESH)
    pl.semaphore_wait(barrier, 4)

    fin_r, fin_l = ring_phase(
        nz, z, z_right, z_left,
        lambda d: x_ref.at[d], lambda d: x_ref[d],
        rr1, rl1, sr1, sl1, ssem, rsem, 0,
    )
    s1[...] = x_ref[z] + fin_r[...] + fin_l[...]
    fin_r, fin_l = ring_phase(
        ny, y, y_right, y_left,
        lambda d: s1.at[d], lambda d: s1[d],
        rr2, rl2, sr2, sl2, ssem, rsem, nz - 1,
    )
    o_ref[...] = s1[y] + fin_r[...] + fin_l[...]


def reduce_scatter(packed, ny, nz):
    rows = packed.shape[2]
    nr1, nl1 = nz // 2, nz - 1 - nz // 2
    nr2, nl2 = ny // 2, ny - 1 - ny // 2
    block = (rows, LANES)
    f32 = jnp.float32
    return pl.pallas_call(
        functools.partial(rs_kernel, ny, nz),
        out_shape=jax.ShapeDtypeStruct(block, f32),
        in_specs=[pl.BlockSpec(memory_space=pltpu.VMEM)],
        out_specs=pl.BlockSpec(memory_space=pltpu.VMEM),
        scratch_shapes=[
            pltpu.VMEM((ny,) + block, f32),
            pltpu.VMEM((nr1, ny) + block, f32),
            pltpu.VMEM((nl1, ny) + block, f32),
            pltpu.VMEM((nr1, ny) + block, f32),
            pltpu.VMEM((nl1, ny) + block, f32),
            pltpu.VMEM((nr2,) + block, f32),
            pltpu.VMEM((nl2,) + block, f32),
            pltpu.VMEM((nr2,) + block, f32),
            pltpu.VMEM((nl2,) + block, f32),
            pltpu.SemaphoreType.DMA((nz + ny - 2,)),
            pltpu.SemaphoreType.DMA((nz + ny - 2,)),
        ],
        compiler_params=pltpu.CompilerParams(collective_id=0, has_side_effects=True),
    )(packed)


def per_device(ny, nz, proj, tiles, owner, lengths):
    view_count, group_rows, footprint = proj.shape
    samples = tiles.shape[2]
    group = lax.axis_index("chord")
    view_place = lax.axis_index("view")
    view_devices = ny * nz
    owned = group_rows // view_devices
    chunks_per_row = samples // LANES
    slots = min(chunks_per_row * owned, (PACK + owned * (LANES - 1)) // LANES)

    tile_rows = tiles.reshape(view_count, footprint, samples)
    sums = jnp.einsum("vkd,vds->ks", proj, tile_rows, preferred_element_type=jnp.float32)

    my_order = lax.dynamic_index_in_dim(owner, group, 0, keepdims=False)
    my_lengths = lax.dynamic_index_in_dim(lengths, group, 0, keepdims=False)
    order_len = pick(my_lengths[None, :], my_order[None, :])
    order_len = order_len.reshape(view_devices, owned)
    order_rows = my_order.reshape(view_devices, owned)

    counts = (order_len + LANES - 1) // LANES
    ends = jnp.cumsum(counts, axis=1)
    starts = ends - counts
    slot = jnp.arange(slots, dtype=jnp.int32)
    member = jnp.sum((ends[:, None, :] <= slot[None, :, None]).astype(jnp.int32), axis=2)
    member = jnp.minimum(member, owned - 1)
    first = pick(starts, member)
    src_row = pick(order_rows, member)
    within = jnp.clip(slot[None, :] - first, 0, chunks_per_row - 1)
    src = src_row * chunks_per_row + within
    src = src.reshape(ny, nz, slots).transpose(1, 0, 2)
    flat = sums.reshape(group_rows * chunks_per_row, LANES)
    packed = jnp.take(flat, src.reshape(-1), axis=0).reshape(nz, ny, slots, LANES)

    mine = reduce_scatter(packed, ny, nz)

    my_starts = lax.dynamic_index_in_dim(starts, view_place, 0, keepdims=False)
    my_len = lax.dynamic_index_in_dim(order_len, view_place, 0, keepdims=False)
    back = my_starts[:, None] + jnp.arange(chunks_per_row, dtype=jnp.int32)[None, :]
    back = jnp.minimum(back, slots - 1)
    rows = jnp.take(mine, back.reshape(-1), axis=0).reshape(owned, samples)

    table = kernel_table(samples, 0.0, samples)
    recon = invert_block(rows, my_len, table, 0.0)
    return recon[None]


def solution(mesh):
    view_devices = mesh.shape["view"]
    ny = int(round(math.sqrt(view_devices)))
    nz = view_devices // ny
    placed = (P("view", "chord", None), P("view", None, None), P(), P())
    return jax.shard_map(
        functools.partial(per_device, ny, nz),
        mesh=mesh,
        in_specs=placed,
        out_specs=P("chord", "view", None),
        check_vma=False,
    )
```

```python
import functools
import math

import jax
import jax.numpy as jnp
from jax import lax
from jax.experimental import pallas as pl
from jax.experimental.pallas import tpu as pltpu
from jax.sharding import PartitionSpec as P

LANES = 128
PACK = 4608
MESH = pl.DeviceIdType.MESH


def kernel_table(rows, start, cols):
    row_pos = start + jnp.arange(rows, dtype=jnp.float32)[:, None]
    col_pos = jnp.arange(cols, dtype=jnp.float32)[None, :]
    return 1.0 / (row_pos - col_pos + 0.5)


def weigh(length, count, start):
    position = start + jnp.arange(count, dtype=jnp.float32)[None, :] + 0.5
    inside = position < length
    return (inside, jnp.sqrt(jnp.where(inside, position * (length - position), 1.0)))


def invert_block(sums, length, table, start):
    length = length.astype(jnp.float32)[:, None]
    col_in, col_w = weigh(length, sums.shape[1], 0.0)
    row_in, row_w = weigh(length, table.shape[0], start)
    scaled = jnp.where(col_in, col_w * sums, 0.0)
    image = jnp.dot(
        scaled, table.T, precision=lax.Precision.HIGHEST, preferred_element_type=jnp.float32
    )
    return jnp.where(row_in, image / (math.pi * row_w), 0.0)


def pick(table, index):
    hit = index[:, :, None] == jnp.arange(table.shape[1], dtype=jnp.int32)
    return jnp.sum(jnp.where(hit, table[:, None, :], 0), axis=-1)


def run_rings(rings):
    copies_at = []
    for s in range(max(r["n"] // 2 for r in rings)):
        copies = []
        for r in rings:
            n = r["n"]
            nr = n // 2
            nl = n - 1 - nr
            for go, steps, to, recv, send, sem in (
                (1, nr, r["right"], r["rr"], r["sr"], r["base"] + s),
                (-1, nl, r["left"], r["rl"], r["sl"], r["base"] + nr + s),
            ):
                if s >= steps:
                    continue
                dest = lax.rem(r["me"] + go * (steps - s) + 2 * n, n)
                if s == 0:
                    src = r["chunk"].at[dest]
                else:
                    send[s] = recv[s - 1] + r["chunk"][dest]
                    src = send.at[s]
                copy = pltpu.make_async_remote_copy(
                    src_ref=src,
                    dst_ref=recv.at[s],
                    send_sem=r["ssem"].at[sem],
                    recv_sem=r["rsem"].at[sem],
                    device_id=to,
                    device_id_type=MESH,
                )
                copy.start()
                copies.append(copy)
        for copy in copies:
            copy.wait()
    return [(r["rr"].at[r["n"] // 2 - 1], r["rl"].at[r["n"] - 2 - r["n"] // 2]) for r in rings]


def rs_kernel(ny, nz, xa, xb, oa, ob, s1a, s1b, *bufs):
    ssem, rsem = bufs[-2:]
    bufs = bufs[:-2]
    view = lax.axis_index("view")
    group = lax.axis_index("chord")
    y = view // nz
    z = lax.rem(view, nz)

    def dev(yy, zz):
        return (yy * nz + zz, group)

    z_right = dev(y, lax.rem(z + 1, nz))
    z_left = dev(y, lax.rem(z + nz - 1, nz))
    y_right = dev(lax.rem(y + 1, ny), z)
    y_left = dev(lax.rem(y + ny - 1, ny), z)

    barrier = pltpu.get_barrier_semaphore()
    for peer in (z_right, z_left, y_right, y_left):
        pl.semaphore_signal(barrier, inc=1, device_id=peer, device_id_type=MESH)
    pl.semaphore_wait(barrier, 4)

    def ring(n, me, right, left, chunk, at, base):
        rr, rl, sr, sl = bufs[4 * at: 4 * at + 4]
        return dict(n=n, me=me, right=right, left=left, chunk=chunk, rr=rr, rl=rl, sr=sr, sl=sl,
                    ssem=ssem, rsem=rsem, base=base)

    (ar, al), (br, bl) = run_rings([
        ring(nz, z, z_right, z_left, xa, 0, 0),
        ring(ny, y, y_right, y_left, xb, 1, nz - 1),
    ])
    s1a[...] = xa[z] + ar[...] + al[...]
    s1b[...] = xb[y] + br[...] + bl[...]
    (ar, al), (br, bl) = run_rings([
        ring(ny, y, y_right, y_left, s1a, 2, nz + ny - 2),
        ring(nz, z, z_right, z_left, s1b, 3, nz + 2 * ny - 3),
    ])
    oa[...] = s1a[y] + ar[...] + al[...]
    ob[...] = s1b[z] + br[...] + bl[...]


def reduce_scatter(xa, xb, ny, nz):
    ra, rb = xa.shape[2], xb.shape[2]
    f32 = jnp.float32

    def slots(n, shape):
        return [pltpu.VMEM((n // 2,) + shape, f32), pltpu.VMEM((n - 1 - n // 2,) + shape, f32)] * 2

    bufs = (
        slots(nz, (ny, ra, LANES)) + slots(ny, (nz, rb, LANES))
        + slots(ny, (ra, LANES)) + slots(nz, (rb, LANES))
    )
    return pl.pallas_call(
        functools.partial(rs_kernel, ny, nz),
        out_shape=(jax.ShapeDtypeStruct((ra, LANES), f32), jax.ShapeDtypeStruct((rb, LANES), f32)),
        in_specs=[pl.BlockSpec(memory_space=pltpu.VMEM)] * 2,
        out_specs=(pl.BlockSpec(memory_space=pltpu.VMEM),) * 2,
        scratch_shapes=[pltpu.VMEM((ny, ra, LANES), f32), pltpu.VMEM((nz, rb, LANES), f32)]
        + bufs
        + [pltpu.SemaphoreType.DMA((2 * (nz + ny - 2),)), pltpu.SemaphoreType.DMA((2 * (nz + ny - 2),))],
        compiler_params=pltpu.CompilerParams(collective_id=0, has_side_effects=True),
    )(xa, xb)


def per_device(ny, nz, proj, tiles, owner, lengths):
    view_count, group_rows, footprint = proj.shape
    samples = tiles.shape[2]
    group = lax.axis_index("chord")
    view_place = lax.axis_index("view")
    view_devices = ny * nz
    owned = group_rows // view_devices
    chunks_per_row = samples // LANES
    slots = min(chunks_per_row * owned, (PACK + owned * (LANES - 1)) // LANES)

    tile_rows = tiles.reshape(view_count, footprint, chunks_per_row, LANES)
    sums = jnp.einsum("vkd,vdcl->kcl", proj, tile_rows, preferred_element_type=jnp.float32)

    my_order = lax.dynamic_index_in_dim(owner, group, 0, keepdims=False)
    my_lengths = lax.dynamic_index_in_dim(lengths, group, 0, keepdims=False)
    order_len = pick(my_lengths[None, :], my_order[None, :])
    order_len = order_len.reshape(view_devices, owned)
    order_rows = my_order.reshape(view_devices, owned)

    counts = (order_len + LANES - 1) // LANES
    ends = jnp.cumsum(counts, axis=1)
    starts = ends - counts
    slot = jnp.arange(slots, dtype=jnp.int32)
    member = jnp.sum((ends[:, None, :] <= slot[None, :, None]).astype(jnp.int32), axis=2)
    member = jnp.minimum(member, owned - 1)
    first = pick(starts, member)
    src_row = pick(order_rows, member)
    within = jnp.clip(slot[None, :] - first, 0, chunks_per_row - 1)
    src = src_row * chunks_per_row + within
    src = src.reshape(ny, nz, slots)
    half = (slots + 1) // 2
    flat = sums.reshape(group_rows * chunks_per_row, LANES)
    xa = jnp.take(flat, src[:, :, :half].transpose(1, 0, 2), axis=0)
    xb = jnp.take(flat, src[:, :, half:], axis=0)

    mine = jnp.concatenate(reduce_scatter(xa, xb, ny, nz), axis=0)

    my_starts = lax.dynamic_index_in_dim(starts, view_place, 0, keepdims=False)
    my_len = lax.dynamic_index_in_dim(order_len, view_place, 0, keepdims=False)
    back = my_starts[:, None] + jnp.arange(chunks_per_row, dtype=jnp.int32)[None, :]
    back = jnp.minimum(back, slots - 1)
    rows = jnp.take(mine, back.reshape(-1), axis=0).reshape(owned, samples)

    table = kernel_table(samples, 0.0, samples)
    recon = invert_block(rows, my_len, table, 0.0)
    return recon[None]


def solution(mesh):
    view_devices = mesh.shape["view"]
    ny = int(round(math.sqrt(view_devices)))
    nz = view_devices // ny
    placed = (P("view", "chord", None), P("view", None, None), P(), P())
    return jax.shard_map(
        functools.partial(per_device, ny, nz),
        mesh=mesh,
        in_specs=placed,
        out_specs=P("chord", "view", None),
        check_vma=False,
    )
```

```python
import functools
import math

import jax
import jax.numpy as jnp
from jax import lax
from jax.experimental import pallas as pl
from jax.experimental.pallas import tpu as pltpu
from jax.sharding import PartitionSpec as P

LANES = 128
PACK = 4608
MESH = pl.DeviceIdType.MESH


def kernel_table(rows, start, cols):
    row_pos = start + jnp.arange(rows, dtype=jnp.float32)[:, None]
    col_pos = jnp.arange(cols, dtype=jnp.float32)[None, :]
    return 1.0 / (row_pos - col_pos + 0.5)


def weigh(length, count, start):
    position = start + jnp.arange(count, dtype=jnp.float32)[None, :] + 0.5
    inside = position < length
    return (inside, jnp.sqrt(jnp.where(inside, position * (length - position), 1.0)))


def invert_block(sums, length, table, start):
    length = length.astype(jnp.float32)[:, None]
    col_in, col_w = weigh(length, sums.shape[1], 0.0)
    row_in, row_w = weigh(length, table.shape[0], start)
    scaled = jnp.where(col_in, col_w * sums, 0.0)
    image = jnp.dot(
        scaled, table.T, precision=lax.Precision.HIGH, preferred_element_type=jnp.float32
    )
    return jnp.where(row_in, image / (math.pi * row_w), 0.0)


def pick(table, index):
    hit = index[:, :, None] == jnp.arange(table.shape[1], dtype=jnp.int32)
    return jnp.sum(jnp.where(hit, table[:, None, :], 0), axis=-1)


def run_rings(rings):
    copies_at = []
    for s in range(max(r["n"] // 2 for r in rings)):
        copies = []
        for r in rings:
            n = r["n"]
            nr = n // 2
            nl = n - 1 - nr
            for go, steps, to, recv, send, sem in (
                (1, nr, r["right"], r["rr"], r["sr"], r["base"] + s),
                (-1, nl, r["left"], r["rl"], r["sl"], r["base"] + nr + s),
            ):
                if s >= steps:
                    continue
                dest = lax.rem(r["me"] + go * (steps - s) + 2 * n, n)
                if s == 0:
                    src = r["chunk"].at[dest]
                else:
                    send[s] = recv[s - 1] + r["chunk"][dest]
                    src = send.at[s]
                copy = pltpu.make_async_remote_copy(
                    src_ref=src,
                    dst_ref=recv.at[s],
                    send_sem=r["ssem"].at[sem],
                    recv_sem=r["rsem"].at[sem],
                    device_id=to,
                    device_id_type=MESH,
                )
                copy.start()
                copies.append(copy)
        for copy in copies:
            copy.wait()
    return [(r["rr"].at[r["n"] // 2 - 1], r["rl"].at[r["n"] - 2 - r["n"] // 2]) for r in rings]


def rs_kernel(ny, nz, xa, xb, oa, ob, s1a, s1b, *bufs):
    ssem, rsem = bufs[-2:]
    bufs = bufs[:-2]
    view = lax.axis_index("view")
    group = lax.axis_index("chord")
    y = view // nz
    z = lax.rem(view, nz)

    def dev(yy, zz):
        return (yy * nz + zz, group)

    z_right = dev(y, lax.rem(z + 1, nz))
    z_left = dev(y, lax.rem(z + nz - 1, nz))
    y_right = dev(lax.rem(y + 1, ny), z)
    y_left = dev(lax.rem(y + ny - 1, ny), z)

    barrier = pltpu.get_barrier_semaphore()
    for peer in (z_right, z_left, y_right, y_left):
        pl.semaphore_signal(barrier, inc=1, device_id=peer, device_id_type=MESH)
    pl.semaphore_wait(barrier, 4)

    def ring(n, me, right, left, chunk, at, base):
        rr, rl, sr, sl = bufs[4 * at: 4 * at + 4]
        return dict(n=n, me=me, right=right, left=left, chunk=chunk, rr=rr, rl=rl, sr=sr, sl=sl,
                    ssem=ssem, rsem=rsem, base=base)

    (ar, al), (br, bl) = run_rings([
        ring(nz, z, z_right, z_left, xa, 0, 0),
        ring(ny, y, y_right, y_left, xb, 1, nz - 1),
    ])
    s1a[...] = xa[z] + ar[...] + al[...]
    s1b[...] = xb[y] + br[...] + bl[...]
    (ar, al), (br, bl) = run_rings([
        ring(ny, y, y_right, y_left, s1a, 2, nz + ny - 2),
        ring(nz, z, z_right, z_left, s1b, 3, nz + 2 * ny - 3),
    ])
    oa[...] = s1a[y] + ar[...] + al[...]
    ob[...] = s1b[z] + br[...] + bl[...]


def reduce_scatter(xa, xb, ny, nz):
    ra, rb = xa.shape[2], xb.shape[2]
    f32 = jnp.float32

    def slots(n, shape):
        return [pltpu.VMEM((n // 2,) + shape, f32), pltpu.VMEM((n - 1 - n // 2,) + shape, f32)] * 2

    bufs = (
        slots(nz, (ny, ra, LANES)) + slots(ny, (nz, rb, LANES))
        + slots(ny, (ra, LANES)) + slots(nz, (rb, LANES))
    )
    return pl.pallas_call(
        functools.partial(rs_kernel, ny, nz),
        out_shape=(jax.ShapeDtypeStruct((ra, LANES), f32), jax.ShapeDtypeStruct((rb, LANES), f32)),
        in_specs=[pl.BlockSpec(memory_space=pltpu.VMEM)] * 2,
        out_specs=(pl.BlockSpec(memory_space=pltpu.VMEM),) * 2,
        scratch_shapes=[pltpu.VMEM((ny, ra, LANES), f32), pltpu.VMEM((nz, rb, LANES), f32)]
        + bufs
        + [pltpu.SemaphoreType.DMA((2 * (nz + ny - 2),)), pltpu.SemaphoreType.DMA((2 * (nz + ny - 2),))],
        compiler_params=pltpu.CompilerParams(collective_id=0, has_side_effects=True),
    )(xa, xb)


def chunk_gather(sums, starts):
    dims = lax.GatherDimensionNumbers(
        offset_dims=(starts.ndim - 1,), collapsed_slice_dims=(0,), start_index_map=(0, 1)
    )
    return lax.gather(
        sums, starts, dims, slice_sizes=(1, LANES),
        mode=lax.GatherScatterMode.PROMISE_IN_BOUNDS,
    )


def per_device(ny, nz, proj, tiles, owner, lengths):
    view_count, group_rows, footprint = proj.shape
    samples = tiles.shape[2]
    group = lax.axis_index("chord")
    view_place = lax.axis_index("view")
    view_devices = ny * nz
    owned = group_rows // view_devices
    chunks_per_row = samples // LANES
    slots = min(chunks_per_row * owned, (PACK + owned * (LANES - 1)) // LANES)

    tile_rows = tiles.reshape(view_count, footprint, samples)
    sums = jnp.einsum("vkd,vds->ks", proj, tile_rows, preferred_element_type=jnp.float32)

    my_order = lax.dynamic_index_in_dim(owner, group, 0, keepdims=False)
    my_lengths = lax.dynamic_index_in_dim(lengths, group, 0, keepdims=False)
    order_len = pick(my_lengths[None, :], my_order[None, :])
    order_len = order_len.reshape(view_devices, owned)
    order_rows = my_order.reshape(view_devices, owned)

    counts = (order_len + LANES - 1) // LANES
    ends = jnp.cumsum(counts, axis=1)
    starts = ends - counts
    slot = jnp.arange(slots, dtype=jnp.int32)
    member = jnp.sum((ends[:, None, :] <= slot[None, :, None]).astype(jnp.int32), axis=2)
    member = jnp.minimum(member, owned - 1)
    first = pick(starts, member)
    src_row = pick(order_rows, member)
    within = jnp.clip(slot[None, :] - first, 0, chunks_per_row - 1)
    src = jnp.stack([src_row, within * LANES], axis=-1).reshape(ny, nz, slots, 2)
    half = (slots + 1) // 2
    xa = chunk_gather(sums, src[:, :, :half].transpose(1, 0, 2, 3))
    xb = chunk_gather(sums, src[:, :, half:])

    mine = jnp.concatenate(reduce_scatter(xa, xb, ny, nz), axis=0)

    my_starts = lax.dynamic_index_in_dim(starts, view_place, 0, keepdims=False)
    my_len = lax.dynamic_index_in_dim(order_len, view_place, 0, keepdims=False)
    back = my_starts[:, None] + jnp.arange(chunks_per_row, dtype=jnp.int32)[None, :]
    back = jnp.minimum(back, slots - 1)
    rows = jnp.take(mine, back.reshape(-1), axis=0, mode="clip").reshape(owned, samples)

    table = kernel_table(samples, 0.0, samples)
    recon = invert_block(rows, my_len, table, 0.0)
    return recon[None]


def solution(mesh):
    view_devices = mesh.shape["view"]
    ny = int(round(math.sqrt(view_devices)))
    nz = view_devices // ny
    placed = (P("view", "chord", None), P("view", None, None), P(), P())
    return jax.shard_map(
        functools.partial(per_device, ny, nz),
        mesh=mesh,
        in_specs=placed,
        out_specs=P("chord", "view", None),
        check_vma=False,
    )
```

```python
import functools
import math

import jax
import jax.numpy as jnp
from jax import lax
from jax.experimental import pallas as pl
from jax.experimental.pallas import tpu as pltpu
from jax.sharding import PartitionSpec as P

LANES = 128
PACK = 4608
MESH = pl.DeviceIdType.MESH


def kernel_table(rows, start, cols):
    row_pos = start + jnp.arange(rows, dtype=jnp.float32)[:, None]
    col_pos = jnp.arange(cols, dtype=jnp.float32)[None, :]
    return 1.0 / (row_pos - col_pos + 0.5)


def weigh(length, count, start):
    position = start + jnp.arange(count, dtype=jnp.float32)[None, :] + 0.5
    inside = position < length
    return (inside, jnp.sqrt(jnp.where(inside, position * (length - position), 1.0)))


def invert_block(sums, length, table, start):
    length = length.astype(jnp.float32)[:, None]
    col_in, col_w = weigh(length, sums.shape[1], 0.0)
    row_in, row_w = weigh(length, table.shape[0], start)
    scaled = jnp.where(col_in, col_w * sums, 0.0)
    image = jnp.dot(
        scaled, table.T, precision=lax.Precision.HIGH, preferred_element_type=jnp.float32
    )
    return jnp.where(row_in, image / (math.pi * row_w), 0.0)


def pick(table, index):
    hit = index[:, :, None] == jnp.arange(table.shape[1], dtype=jnp.int32)
    return jnp.sum(jnp.where(hit, table[:, None, :], 0), axis=-1)


def run_rings(rings):
    copies_at = []
    for s in range(max(r["n"] // 2 for r in rings)):
        copies = []
        for r in rings:
            n = r["n"]
            nr = n // 2
            nl = n - 1 - nr
            for go, steps, to, recv, send, sem in (
                (1, nr, r["right"], r["rr"], r["sr"], r["base"] + s),
                (-1, nl, r["left"], r["rl"], r["sl"], r["base"] + nr + s),
            ):
                if s >= steps:
                    continue
                dest = lax.rem(r["me"] + go * (steps - s) + 2 * n, n)
                if s == 0:
                    src = r["chunk"].at[dest]
                else:
                    send[s] = recv[s - 1] + r["chunk"][dest]
                    src = send.at[s]
                copy = pltpu.make_async_remote_copy(
                    src_ref=src,
                    dst_ref=recv.at[s],
                    send_sem=r["ssem"].at[sem],
                    recv_sem=r["rsem"].at[sem],
                    device_id=to,
                    device_id_type=MESH,
                )
                copy.start()
                copies.append(copy)
        for copy in copies:
            copy.wait()
    return [(r["rr"].at[r["n"] // 2 - 1], r["rl"].at[r["n"] - 2 - r["n"] // 2]) for r in rings]


def rs_kernel(ny, nz, xa, xb, oa, ob, s1a, s1b, *bufs):
    ssem, rsem = bufs[-2:]
    bufs = bufs[:-2]
    view = lax.axis_index("view")
    group = lax.axis_index("chord")
    y = view // nz
    z = lax.rem(view, nz)

    def dev(yy, zz):
        return (yy * nz + zz, group)

    z_right = dev(y, lax.rem(z + 1, nz))
    z_left = dev(y, lax.rem(z + nz - 1, nz))
    y_right = dev(lax.rem(y + 1, ny), z)
    y_left = dev(lax.rem(y + ny - 1, ny), z)

    barrier = pltpu.get_barrier_semaphore()
    for peer in (z_right, z_left, y_right, y_left):
        pl.semaphore_signal(barrier, inc=1, device_id=peer, device_id_type=MESH)
    pl.semaphore_wait(barrier, 4)

    def ring(n, me, right, left, chunk, at, base):
        rr, rl, sr, sl = bufs[4 * at: 4 * at + 4]
        return dict(n=n, me=me, right=right, left=left, chunk=chunk, rr=rr, rl=rl, sr=sr, sl=sl,
                    ssem=ssem, rsem=rsem, base=base)

    (ar, al), (br, bl) = run_rings([
        ring(nz, z, z_right, z_left, xa, 0, 0),
        ring(ny, y, y_right, y_left, xb, 1, nz - 1),
    ])
    s1a[...] = xa[z] + ar[...] + al[...]
    s1b[...] = xb[y] + br[...] + bl[...]
    (ar, al), (br, bl) = run_rings([
        ring(ny, y, y_right, y_left, s1a, 2, nz + ny - 2),
        ring(nz, z, z_right, z_left, s1b, 3, nz + 2 * ny - 3),
    ])
    oa[...] = s1a[y] + ar[...] + al[...]
    ob[...] = s1b[z] + br[...] + bl[...]


def reduce_scatter(xa, xb, ny, nz):
    ra, rb = xa.shape[2], xb.shape[2]
    f32 = jnp.float32

    def slots(n, shape):
        return [pltpu.VMEM((n // 2,) + shape, f32), pltpu.VMEM((n - 1 - n // 2,) + shape, f32)] * 2

    bufs = (
        slots(nz, (ny, ra, LANES)) + slots(ny, (nz, rb, LANES))
        + slots(ny, (ra, LANES)) + slots(nz, (rb, LANES))
    )
    return pl.pallas_call(
        functools.partial(rs_kernel, ny, nz),
        out_shape=(jax.ShapeDtypeStruct((ra, LANES), f32), jax.ShapeDtypeStruct((rb, LANES), f32)),
        in_specs=[pl.BlockSpec(memory_space=pltpu.VMEM)] * 2,
        out_specs=(pl.BlockSpec(memory_space=pltpu.VMEM),) * 2,
        scratch_shapes=[pltpu.VMEM((ny, ra, LANES), f32), pltpu.VMEM((nz, rb, LANES), f32)]
        + bufs
        + [pltpu.SemaphoreType.DMA((2 * (nz + ny - 2),)), pltpu.SemaphoreType.DMA((2 * (nz + ny - 2),))],
        compiler_params=pltpu.CompilerParams(collective_id=0, has_side_effects=True),
    )(xa, xb)


def per_device(ny, nz, proj, tiles, owner, lengths):
    view_count, group_rows, footprint = proj.shape
    samples = tiles.shape[2]
    group = lax.axis_index("chord")
    view_place = lax.axis_index("view")
    view_devices = ny * nz
    owned = group_rows // view_devices
    chunks_per_row = samples // LANES
    slots = min(chunks_per_row * owned, (PACK + owned * (LANES - 1)) // LANES)

    tile_rows = tiles.reshape(view_count, footprint, samples)
    sums = jnp.einsum("vkd,vds->ks", proj, tile_rows, preferred_element_type=jnp.float32)

    my_order = lax.dynamic_index_in_dim(owner, group, 0, keepdims=False)
    my_lengths = lax.dynamic_index_in_dim(lengths, group, 0, keepdims=False)
    order_len = pick(my_lengths[None, :], my_order[None, :])
    order_len = order_len.reshape(view_devices, owned)
    order_rows = my_order.reshape(view_devices, owned)

    counts = (order_len + LANES - 1) // LANES
    ends = jnp.cumsum(counts, axis=1)
    starts = ends - counts
    slot = jnp.arange(slots, dtype=jnp.int32)
    member = jnp.sum((ends[:, None, :] <= slot[None, :, None]).astype(jnp.int32), axis=2)
    member = jnp.minimum(member, owned - 1)
    first = pick(starts, member)
    src_row = pick(order_rows, member)
    within = jnp.clip(slot[None, :] - first, 0, chunks_per_row - 1)
    src = (src_row * chunks_per_row + within).reshape(ny, nz, slots)
    half = (slots + 1) // 2
    flat = sums.reshape(group_rows * chunks_per_row, LANES)
    xa = jnp.take(flat, src[:, :, :half].transpose(1, 0, 2), axis=0, mode="clip")
    xb = jnp.take(flat, src[:, :, half:], axis=0, mode="clip")

    mine = jnp.concatenate(reduce_scatter(xa, xb, ny, nz), axis=0)

    my_starts = lax.dynamic_index_in_dim(starts, view_place, 0, keepdims=False)
    my_len = lax.dynamic_index_in_dim(order_len, view_place, 0, keepdims=False)
    back = my_starts[:, None] + jnp.arange(chunks_per_row, dtype=jnp.int32)[None, :]
    back = jnp.minimum(back, slots - 1)
    rows = jnp.take(mine, back.reshape(-1), axis=0, mode="clip").reshape(owned, samples)

    table = kernel_table(samples, 0.0, samples)
    recon = invert_block(rows, my_len, table, 0.0)
    return recon[None]


def solution(mesh):
    view_devices = mesh.shape["view"]
    ny = int(round(math.sqrt(view_devices)))
    nz = view_devices // ny
    placed = (P("view", "chord", None), P("view", None, None), P(), P())
    return jax.shard_map(
        functools.partial(per_device, ny, nz),
        mesh=mesh,
        in_specs=placed,
        out_specs=P("chord", "view", None),
        check_vma=False,
    )
```

```python
import functools
import math

import jax
import jax.numpy as jnp
from jax import lax
from jax.experimental import pallas as pl
from jax.experimental.pallas import tpu as pltpu
from jax.sharding import PartitionSpec as P

LANES = 128
PACK = 4608
MESH = pl.DeviceIdType.MESH


def kernel_table(rows, start, cols):
    row_pos = start + jnp.arange(rows, dtype=jnp.float32)[:, None]
    col_pos = jnp.arange(cols, dtype=jnp.float32)[None, :]
    return 1.0 / (row_pos - col_pos + 0.5)


def weigh(length, count, start):
    position = start + jnp.arange(count, dtype=jnp.float32)[None, :] + 0.5
    inside = position < length
    return (inside, jnp.sqrt(jnp.where(inside, position * (length - position), 1.0)))


def invert_block(sums, length, table, start):
    length = length.astype(jnp.float32)[:, None]
    col_in, col_w = weigh(length, sums.shape[1], 0.0)
    row_in, row_w = weigh(length, table.shape[0], start)
    scaled = jnp.where(col_in, col_w * sums, 0.0)
    image = jnp.dot(
        scaled, table.T, precision=lax.Precision.HIGH, preferred_element_type=jnp.float32
    )
    return jnp.where(row_in, image / (math.pi * row_w), 0.0)


def pick(table, index):
    hit = index[:, :, None] == jnp.arange(table.shape[1], dtype=jnp.int32)
    return jnp.sum(jnp.where(hit, table[:, None, :], 0), axis=-1)


def run_rings(rings):
    copies_at = []
    for s in range(max(r["n"] // 2 for r in rings)):
        copies = []
        for r in rings:
            n = r["n"]
            nr = n // 2
            nl = n - 1 - nr
            for go, steps, to, recv, send, sem in (
                (1, nr, r["right"], r["rr"], r["sr"], r["base"] + s),
                (-1, nl, r["left"], r["rl"], r["sl"], r["base"] + nr + s),
            ):
                if s >= steps:
                    continue
                dest = lax.rem(r["me"] + go * (steps - s) + 2 * n, n)
                if s == 0:
                    src = r["chunk"].at[dest]
                else:
                    send[s] = recv[s - 1] + r["chunk"][dest]
                    src = send.at[s]
                copy = pltpu.make_async_remote_copy(
                    src_ref=src,
                    dst_ref=recv.at[s],
                    send_sem=r["ssem"].at[sem],
                    recv_sem=r["rsem"].at[sem],
                    device_id=to,
                    device_id_type=MESH,
                )
                copy.start()
                copies.append(copy)
        for copy in copies:
            copy.wait()
    return [(r["rr"].at[r["n"] // 2 - 1], r["rl"].at[r["n"] - 2 - r["n"] // 2]) for r in rings]


def rs_kernel(ny, nz, xa, xb, oa, ob, s1a, s1b, *bufs):
    ssem, rsem = bufs[-2:]
    bufs = bufs[:-2]
    view = lax.axis_index("view")
    group = lax.axis_index("chord")
    y = view // nz
    z = lax.rem(view, nz)

    def dev(yy, zz):
        return (yy * nz + zz, group)

    z_right = dev(y, lax.rem(z + 1, nz))
    z_left = dev(y, lax.rem(z + nz - 1, nz))
    y_right = dev(lax.rem(y + 1, ny), z)
    y_left = dev(lax.rem(y + ny - 1, ny), z)

    barrier = pltpu.get_barrier_semaphore()
    for peer in (z_right, z_left, y_right, y_left):
        pl.semaphore_signal(barrier, inc=1, device_id=peer, device_id_type=MESH)
    pl.semaphore_wait(barrier, 4)

    def ring(n, me, right, left, chunk, at, base):
        rr, rl, sr, sl = bufs[4 * at: 4 * at + 4]
        return dict(n=n, me=me, right=right, left=left, chunk=chunk, rr=rr, rl=rl, sr=sr, sl=sl,
                    ssem=ssem, rsem=rsem, base=base)

    (ar, al), (br, bl) = run_rings([
        ring(nz, z, z_right, z_left, xa, 0, 0),
        ring(ny, y, y_right, y_left, xb, 1, nz - 1),
    ])
    s1a[...] = xa[z] + ar[...] + al[...]
    s1b[...] = xb[y] + br[...] + bl[...]
    (ar, al), (br, bl) = run_rings([
        ring(ny, y, y_right, y_left, s1a, 2, nz + ny - 2),
        ring(nz, z, z_right, z_left, s1b, 3, nz + 2 * ny - 3),
    ])
    oa[...] = s1a[y] + ar[...] + al[...]
    ob[...] = s1b[z] + br[...] + bl[...]


def reduce_scatter(xa, xb, ny, nz):
    ra, rb = xa.shape[2], xb.shape[2]
    f32 = jnp.float32

    def slots(n, shape):
        return [pltpu.VMEM((n // 2,) + shape, f32), pltpu.VMEM((n - 1 - n // 2,) + shape, f32)] * 2

    bufs = (
        slots(nz, (ny, ra, LANES)) + slots(ny, (nz, rb, LANES))
        + slots(ny, (ra, LANES)) + slots(nz, (rb, LANES))
    )
    return pl.pallas_call(
        functools.partial(rs_kernel, ny, nz),
        out_shape=(jax.ShapeDtypeStruct((ra, LANES), f32), jax.ShapeDtypeStruct((rb, LANES), f32)),
        in_specs=[pl.BlockSpec(memory_space=pltpu.VMEM)] * 2,
        out_specs=(pl.BlockSpec(memory_space=pltpu.VMEM),) * 2,
        scratch_shapes=[pltpu.VMEM((ny, ra, LANES), f32), pltpu.VMEM((nz, rb, LANES), f32)]
        + bufs
        + [pltpu.SemaphoreType.DMA((2 * (nz + ny - 2),)), pltpu.SemaphoreType.DMA((2 * (nz + ny - 2),))],
        compiler_params=pltpu.CompilerParams(collective_id=0, has_side_effects=True),
    )(xa, xb)


def per_device(ny, nz, proj, tiles, owner, lengths):
    view_count, group_rows, footprint = proj.shape
    samples = tiles.shape[2]
    group = lax.axis_index("chord")
    view_place = lax.axis_index("view")
    view_devices = ny * nz
    owned = group_rows // view_devices
    chunks_per_row = samples // LANES
    slots = min(chunks_per_row * owned, (PACK + owned * (LANES - 1)) // LANES)

    tile_rows = tiles.reshape(view_count, footprint, samples)
    sums = jnp.einsum("vkd,vds->ks", proj, tile_rows, preferred_element_type=jnp.float32)

    my_order = lax.dynamic_index_in_dim(owner, group, 0, keepdims=False)
    my_lengths = lax.dynamic_index_in_dim(lengths, group, 0, keepdims=False)
    order_len = pick(my_lengths[None, :], my_order[None, :])
    order_len = order_len.reshape(view_devices, owned)
    order_rows = my_order.reshape(view_devices, owned)

    counts = (order_len + LANES - 1) // LANES
    ends = jnp.cumsum(counts, axis=1)
    starts = ends - counts
    slot = jnp.arange(slots, dtype=jnp.int32)
    member = jnp.sum((ends[:, None, :] <= slot[None, :, None]).astype(jnp.int32), axis=2)
    member = jnp.minimum(member, owned - 1)
    first = pick(starts, member)
    src_row = pick(order_rows, member)
    within = jnp.clip(slot[None, :] - first, 0, chunks_per_row - 1)
    src = (src_row * chunks_per_row + within).reshape(ny, nz, slots)
    half = (slots + 1) // 2
    flat = sums.reshape(group_rows * chunks_per_row, LANES)
    xa = jnp.take(flat, src[:, :, :half].transpose(1, 0, 2), axis=0, mode="wrap")
    xb = jnp.take(flat, src[:, :, half:], axis=0, mode="wrap")

    mine = jnp.concatenate(reduce_scatter(xa, xb, ny, nz), axis=0)

    my_starts = lax.dynamic_index_in_dim(starts, view_place, 0, keepdims=False)
    my_len = lax.dynamic_index_in_dim(order_len, view_place, 0, keepdims=False)
    back = my_starts[:, None] + jnp.arange(chunks_per_row, dtype=jnp.int32)[None, :]
    back = jnp.minimum(back, slots - 1)
    rows = jnp.take(mine, back.reshape(-1), axis=0, mode="clip").reshape(owned, samples)

    table = kernel_table(samples, 0.0, samples)
    recon = invert_block(rows, my_len, table, 0.0)
    return recon[None]


def solution(mesh):
    view_devices = mesh.shape["view"]
    ny = int(round(math.sqrt(view_devices)))
    nz = view_devices // ny
    placed = (P("view", "chord", None), P("view", None, None), P(), P())
    return jax.shard_map(
        functools.partial(per_device, ny, nz),
        mesh=mesh,
        in_specs=placed,
        out_specs=P("chord", "view", None),
        check_vma=False,
    )
```

```python
import functools
import math

import jax
import jax.numpy as jnp
from jax import lax
from jax.experimental import pallas as pl
from jax.experimental.pallas import tpu as pltpu
from jax.sharding import PartitionSpec as P

LANES = 128
PACK = 4608
MESH = pl.DeviceIdType.MESH


def kernel_table(rows, start, cols):
    row_pos = start + jnp.arange(rows, dtype=jnp.float32)[:, None]
    col_pos = jnp.arange(cols, dtype=jnp.float32)[None, :]
    return 1.0 / (row_pos - col_pos + 0.5)


def weigh(length, count, start):
    position = start + jnp.arange(count, dtype=jnp.float32)[None, :] + 0.5
    inside = position < length
    return (inside, jnp.sqrt(jnp.where(inside, position * (length - position), 1.0)))


def invert_block(sums, length, table, start):
    length = length.astype(jnp.float32)[:, None]
    col_in, col_w = weigh(length, sums.shape[1], 0.0)
    row_in, row_w = weigh(length, table.shape[0], start)
    scaled = jnp.where(col_in, col_w * sums, 0.0)
    image = jnp.dot(
        scaled, table.T, precision=lax.Precision.HIGH, preferred_element_type=jnp.float32
    )
    return jnp.where(row_in, image / (math.pi * row_w), 0.0)


def pick(table, index):
    hit = index[:, :, None] == jnp.arange(table.shape[1], dtype=jnp.int32)
    return jnp.sum(jnp.where(hit, table[:, None, :], 0), axis=-1)


def run_rings(rings):
    copies_at = []
    for s in range(max(r["n"] // 2 for r in rings)):
        copies = []
        for r in rings:
            n = r["n"]
            nr = n // 2
            nl = n - 1 - nr
            for go, steps, to, recv, send, sem in (
                (1, nr, r["right"], r["rr"], r["sr"], r["base"] + s),
                (-1, nl, r["left"], r["rl"], r["sl"], r["base"] + nr + s),
            ):
                if s >= steps:
                    continue
                dest = lax.rem(r["me"] + go * (steps - s) + 2 * n, n)
                if s == 0:
                    src = r["chunk"].at[dest]
                else:
                    send[s] = recv[s - 1] + r["chunk"][dest]
                    src = send.at[s]
                copy = pltpu.make_async_remote_copy(
                    src_ref=src,
                    dst_ref=recv.at[s],
                    send_sem=r["ssem"].at[sem],
                    recv_sem=r["rsem"].at[sem],
                    device_id=to,
                    device_id_type=MESH,
                )
                copy.start()
                copies.append(copy)
        for copy in copies:
            copy.wait()
    return [(r["rr"].at[r["n"] // 2 - 1], r["rl"].at[r["n"] - 2 - r["n"] // 2]) for r in rings]


def rs_kernel(ny, nz, xa, xb, oa, ob, s1a, s1b, *bufs):
    ssem, rsem = bufs[-2:]
    bufs = bufs[:-2]
    view = lax.axis_index("view")
    group = lax.axis_index("chord")
    y = view // nz
    z = lax.rem(view, nz)

    def dev(yy, zz):
        return (yy * nz + zz, group)

    z_right = dev(y, lax.rem(z + 1, nz))
    z_left = dev(y, lax.rem(z + nz - 1, nz))
    y_right = dev(lax.rem(y + 1, ny), z)
    y_left = dev(lax.rem(y + ny - 1, ny), z)

    barrier = pltpu.get_barrier_semaphore()
    for peer in (z_right, z_left, y_right, y_left):
        pl.semaphore_signal(barrier, inc=1, device_id=peer, device_id_type=MESH)
    pl.semaphore_wait(barrier, 4)

    def ring(n, me, right, left, chunk, at, base):
        rr, rl, sr, sl = bufs[4 * at: 4 * at + 4]
        return dict(n=n, me=me, right=right, left=left, chunk=chunk, rr=rr, rl=rl, sr=sr, sl=sl,
                    ssem=ssem, rsem=rsem, base=base)

    (ar, al), (br, bl) = run_rings([
        ring(nz, z, z_right, z_left, xa, 0, 0),
        ring(ny, y, y_right, y_left, xb, 1, nz - 1),
    ])
    s1a[...] = xa[z] + ar[...] + al[...]
    s1b[...] = xb[y] + br[...] + bl[...]
    (ar, al), (br, bl) = run_rings([
        ring(ny, y, y_right, y_left, s1a, 2, nz + ny - 2),
        ring(nz, z, z_right, z_left, s1b, 3, nz + 2 * ny - 3),
    ])
    oa[...] = s1a[y] + ar[...] + al[...]
    ob[...] = s1b[z] + br[...] + bl[...]


def reduce_scatter(xa, xb, ny, nz):
    ra, rb = xa.shape[2], xb.shape[2]
    f32 = jnp.float32

    def slots(n, shape):
        return [pltpu.VMEM((n // 2,) + shape, f32), pltpu.VMEM((n - 1 - n // 2,) + shape, f32)] * 2

    bufs = (
        slots(nz, (ny, ra, LANES)) + slots(ny, (nz, rb, LANES))
        + slots(ny, (ra, LANES)) + slots(nz, (rb, LANES))
    )
    return pl.pallas_call(
        functools.partial(rs_kernel, ny, nz),
        out_shape=(jax.ShapeDtypeStruct((ra, LANES), f32), jax.ShapeDtypeStruct((rb, LANES), f32)),
        in_specs=[pl.BlockSpec(memory_space=pltpu.VMEM)] * 2,
        out_specs=(pl.BlockSpec(memory_space=pltpu.VMEM),) * 2,
        scratch_shapes=[pltpu.VMEM((ny, ra, LANES), f32), pltpu.VMEM((nz, rb, LANES), f32)]
        + bufs
        + [pltpu.SemaphoreType.DMA((2 * (nz + ny - 2),)), pltpu.SemaphoreType.DMA((2 * (nz + ny - 2),))],
        compiler_params=pltpu.CompilerParams(collective_id=0, has_side_effects=True),
    )(xa, xb)


def pack_kernel(ia_ref, ib_ref, proj_ref, tiles_ref, xa_ref, xb_ref, acc_ref):
    blocks, pair, samples = tiles_ref.shape
    footprint = proj_ref.shape[2]
    per = pair // footprint
    chunks = samples // LANES
    width = min(samples, 256)
    for cb in range(samples // width):
        cols = pl.ds(cb * width, width)
        total = None
        for b in range(blocks):
            lhs = jnp.concatenate([proj_ref[b * per + h] for h in range(per)], axis=1)
            term = jnp.dot(lhs, tiles_ref[b, :, cols], preferred_element_type=jnp.float32)
            total = term if total is None else total + term
        acc_ref[:, cols] = total

    for idx_ref, out_ref in ((ia_ref, xa_ref), (ib_ref, xb_ref)):
        n0, n1, rows = out_ref.shape[:3]

        def body(i, carry, idx_ref=idx_ref, out_ref=out_ref, n1=n1, rows=rows):
            a = i // n1
            c = lax.rem(i, n1)
            for r in range(rows):
                flat = idx_ref[i * rows + r]
                row = flat // chunks
                col = pl.multiple_of(lax.rem(flat, chunks) * LANES, LANES)
                top = pl.multiple_of((row // 8) * 8, 8)
                tile = acc_ref[pl.ds(top, 8), pl.ds(col, LANES)]
                hit = lax.broadcasted_iota(jnp.int32, tile.shape, 0) == row - top
                out_ref[a, c, pl.ds(r, 1), :] = jnp.sum(
                    jnp.where(hit, tile, 0.0), axis=0, keepdims=True
                )
            return carry

        lax.fori_loop(0, n0 * n1, body, 0)


def pack(ia, ib, proj, tiles, shape_a, shape_b):
    f32 = jnp.float32
    samples = tiles.shape[2]
    return pl.pallas_call(
        pack_kernel,
        out_shape=(jax.ShapeDtypeStruct(shape_a, f32), jax.ShapeDtypeStruct(shape_b, f32)),
        in_specs=[pl.BlockSpec(memory_space=pltpu.SMEM)] * 2
        + [pl.BlockSpec(memory_space=pltpu.VMEM)] * 2,
        out_specs=(pl.BlockSpec(memory_space=pltpu.VMEM),) * 2,
        scratch_shapes=[pltpu.VMEM((proj.shape[1], samples), f32)],
    )(ia, ib, proj, tiles)


def per_device(ny, nz, proj, tiles, owner, lengths):
    view_count, group_rows, footprint = proj.shape
    samples = tiles.shape[2]
    group = lax.axis_index("chord")
    view_place = lax.axis_index("view")
    view_devices = ny * nz
    owned = group_rows // view_devices
    chunks_per_row = samples // LANES
    slots = min(chunks_per_row * owned, (PACK + owned * (LANES - 1)) // LANES)


    my_order = lax.dynamic_index_in_dim(owner, group, 0, keepdims=False)
    my_lengths = lax.dynamic_index_in_dim(lengths, group, 0, keepdims=False)
    order_len = pick(my_lengths[None, :], my_order[None, :])
    order_len = order_len.reshape(view_devices, owned)
    order_rows = my_order.reshape(view_devices, owned)

    counts = (order_len + LANES - 1) // LANES
    ends = jnp.cumsum(counts, axis=1)
    starts = ends - counts
    slot = jnp.arange(slots, dtype=jnp.int32)
    member = jnp.sum((ends[:, None, :] <= slot[None, :, None]).astype(jnp.int32), axis=2)
    member = jnp.minimum(member, owned - 1)
    first = pick(starts, member)
    src_row = pick(order_rows, member)
    within = jnp.clip(slot[None, :] - first, 0, chunks_per_row - 1)
    src = (src_row * chunks_per_row + within).reshape(ny, nz, slots)
    half = (slots + 1) // 2
    ia = src[:, :, :half].transpose(1, 0, 2)
    ib = src[:, :, half:]
    xa, xb = pack(ia.reshape(-1), ib.reshape(-1), proj, tiles,
                  ia.shape + (LANES,), ib.shape + (LANES,))

    mine = jnp.concatenate(reduce_scatter(xa, xb, ny, nz), axis=0)

    my_starts = lax.dynamic_index_in_dim(starts, view_place, 0, keepdims=False)
    my_len = lax.dynamic_index_in_dim(order_len, view_place, 0, keepdims=False)
    back = my_starts[:, None] + jnp.arange(chunks_per_row, dtype=jnp.int32)[None, :]
    back = jnp.minimum(back, slots - 1)
    rows = jnp.take(mine, back.reshape(-1), axis=0, mode="clip").reshape(owned, samples)

    table = kernel_table(samples, 0.0, samples)
    recon = invert_block(rows, my_len, table, 0.0)
    return recon[None]


def solution(mesh):
    view_devices = mesh.shape["view"]
    ny = int(round(math.sqrt(view_devices)))
    nz = view_devices // ny
    placed = (P("view", "chord", None), P("view", None, None), P(), P())
    return jax.shard_map(
        functools.partial(per_device, ny, nz),
        mesh=mesh,
        in_specs=placed,
        out_specs=P("chord", "view", None),
        check_vma=False,
    )
```

```python
import functools
import math

import jax
import jax.numpy as jnp
from jax import lax
from jax.experimental import pallas as pl
from jax.experimental.pallas import tpu as pltpu
from jax.sharding import PartitionSpec as P

LANES = 128
PACK = 4608
MESH = pl.DeviceIdType.MESH


def kernel_table(rows, start, cols):
    row_pos = start + jnp.arange(rows, dtype=jnp.float32)[:, None]
    col_pos = jnp.arange(cols, dtype=jnp.float32)[None, :]
    return 1.0 / (row_pos - col_pos + 0.5)


def weigh(length, count, start):
    position = start + jnp.arange(count, dtype=jnp.float32)[None, :] + 0.5
    inside = position < length
    return (inside, jnp.sqrt(jnp.where(inside, position * (length - position), 1.0)))


def invert_block(sums, length, table, start):
    length = length.astype(jnp.float32)[:, None]
    col_in, col_w = weigh(length, sums.shape[1], 0.0)
    row_in, row_w = weigh(length, table.shape[0], start)
    scaled = jnp.where(col_in, col_w * sums, 0.0)
    image = jnp.dot(
        scaled, table.T, precision=lax.Precision.HIGH, preferred_element_type=jnp.float32
    )
    return jnp.where(row_in, image / (math.pi * row_w), 0.0)


def pick(table, index):
    hit = index[:, :, None] == jnp.arange(table.shape[1], dtype=jnp.int32)
    return jnp.sum(jnp.where(hit, table[:, None, :], 0), axis=-1)


def run_rings(rings):
    copies_at = []
    for s in range(max(r["n"] // 2 for r in rings)):
        copies = []
        for r in rings:
            n = r["n"]
            nr = n // 2
            nl = n - 1 - nr
            for go, steps, to, recv, send, sem in (
                (1, nr, r["right"], r["rr"], r["sr"], r["base"] + s),
                (-1, nl, r["left"], r["rl"], r["sl"], r["base"] + nr + s),
            ):
                if s >= steps:
                    continue
                dest = lax.rem(r["me"] + go * (steps - s) + 2 * n, n)
                if s == 0:
                    src = r["chunk"].at[dest]
                else:
                    send[s] = recv[s - 1] + r["chunk"][dest]
                    src = send.at[s]
                copy = pltpu.make_async_remote_copy(
                    src_ref=src,
                    dst_ref=recv.at[s],
                    send_sem=r["ssem"].at[sem],
                    recv_sem=r["rsem"].at[sem],
                    device_id=to,
                    device_id_type=MESH,
                )
                copy.start()
                copies.append(copy)
        for copy in copies:
            copy.wait()
    return [(r["rr"].at[r["n"] // 2 - 1], r["rl"].at[r["n"] - 2 - r["n"] // 2]) for r in rings]


def rs_kernel(ny, nz, xa, xb, oa, ob, s1a, s1b, *bufs):
    ssem, rsem = bufs[-2:]
    bufs = bufs[:-2]
    view = lax.axis_index("view")
    group = lax.axis_index("chord")
    y = view // nz
    z = lax.rem(view, nz)

    def dev(yy, zz):
        return (yy * nz + zz, group)

    z_right = dev(y, lax.rem(z + 1, nz))
    z_left = dev(y, lax.rem(z + nz - 1, nz))
    y_right = dev(lax.rem(y + 1, ny), z)
    y_left = dev(lax.rem(y + ny - 1, ny), z)

    barrier = pltpu.get_barrier_semaphore()
    for peer in (z_right, z_left, y_right, y_left):
        pl.semaphore_signal(barrier, inc=1, device_id=peer, device_id_type=MESH)
    pl.semaphore_wait(barrier, 4)

    def ring(n, me, right, left, chunk, at, base):
        rr, rl, sr, sl = bufs[4 * at: 4 * at + 4]
        return dict(n=n, me=me, right=right, left=left, chunk=chunk, rr=rr, rl=rl, sr=sr, sl=sl,
                    ssem=ssem, rsem=rsem, base=base)

    (ar, al), (br, bl) = run_rings([
        ring(nz, z, z_right, z_left, xa, 0, 0),
        ring(ny, y, y_right, y_left, xb, 1, nz - 1),
    ])
    s1a[...] = xa[z] + ar[...] + al[...]
    s1b[...] = xb[y] + br[...] + bl[...]
    (ar, al), (br, bl) = run_rings([
        ring(ny, y, y_right, y_left, s1a, 2, nz + ny - 2),
        ring(nz, z, z_right, z_left, s1b, 3, nz + 2 * ny - 3),
    ])
    oa[...] = s1a[y] + ar[...] + al[...]
    ob[...] = s1b[z] + br[...] + bl[...]


def reduce_scatter(xa, xb, ny, nz):
    ra, rb = xa.shape[2], xb.shape[2]
    f32 = jnp.float32

    def slots(n, shape):
        return [pltpu.VMEM((n // 2,) + shape, f32), pltpu.VMEM((n - 1 - n // 2,) + shape, f32)] * 2

    bufs = (
        slots(nz, (ny, ra, LANES)) + slots(ny, (nz, rb, LANES))
        + slots(ny, (ra, LANES)) + slots(nz, (rb, LANES))
    )
    return pl.pallas_call(
        functools.partial(rs_kernel, ny, nz),
        out_shape=(jax.ShapeDtypeStruct((ra, LANES), f32), jax.ShapeDtypeStruct((rb, LANES), f32)),
        in_specs=[pl.BlockSpec(memory_space=pltpu.VMEM)] * 2,
        out_specs=(pl.BlockSpec(memory_space=pltpu.VMEM),) * 2,
        scratch_shapes=[pltpu.VMEM((ny, ra, LANES), f32), pltpu.VMEM((nz, rb, LANES), f32)]
        + bufs
        + [pltpu.SemaphoreType.DMA((2 * (nz + ny - 2),)), pltpu.SemaphoreType.DMA((2 * (nz + ny - 2),))],
        compiler_params=pltpu.CompilerParams(collective_id=0, has_side_effects=True),
    )(xa, xb)


def per_device(ny, nz, proj, tiles, owner, lengths):
    view_count, group_rows, footprint = proj.shape
    samples = tiles.shape[2]
    group = lax.axis_index("chord")
    view_place = lax.axis_index("view")
    view_devices = ny * nz
    owned = group_rows // view_devices
    chunks_per_row = samples // LANES
    slots = min(chunks_per_row * owned, (PACK + owned * (LANES - 1)) // LANES)

    my_order = lax.dynamic_index_in_dim(owner, group, 0, keepdims=False)
    my_lengths = lax.dynamic_index_in_dim(lengths, group, 0, keepdims=False)
    order_len = pick(my_lengths[None, :], my_order[None, :])
    order_len = order_len.reshape(view_devices, owned)

    perm = (my_order[:, None] == jnp.arange(group_rows, dtype=jnp.int32)[None, :]).astype(proj.dtype)
    proj_ord = jnp.einsum("rk,vkd->vrd", perm, proj, preferred_element_type=jnp.float32)
    proj_ord = proj_ord.astype(proj.dtype)
    tile_rows = tiles.reshape(view_count, footprint, samples)
    sums = jnp.einsum("vrd,vds->rs", proj_ord, tile_rows, preferred_element_type=jnp.float32)
    blocks = sums.reshape(ny, nz, owned, chunks_per_row, LANES).transpose(0, 1, 3, 2, 4)
    blocks = blocks.reshape(ny, nz, owned * chunks_per_row, LANES)

    counts = (order_len + LANES - 1) // LANES
    ends = jnp.cumsum(counts, axis=1)
    starts = ends - counts
    slot = jnp.arange(slots, dtype=jnp.int32)
    member = jnp.sum((ends[:, None, :] <= slot[None, :, None]).astype(jnp.int32), axis=2)
    member = jnp.minimum(member, owned - 1)
    first = pick(starts, member)
    within = jnp.clip(slot[None, :] - first, 0, chunks_per_row - 1)
    src = (within * owned + member).reshape(ny, nz, slots)
    half = (slots + 1) // 2
    choose = (src[..., None] == jnp.arange(owned * chunks_per_row, dtype=jnp.int32)).astype(jnp.float32)
    xa = jnp.einsum("yzbj,yzjl->zybl", choose[:, :, :half], blocks,
                    precision=lax.Precision.HIGHEST, preferred_element_type=jnp.float32)
    xb = jnp.einsum("yzbj,yzjl->yzbl", choose[:, :, half:], blocks,
                    precision=lax.Precision.HIGHEST, preferred_element_type=jnp.float32)

    mine = jnp.concatenate(reduce_scatter(xa, xb, ny, nz), axis=0)

    my_starts = lax.dynamic_index_in_dim(starts, view_place, 0, keepdims=False)
    my_len = lax.dynamic_index_in_dim(order_len, view_place, 0, keepdims=False)
    back = my_starts[:, None] + jnp.arange(chunks_per_row, dtype=jnp.int32)[None, :]
    back = jnp.minimum(back, slots - 1)
    rows = jnp.take(mine, back.reshape(-1), axis=0).reshape(owned, samples)

    table = kernel_table(samples, 0.0, samples)
    recon = invert_block(rows, my_len, table, 0.0)
    return recon[None]


def solution(mesh):
    view_devices = mesh.shape["view"]
    ny = int(round(math.sqrt(view_devices)))
    nz = view_devices // ny
    placed = (P("view", "chord", None), P("view", None, None), P(), P())
    return jax.shard_map(
        functools.partial(per_device, ny, nz),
        mesh=mesh,
        in_specs=placed,
        out_specs=P("chord", "view", None),
        check_vma=False,
    )
```

```python
import functools
import math

import jax
import jax.numpy as jnp
from jax import lax
from jax.experimental import pallas as pl
from jax.experimental.pallas import tpu as pltpu
from jax.sharding import PartitionSpec as P

LANES = 128
PACK = 4608
MESH = pl.DeviceIdType.MESH


def kernel_table(rows, start, cols):
    row_pos = start + jnp.arange(rows, dtype=jnp.float32)[:, None]
    col_pos = jnp.arange(cols, dtype=jnp.float32)[None, :]
    return 1.0 / (row_pos - col_pos + 0.5)


def weigh(length, count, start):
    position = start + jnp.arange(count, dtype=jnp.float32)[None, :] + 0.5
    inside = position < length
    return (inside, jnp.sqrt(jnp.where(inside, position * (length - position), 1.0)))


def invert_block(sums, length, table, start):
    length = length.astype(jnp.float32)[:, None]
    col_in, col_w = weigh(length, sums.shape[1], 0.0)
    row_in, row_w = weigh(length, table.shape[0], start)
    scaled = jnp.where(col_in, col_w * sums, 0.0)
    image = jnp.dot(
        scaled, table.T, precision=lax.Precision.HIGH, preferred_element_type=jnp.float32
    )
    return jnp.where(row_in, image / (math.pi * row_w), 0.0)


def pick(table, index):
    hit = index[:, :, None] == jnp.arange(table.shape[1], dtype=jnp.int32)
    return jnp.sum(jnp.where(hit, table[:, None, :], 0), axis=-1)


def run_rings(rings):
    copies_at = []
    for s in range(max(r["n"] // 2 for r in rings)):
        copies = []
        for r in rings:
            n = r["n"]
            nr = n // 2
            nl = n - 1 - nr
            for go, steps, to, recv, send, sem in (
                (1, nr, r["right"], r["rr"], r["sr"], r["base"] + s),
                (-1, nl, r["left"], r["rl"], r["sl"], r["base"] + nr + s),
            ):
                if s >= steps:
                    continue
                dest = lax.rem(r["me"] + go * (steps - s) + 2 * n, n)
                if s == 0:
                    src = r["chunk"].at[dest]
                else:
                    send[s] = recv[s - 1] + r["chunk"][dest]
                    src = send.at[s]
                copy = pltpu.make_async_remote_copy(
                    src_ref=src,
                    dst_ref=recv.at[s],
                    send_sem=r["ssem"].at[sem],
                    recv_sem=r["rsem"].at[sem],
                    device_id=to,
                    device_id_type=MESH,
                )
                copy.start()
                copies.append(copy)
        for copy in copies:
            copy.wait()
    return [(r["rr"].at[r["n"] // 2 - 1], r["rl"].at[r["n"] - 2 - r["n"] // 2]) for r in rings]


def rs_kernel(ny, nz, xa, xb, oa, ob, s1a, s1b, *bufs):
    ssem, rsem = bufs[-2:]
    bufs = bufs[:-2]
    view = lax.axis_index("view")
    group = lax.axis_index("chord")
    y = view // nz
    z = lax.rem(view, nz)

    def dev(yy, zz):
        return (yy * nz + zz, group)

    z_right = dev(y, lax.rem(z + 1, nz))
    z_left = dev(y, lax.rem(z + nz - 1, nz))
    y_right = dev(lax.rem(y + 1, ny), z)
    y_left = dev(lax.rem(y + ny - 1, ny), z)

    barrier = pltpu.get_barrier_semaphore()
    for peer in (z_right, z_left, y_right, y_left):
        pl.semaphore_signal(barrier, inc=1, device_id=peer, device_id_type=MESH)
    pl.semaphore_wait(barrier, 4)

    def ring(n, me, right, left, chunk, at, base):
        rr, rl, sr, sl = bufs[4 * at: 4 * at + 4]
        return dict(n=n, me=me, right=right, left=left, chunk=chunk, rr=rr, rl=rl, sr=sr, sl=sl,
                    ssem=ssem, rsem=rsem, base=base)

    (ar, al), (br, bl) = run_rings([
        ring(nz, z, z_right, z_left, xa, 0, 0),
        ring(ny, y, y_right, y_left, xb, 1, nz - 1),
    ])
    s1a[...] = xa[z] + ar[...] + al[...]
    s1b[...] = xb[y] + br[...] + bl[...]
    (ar, al), (br, bl) = run_rings([
        ring(ny, y, y_right, y_left, s1a, 2, nz + ny - 2),
        ring(nz, z, z_right, z_left, s1b, 3, nz + 2 * ny - 3),
    ])
    oa[...] = s1a[y] + ar[...] + al[...]
    ob[...] = s1b[z] + br[...] + bl[...]


def reduce_scatter(xa, xb, ny, nz):
    ra, rb = xa.shape[2], xb.shape[2]
    f32 = jnp.float32

    def slots(n, shape):
        return [pltpu.VMEM((n // 2,) + shape, f32), pltpu.VMEM((n - 1 - n // 2,) + shape, f32)] * 2

    bufs = (
        slots(nz, (ny, ra, LANES)) + slots(ny, (nz, rb, LANES))
        + slots(ny, (ra, LANES)) + slots(nz, (rb, LANES))
    )
    return pl.pallas_call(
        functools.partial(rs_kernel, ny, nz),
        out_shape=(jax.ShapeDtypeStruct((ra, LANES), f32), jax.ShapeDtypeStruct((rb, LANES), f32)),
        in_specs=[pl.BlockSpec(memory_space=pltpu.VMEM)] * 2,
        out_specs=(pl.BlockSpec(memory_space=pltpu.VMEM),) * 2,
        scratch_shapes=[pltpu.VMEM((ny, ra, LANES), f32), pltpu.VMEM((nz, rb, LANES), f32)]
        + bufs
        + [pltpu.SemaphoreType.DMA((2 * (nz + ny - 2),)), pltpu.SemaphoreType.DMA((2 * (nz + ny - 2),))],
        compiler_params=pltpu.CompilerParams(collective_id=0, has_side_effects=True),
    )(xa, xb)


def sums_kernel(perm_ref, proj_ref, tiles_ref, out_ref):
    blocks, pair, samples = tiles_ref.shape
    footprint = proj_ref.shape[2]
    per = pair // footprint
    perm = perm_ref[...]
    total = None
    for b in range(blocks):
        lhs = jnp.concatenate(
            [
                jnp.dot(perm, proj_ref[b * per + h], preferred_element_type=jnp.float32)
                for h in range(per)
            ],
            axis=1,
        ).astype(proj_ref.dtype)
        term = jnp.dot(lhs, tiles_ref[b], preferred_element_type=jnp.float32)
        total = term if total is None else total + term
    out_ref[...] = total


def owner_sums(perm, proj, tiles):
    return pl.pallas_call(
        sums_kernel,
        out_shape=jax.ShapeDtypeStruct((proj.shape[1], tiles.shape[2]), jnp.float32),
        in_specs=[pl.BlockSpec(memory_space=pltpu.VMEM)] * 3,
        out_specs=pl.BlockSpec(memory_space=pltpu.VMEM),
    )(perm, proj, tiles)


def per_device(ny, nz, proj, tiles, owner, lengths):
    view_count, group_rows, footprint = proj.shape
    samples = tiles.shape[2]
    group = lax.axis_index("chord")
    view_place = lax.axis_index("view")
    view_devices = ny * nz
    owned = group_rows // view_devices
    chunks_per_row = samples // LANES
    slots = min(chunks_per_row * owned, (PACK + owned * (LANES - 1)) // LANES)

    my_order = lax.dynamic_index_in_dim(owner, group, 0, keepdims=False)
    my_lengths = lax.dynamic_index_in_dim(lengths, group, 0, keepdims=False)
    order_len = pick(my_lengths[None, :], my_order[None, :])
    order_len = order_len.reshape(view_devices, owned)

    perm = (my_order[:, None] == jnp.arange(group_rows, dtype=jnp.int32)[None, :]).astype(proj.dtype)
    sums = owner_sums(perm, proj, tiles)
    blocks = sums.reshape(ny, nz, owned, chunks_per_row, LANES)

    counts = (order_len + LANES - 1) // LANES
    ends = jnp.cumsum(counts, axis=1)
    starts = ends - counts
    slot = jnp.arange(slots, dtype=jnp.int32)
    member = jnp.sum((ends[:, None, :] <= slot[None, :, None]).astype(jnp.int32), axis=2)
    member = jnp.minimum(member, owned - 1)
    first = pick(starts, member)
    within = jnp.clip(slot[None, :] - first, 0, chunks_per_row - 1)
    member = member.reshape(ny, nz, slots)
    within = within.reshape(ny, nz, slots)
    half = (slots + 1) // 2
    choose = (
        (member[..., None, None] == jnp.arange(owned, dtype=jnp.int32)[:, None])
        & (within[..., None, None] == jnp.arange(chunks_per_row, dtype=jnp.int32)[None, :])
    ).astype(jnp.float32)
    xa = jnp.einsum("yzbmc,yzmcl->zybl", choose[:, :, :half], blocks,
                    precision=lax.Precision.HIGHEST, preferred_element_type=jnp.float32)
    xb = jnp.einsum("yzbmc,yzmcl->yzbl", choose[:, :, half:], blocks,
                    precision=lax.Precision.HIGHEST, preferred_element_type=jnp.float32)

    mine = jnp.concatenate(reduce_scatter(xa, xb, ny, nz), axis=0)

    my_starts = lax.dynamic_index_in_dim(starts, view_place, 0, keepdims=False)
    my_len = lax.dynamic_index_in_dim(order_len, view_place, 0, keepdims=False)
    back = my_starts[:, None] + jnp.arange(chunks_per_row, dtype=jnp.int32)[None, :]
    back = jnp.minimum(back, slots - 1)
    rows = jnp.take(mine, back.reshape(-1), axis=0).reshape(owned, samples)

    table = kernel_table(samples, 0.0, samples)
    recon = invert_block(rows, my_len, table, 0.0)
    return recon[None]


def solution(mesh):
    view_devices = mesh.shape["view"]
    ny = int(round(math.sqrt(view_devices)))
    nz = view_devices // ny
    placed = (P("view", "chord", None), P("view", None, None), P(), P())
    return jax.shard_map(
        functools.partial(per_device, ny, nz),
        mesh=mesh,
        in_specs=placed,
        out_specs=P("chord", "view", None),
        check_vma=False,
    )
```

```python
import functools
import math

import jax
import jax.numpy as jnp
from jax import lax
from jax.experimental import pallas as pl
from jax.experimental.pallas import tpu as pltpu
from jax.sharding import PartitionSpec as P

LANES = 128
PACK = 4608
MESH = pl.DeviceIdType.MESH


def kernel_table(rows, start, cols):
    row_pos = start + jnp.arange(rows, dtype=jnp.float32)[:, None]
    col_pos = jnp.arange(cols, dtype=jnp.float32)[None, :]
    return 1.0 / (row_pos - col_pos + 0.5)


def weigh(length, count, start):
    position = start + jnp.arange(count, dtype=jnp.float32)[None, :] + 0.5
    inside = position < length
    return (inside, jnp.sqrt(jnp.where(inside, position * (length - position), 1.0)))


def invert_block(sums, length, table, start):
    length = length.astype(jnp.float32)[:, None]
    col_in, col_w = weigh(length, sums.shape[1], 0.0)
    row_in, row_w = weigh(length, table.shape[0], start)
    scaled = jnp.where(col_in, col_w * sums, 0.0)
    image = jnp.dot(
        scaled, table.T, precision=lax.Precision.HIGH, preferred_element_type=jnp.float32
    )
    return jnp.where(row_in, image / (math.pi * row_w), 0.0)


def pick(table, index):
    hit = index[:, :, None] == jnp.arange(table.shape[1], dtype=jnp.int32)
    return jnp.sum(jnp.where(hit, table[:, None, :], 0), axis=-1)


def run_rings(rings):
    copies_at = []
    for s in range(max(r["n"] // 2 for r in rings)):
        copies = []
        for r in rings:
            n = r["n"]
            nr = n // 2
            nl = n - 1 - nr
            for go, steps, to, recv, send, sem in (
                (1, nr, r["right"], r["rr"], r["sr"], r["base"] + s),
                (-1, nl, r["left"], r["rl"], r["sl"], r["base"] + nr + s),
            ):
                if s >= steps:
                    continue
                dest = lax.rem(r["me"] + go * (steps - s) + 2 * n, n)
                if s == 0:
                    src = r["chunk"].at[dest]
                else:
                    send[s] = recv[s - 1] + r["chunk"][dest]
                    src = send.at[s]
                copy = pltpu.make_async_remote_copy(
                    src_ref=src,
                    dst_ref=recv.at[s],
                    send_sem=r["ssem"].at[sem],
                    recv_sem=r["rsem"].at[sem],
                    device_id=to,
                    device_id_type=MESH,
                )
                copy.start()
                copies.append(copy)
        for copy in copies:
            copy.wait()
    return [(r["rr"].at[r["n"] // 2 - 1], r["rl"].at[r["n"] - 2 - r["n"] // 2]) for r in rings]


def rs_kernel(ny, nz, xa, xb, oa, ob, s1a, s1b, *bufs):
    ssem, rsem = bufs[-2:]
    bufs = bufs[:-2]
    view = lax.axis_index("view")
    group = lax.axis_index("chord")
    y = view // nz
    z = lax.rem(view, nz)

    def dev(yy, zz):
        return (yy * nz + zz, group)

    z_right = dev(y, lax.rem(z + 1, nz))
    z_left = dev(y, lax.rem(z + nz - 1, nz))
    y_right = dev(lax.rem(y + 1, ny), z)
    y_left = dev(lax.rem(y + ny - 1, ny), z)

    barrier = pltpu.get_barrier_semaphore()
    for peer in (z_right, z_left, y_right, y_left):
        pl.semaphore_signal(barrier, inc=1, device_id=peer, device_id_type=MESH)
    pl.semaphore_wait(barrier, 4)

    def ring(n, me, right, left, chunk, at, base):
        rr, rl, sr, sl = bufs[4 * at: 4 * at + 4]
        return dict(n=n, me=me, right=right, left=left, chunk=chunk, rr=rr, rl=rl, sr=sr, sl=sl,
                    ssem=ssem, rsem=rsem, base=base)

    (ar, al), (br, bl) = run_rings([
        ring(nz, z, z_right, z_left, xa, 0, 0),
        ring(ny, y, y_right, y_left, xb, 1, nz - 1),
    ])
    s1a[...] = xa[z] + ar[...] + al[...]
    s1b[...] = xb[y] + br[...] + bl[...]
    (ar, al), (br, bl) = run_rings([
        ring(ny, y, y_right, y_left, s1a, 2, nz + ny - 2),
        ring(nz, z, z_right, z_left, s1b, 3, nz + 2 * ny - 3),
    ])
    oa[...] = s1a[y] + ar[...] + al[...]
    ob[...] = s1b[z] + br[...] + bl[...]


def reduce_scatter(xa, xb, ny, nz):
    ra, rb = xa.shape[2], xb.shape[2]
    f32 = jnp.float32

    def slots(n, shape):
        return [pltpu.VMEM((n // 2,) + shape, f32), pltpu.VMEM((n - 1 - n // 2,) + shape, f32)] * 2

    bufs = (
        slots(nz, (ny, ra, LANES)) + slots(ny, (nz, rb, LANES))
        + slots(ny, (ra, LANES)) + slots(nz, (rb, LANES))
    )
    return pl.pallas_call(
        functools.partial(rs_kernel, ny, nz),
        out_shape=(jax.ShapeDtypeStruct((ra, LANES), f32), jax.ShapeDtypeStruct((rb, LANES), f32)),
        in_specs=[pl.BlockSpec(memory_space=pltpu.VMEM)] * 2,
        out_specs=(pl.BlockSpec(memory_space=pltpu.VMEM),) * 2,
        scratch_shapes=[pltpu.VMEM((ny, ra, LANES), f32), pltpu.VMEM((nz, rb, LANES), f32)]
        + bufs
        + [pltpu.SemaphoreType.DMA((2 * (nz + ny - 2),)), pltpu.SemaphoreType.DMA((2 * (nz + ny - 2),))],
        compiler_params=pltpu.CompilerParams(collective_id=0, has_side_effects=True),
    )(xa, xb)


def sums_kernel(perm_ref, proj_ref, tiles_ref, out_ref):
    blocks, pair, samples = tiles_ref.shape
    footprint = proj_ref.shape[2]
    per = pair // footprint
    perm = perm_ref[...]
    total = None
    for b in range(blocks):
        lhs = jnp.concatenate(
            [
                jnp.dot(perm, proj_ref[b * per + h], preferred_element_type=jnp.float32)
                for h in range(per)
            ],
            axis=1,
        ).astype(proj_ref.dtype)
        term = jnp.dot(lhs, tiles_ref[b], preferred_element_type=jnp.float32)
        total = term if total is None else total + term
    out_ref[...] = total


def owner_sums(perm, proj, tiles):
    return pl.pallas_call(
        sums_kernel,
        out_shape=jax.ShapeDtypeStruct((proj.shape[1], tiles.shape[2]), jnp.float32),
        in_specs=[pl.BlockSpec(memory_space=pltpu.VMEM)] * 3,
        out_specs=pl.BlockSpec(memory_space=pltpu.VMEM),
    )(perm, proj, tiles)


def per_device(ny, nz, proj, tiles, owner, lengths):
    view_count, group_rows, footprint = proj.shape
    samples = tiles.shape[2]
    group = lax.axis_index("chord")
    view_place = lax.axis_index("view")
    view_devices = ny * nz
    owned = group_rows // view_devices
    chunks_per_row = samples // LANES
    slots = min(chunks_per_row * owned, (PACK + owned * (LANES - 1)) // LANES)

    my_order = lax.dynamic_index_in_dim(owner, group, 0, keepdims=False)
    my_lengths = lax.dynamic_index_in_dim(lengths, group, 0, keepdims=False)
    order_len = pick(my_lengths[None, :], my_order[None, :])
    order_len = order_len.reshape(view_devices, owned)

    perm = (my_order[:, None] == jnp.arange(group_rows, dtype=jnp.int32)[None, :]).astype(proj.dtype)
    sums = owner_sums(perm, proj, tiles)
    blocks = sums.reshape(ny, nz, owned, chunks_per_row, LANES)

    counts = (order_len + LANES - 1) // LANES
    ends = jnp.cumsum(counts, axis=1)
    starts = ends - counts
    slot = jnp.arange(slots, dtype=jnp.int32)
    member = jnp.sum((ends[:, None, :] <= slot[None, :, None]).astype(jnp.int32), axis=2)
    member = jnp.minimum(member, owned - 1)
    first = pick(starts, member)
    within = jnp.clip(slot[None, :] - first, 0, chunks_per_row - 1)
    member = member.reshape(ny, nz, slots)
    within = within.reshape(ny, nz, slots)
    half = (slots + 1) // 2
    choose = (
        (member[..., None, None] == jnp.arange(owned, dtype=jnp.int32)[:, None])
        & (within[..., None, None] == jnp.arange(chunks_per_row, dtype=jnp.int32)[None, :])
    ).astype(jnp.float32)
    bf16 = jnp.bfloat16
    hi = lax.reduce_precision(blocks, exponent_bits=8, mantissa_bits=7)
    rest = blocks - hi
    mid = lax.reduce_precision(rest, exponent_bits=8, mantissa_bits=7)
    lo = rest - mid
    parts = jnp.stack([hi, mid, lo]).astype(bf16)
    choose = choose.astype(bf16)
    xa = jnp.einsum("yzbmc,pyzmcl->pzybl", choose[:, :, :half], parts,
                    preferred_element_type=jnp.float32).sum(axis=0)
    xb = jnp.einsum("yzbmc,pyzmcl->pyzbl", choose[:, :, half:], parts,
                    preferred_element_type=jnp.float32).sum(axis=0)

    mine = jnp.concatenate(reduce_scatter(xa, xb, ny, nz), axis=0)

    my_starts = lax.dynamic_index_in_dim(starts, view_place, 0, keepdims=False)
    my_len = lax.dynamic_index_in_dim(order_len, view_place, 0, keepdims=False)
    back = my_starts[:, None] + jnp.arange(chunks_per_row, dtype=jnp.int32)[None, :]
    back = jnp.minimum(back, slots - 1)
    rows = jnp.take(mine, back.reshape(-1), axis=0).reshape(owned, samples)

    table = kernel_table(samples, 0.0, samples)
    recon = invert_block(rows, my_len, table, 0.0)
    return recon[None]


def solution(mesh):
    view_devices = mesh.shape["view"]
    ny = int(round(math.sqrt(view_devices)))
    nz = view_devices // ny
    placed = (P("view", "chord", None), P("view", None, None), P(), P())
    return jax.shard_map(
        functools.partial(per_device, ny, nz),
        mesh=mesh,
        in_specs=placed,
        out_specs=P("chord", "view", None),
        check_vma=False,
    )
```

```python
import functools
import math

import jax
import jax.numpy as jnp
from jax import lax
from jax.experimental import pallas as pl
from jax.experimental.pallas import tpu as pltpu
from jax.sharding import PartitionSpec as P

LANES = 128
PACK = 4608
MESH = pl.DeviceIdType.MESH


def kernel_table(rows, start, cols):
    row_pos = start + jnp.arange(rows, dtype=jnp.float32)[:, None]
    col_pos = jnp.arange(cols, dtype=jnp.float32)[None, :]
    return 1.0 / (row_pos - col_pos + 0.5)


def weigh(length, count, start):
    position = start + jnp.arange(count, dtype=jnp.float32)[None, :] + 0.5
    inside = position < length
    return (inside, jnp.sqrt(jnp.where(inside, position * (length - position), 1.0)))


def invert_block(sums, length, table, start):
    length = length.astype(jnp.float32)[:, None]
    col_in, col_w = weigh(length, sums.shape[1], 0.0)
    row_in, row_w = weigh(length, table.shape[0], start)
    scaled = jnp.where(col_in, col_w * sums, 0.0)
    image = jnp.dot(
        scaled, table.T, precision=lax.Precision.HIGH, preferred_element_type=jnp.float32
    )
    return jnp.where(row_in, image / (math.pi * row_w), 0.0)


def pick(table, index):
    hit = index[:, :, None] == jnp.arange(table.shape[1], dtype=jnp.int32)
    return jnp.sum(jnp.where(hit, table[:, None, :], 0), axis=-1)


def run_rings(rings):
    copies_at = []
    for s in range(max(r["n"] // 2 for r in rings)):
        copies = []
        for r in rings:
            n = r["n"]
            nr = n // 2
            nl = n - 1 - nr
            for go, steps, to, recv, send, sem in (
                (1, nr, r["right"], r["rr"], r["sr"], r["base"] + s),
                (-1, nl, r["left"], r["rl"], r["sl"], r["base"] + nr + s),
            ):
                if s >= steps:
                    continue
                dest = lax.rem(r["me"] + go * (steps - s) + 2 * n, n)
                if s == 0:
                    src = r["chunk"].at[dest]
                else:
                    send[s] = recv[s - 1] + r["chunk"][dest]
                    src = send.at[s]
                copy = pltpu.make_async_remote_copy(
                    src_ref=src,
                    dst_ref=recv.at[s],
                    send_sem=r["ssem"].at[sem],
                    recv_sem=r["rsem"].at[sem],
                    device_id=to,
                    device_id_type=MESH,
                )
                copy.start()
                copies.append(copy)
        for copy in copies:
            copy.wait()
    return [(r["rr"].at[r["n"] // 2 - 1], r["rl"].at[r["n"] - 2 - r["n"] // 2]) for r in rings]


def run_direct(rings):
    copies = []
    for r in rings:
        n = r["n"]
        for k in range(1, n):
            dest = lax.rem(r["me"] + k, n)
            copy = pltpu.make_async_remote_copy(
                src_ref=r["chunk"].at[dest],
                dst_ref=r["recv"].at[k - 1],
                send_sem=r["ssem"].at[r["base"] + k - 1],
                recv_sem=r["rsem"].at[r["base"] + k - 1],
                device_id=r["dev"](dest),
                device_id_type=MESH,
            )
            copy.start()
            copies.append(copy)
    for copy in copies:
        copy.wait()


def rs_kernel(ny, nz, xa, xb, oa, ob, s1a, s1b, *bufs):
    ssem, rsem = bufs[-2:]
    bufs = bufs[:-2]
    view = lax.axis_index("view")
    group = lax.axis_index("chord")
    y = view // nz
    z = lax.rem(view, nz)

    def dev(yy, zz):
        return (yy * nz + zz, group)

    z_right = dev(y, lax.rem(z + 1, nz))
    z_left = dev(y, lax.rem(z + nz - 1, nz))
    y_right = dev(lax.rem(y + 1, ny), z)
    y_left = dev(lax.rem(y + ny - 1, ny), z)

    barrier = pltpu.get_barrier_semaphore()
    for k in range(1, ny):
        pl.semaphore_signal(barrier, inc=1, device_id=dev(lax.rem(y + k, ny), z), device_id_type=MESH)
    for k in range(1, nz):
        pl.semaphore_signal(barrier, inc=1, device_id=dev(y, lax.rem(z + k, nz)), device_id_type=MESH)
    pl.semaphore_wait(barrier, ny + nz - 2)

    def ring(n, me, right, left, chunk, at, base):
        rr, rl, sr, sl = bufs[4 * at: 4 * at + 4]
        return dict(n=n, me=me, right=right, left=left, chunk=chunk, rr=rr, rl=rl, sr=sr, sl=sl,
                    ssem=ssem, rsem=rsem, base=base)

    (ar, al), (br, bl) = run_rings([
        ring(nz, z, z_right, z_left, xa, 0, 0),
        ring(ny, y, y_right, y_left, xb, 1, nz - 1),
    ])
    s1a[...] = xa[z] + ar[...] + al[...]
    s1b[...] = xb[y] + br[...] + bl[...]
    recv_a, recv_b = bufs[8], bufs[9]
    run_direct([
        dict(n=ny, me=y, dev=lambda d: dev(d, z), chunk=s1a, recv=recv_a,
             ssem=ssem, rsem=rsem, base=nz + ny - 2),
        dict(n=nz, me=z, dev=lambda d: dev(y, d), chunk=s1b, recv=recv_b,
             ssem=ssem, rsem=rsem, base=nz + 2 * ny - 3),
    ])
    oa[...] = s1a[y] + jnp.sum(recv_a[...], axis=0)
    ob[...] = s1b[z] + jnp.sum(recv_b[...], axis=0)


def reduce_scatter(xa, xb, ny, nz):
    ra, rb = xa.shape[2], xb.shape[2]
    f32 = jnp.float32

    def slots(n, shape):
        return [pltpu.VMEM((n // 2,) + shape, f32), pltpu.VMEM((n - 1 - n // 2,) + shape, f32)] * 2

    bufs = (
        slots(nz, (ny, ra, LANES)) + slots(ny, (nz, rb, LANES))
        + [pltpu.VMEM((ny - 1, ra, LANES), f32), pltpu.VMEM((nz - 1, rb, LANES), f32)]
    )
    return pl.pallas_call(
        functools.partial(rs_kernel, ny, nz),
        out_shape=(jax.ShapeDtypeStruct((ra, LANES), f32), jax.ShapeDtypeStruct((rb, LANES), f32)),
        in_specs=[pl.BlockSpec(memory_space=pltpu.VMEM)] * 2,
        out_specs=(pl.BlockSpec(memory_space=pltpu.VMEM),) * 2,
        scratch_shapes=[pltpu.VMEM((ny, ra, LANES), f32), pltpu.VMEM((nz, rb, LANES), f32)]
        + bufs
        + [pltpu.SemaphoreType.DMA((2 * (nz + ny - 2),)), pltpu.SemaphoreType.DMA((2 * (nz + ny - 2),))],
        compiler_params=pltpu.CompilerParams(collective_id=0, has_side_effects=True),
    )(xa, xb)


def sums_kernel(perm_ref, proj_ref, tiles_ref, out_ref):
    blocks, pair, samples = tiles_ref.shape
    footprint = proj_ref.shape[2]
    per = pair // footprint
    perm = perm_ref[...]
    total = None
    for b in range(blocks):
        lhs = jnp.concatenate(
            [
                jnp.dot(perm, proj_ref[b * per + h], preferred_element_type=jnp.float32)
                for h in range(per)
            ],
            axis=1,
        ).astype(proj_ref.dtype)
        term = jnp.dot(lhs, tiles_ref[b], preferred_element_type=jnp.float32)
        total = term if total is None else total + term
    out_ref[...] = total


def owner_sums(perm, proj, tiles):
    return pl.pallas_call(
        sums_kernel,
        out_shape=jax.ShapeDtypeStruct((proj.shape[1], tiles.shape[2]), jnp.float32),
        in_specs=[pl.BlockSpec(memory_space=pltpu.VMEM)] * 3,
        out_specs=pl.BlockSpec(memory_space=pltpu.VMEM),
    )(perm, proj, tiles)


def per_device(ny, nz, proj, tiles, owner, lengths):
    view_count, group_rows, footprint = proj.shape
    samples = tiles.shape[2]
    group = lax.axis_index("chord")
    view_place = lax.axis_index("view")
    view_devices = ny * nz
    owned = group_rows // view_devices
    chunks_per_row = samples // LANES
    slots = min(chunks_per_row * owned, (PACK + owned * (LANES - 1)) // LANES)

    my_order = lax.dynamic_index_in_dim(owner, group, 0, keepdims=False)
    my_lengths = lax.dynamic_index_in_dim(lengths, group, 0, keepdims=False)
    order_len = pick(my_lengths[None, :], my_order[None, :])
    order_len = order_len.reshape(view_devices, owned)

    perm = (my_order[:, None] == jnp.arange(group_rows, dtype=jnp.int32)[None, :]).astype(proj.dtype)
    sums = owner_sums(perm, proj, tiles)
    blocks = sums.reshape(ny, nz, owned, chunks_per_row, LANES)

    counts = (order_len + LANES - 1) // LANES
    ends = jnp.cumsum(counts, axis=1)
    starts = ends - counts
    slot = jnp.arange(slots, dtype=jnp.int32)
    member = jnp.sum((ends[:, None, :] <= slot[None, :, None]).astype(jnp.int32), axis=2)
    member = jnp.minimum(member, owned - 1)
    first = pick(starts, member)
    within = jnp.clip(slot[None, :] - first, 0, chunks_per_row - 1)
    member = member.reshape(ny, nz, slots)
    within = within.reshape(ny, nz, slots)
    half = (slots + 1) // 2
    choose = (
        (member[..., None, None] == jnp.arange(owned, dtype=jnp.int32)[:, None])
        & (within[..., None, None] == jnp.arange(chunks_per_row, dtype=jnp.int32)[None, :])
    ).astype(jnp.float32)
    bf16 = jnp.bfloat16
    hi = lax.reduce_precision(blocks, exponent_bits=8, mantissa_bits=7)
    rest = blocks - hi
    mid = lax.reduce_precision(rest, exponent_bits=8, mantissa_bits=7)
    lo = rest - mid
    parts = jnp.stack([hi, mid, lo]).astype(bf16)
    choose = choose.astype(bf16)
    xa = jnp.einsum("yzbmc,pyzmcl->pzybl", choose[:, :, :half], parts,
                    preferred_element_type=jnp.float32).sum(axis=0)
    xb = jnp.einsum("yzbmc,pyzmcl->pyzbl", choose[:, :, half:], parts,
                    preferred_element_type=jnp.float32).sum(axis=0)

    mine = jnp.concatenate(reduce_scatter(xa, xb, ny, nz), axis=0)

    my_starts = lax.dynamic_index_in_dim(starts, view_place, 0, keepdims=False)
    my_len = lax.dynamic_index_in_dim(order_len, view_place, 0, keepdims=False)
    back = my_starts[:, None] + jnp.arange(chunks_per_row, dtype=jnp.int32)[None, :]
    back = jnp.minimum(back, slots - 1)
    rows = jnp.take(mine, back.reshape(-1), axis=0).reshape(owned, samples)

    table = kernel_table(samples, 0.0, samples)
    recon = invert_block(rows, my_len, table, 0.0)
    return recon[None]


def solution(mesh):
    view_devices = mesh.shape["view"]
    ny = int(round(math.sqrt(view_devices)))
    nz = view_devices // ny
    placed = (P("view", "chord", None), P("view", None, None), P(), P())
    return jax.shard_map(
        functools.partial(per_device, ny, nz),
        mesh=mesh,
        in_specs=placed,
        out_specs=P("chord", "view", None),
        check_vma=False,
    )
```

```python
import functools
import math

import jax
import jax.numpy as jnp
from jax import lax
from jax.experimental import pallas as pl
from jax.experimental.pallas import tpu as pltpu
from jax.sharding import PartitionSpec as P

LANES = 128
PACK = 4608
MESH = pl.DeviceIdType.MESH


def kernel_table(rows, start, cols):
    row_pos = start + jnp.arange(rows, dtype=jnp.float32)[:, None]
    col_pos = jnp.arange(cols, dtype=jnp.float32)[None, :]
    return 1.0 / (row_pos - col_pos + 0.5)


def weigh(length, count, start):
    position = start + jnp.arange(count, dtype=jnp.float32)[None, :] + 0.5
    inside = position < length
    return (inside, jnp.sqrt(jnp.where(inside, position * (length - position), 1.0)))


def invert_block(sums, length, table, start):
    length = length.astype(jnp.float32)[:, None]
    col_in, col_w = weigh(length, sums.shape[1], 0.0)
    row_in, row_w = weigh(length, table.shape[0], start)
    scaled = jnp.where(col_in, col_w * sums, 0.0)
    image = jnp.dot(
        scaled, table.T, precision=lax.Precision.HIGH, preferred_element_type=jnp.float32
    )
    return jnp.where(row_in, image / (math.pi * row_w), 0.0)


def pick(table, index):
    hit = index[:, :, None] == jnp.arange(table.shape[1], dtype=jnp.int32)
    return jnp.sum(jnp.where(hit, table[:, None, :], 0), axis=-1)


def run_rings(rings):
    chains = []
    for r in rings:
        n = r["n"]
        nr = n // 2
        nl = n - 1 - nr
        chains.append((r, 1, nr, r["right"], r["rr"], r["sr"], r["base"]))
        chains.append((r, -1, nl, r["left"], r["rl"], r["sl"], r["base"] + nr))
    pending = [None] * len(chains)
    for s in range(max(c[2] for c in chains)):
        for i, (r, go, steps, to, recv, send, base) in enumerate(chains):
            if s >= steps:
                continue
            n = r["n"]
            dest = lax.rem(r["me"] + go * (steps - s) + 2 * n, n)
            if s == 0:
                src = r["src"](dest)
            else:
                pending[i].wait()
                send[s] = recv[s - 1] + r["val"](dest)
                src = send.at[s]
            copy = pltpu.make_async_remote_copy(
                src_ref=src,
                dst_ref=recv.at[s],
                send_sem=r["ssem"].at[base + s],
                recv_sem=r["rsem"].at[base + s],
                device_id=to,
                device_id_type=MESH,
            )
            copy.start()
            pending[i] = copy
    for copy in pending:
        copy.wait()
    return [(r["rr"].at[r["n"] // 2 - 1], r["rl"].at[r["n"] - 2 - r["n"] // 2]) for r in rings]


def run_direct(rings):
    copies = []
    for r in rings:
        n = r["n"]
        for k in range(1, n):
            dest = lax.rem(r["me"] + k, n)
            copy = pltpu.make_async_remote_copy(
                src_ref=r["chunk"].at[dest],
                dst_ref=r["recv"].at[k - 1],
                send_sem=r["ssem"].at[r["base"] + k - 1],
                recv_sem=r["rsem"].at[r["base"] + k - 1],
                device_id=r["dev"](dest),
                device_id_type=MESH,
            )
            copy.start()
            copies.append(copy)
    for copy in copies:
        copy.wait()


def rs_kernel(ny, nz, xa, xb, oa, ob, s1a, s1b, *bufs):
    ssem, rsem = bufs[-2:]
    bufs = bufs[:-2]
    view = lax.axis_index("view")
    group = lax.axis_index("chord")
    y = view // nz
    z = lax.rem(view, nz)

    def dev(yy, zz):
        return (yy * nz + zz, group)

    z_right = dev(y, lax.rem(z + 1, nz))
    z_left = dev(y, lax.rem(z + nz - 1, nz))
    y_right = dev(lax.rem(y + 1, ny), z)
    y_left = dev(lax.rem(y + ny - 1, ny), z)

    barrier = pltpu.get_barrier_semaphore()
    for k in range(1, ny):
        pl.semaphore_signal(barrier, inc=1, device_id=dev(lax.rem(y + k, ny), z), device_id_type=MESH)
    for k in range(1, nz):
        pl.semaphore_signal(barrier, inc=1, device_id=dev(y, lax.rem(z + k, nz)), device_id_type=MESH)
    pl.semaphore_wait(barrier, ny + nz - 2)

    def ring(n, me, right, left, x, part, at, base):
        rr, rl, sr, sl = bufs[4 * at: 4 * at + 4]
        return dict(n=n, me=me, right=right, left=left, rr=rr, rl=rl, sr=sr, sl=sl,
                    src=lambda d: x.at[d, part], val=lambda d: x[d, part],
                    ssem=ssem, rsem=rsem, base=base)

    ha, hb = ny // 2, nz // 2
    lo_a, hi_a = pl.ds(0, ha), pl.ds(ha, ny - ha)
    lo_b, hi_b = pl.ds(0, hb), pl.ds(hb, nz - hb)
    fins = run_rings([
        ring(nz, z, z_right, z_left, xa, lo_a, 0, 0),
        ring(nz, z, z_right, z_left, xa, hi_a, 1, nz - 1),
        ring(ny, y, y_right, y_left, xb, lo_b, 2, 2 * (nz - 1)),
        ring(ny, y, y_right, y_left, xb, hi_b, 3, 2 * (nz - 1) + ny - 1),
    ])
    s1a[lo_a] = xa[z, lo_a] + fins[0][0][...] + fins[0][1][...]
    s1a[hi_a] = xa[z, hi_a] + fins[1][0][...] + fins[1][1][...]
    s1b[lo_b] = xb[y, lo_b] + fins[2][0][...] + fins[2][1][...]
    s1b[hi_b] = xb[y, hi_b] + fins[3][0][...] + fins[3][1][...]
    recv_a, recv_b = bufs[16], bufs[17]
    run_direct([
        dict(n=ny, me=y, dev=lambda d: dev(d, z), chunk=s1a, recv=recv_a,
             ssem=ssem, rsem=rsem, base=2 * (nz + ny - 2)),
        dict(n=nz, me=z, dev=lambda d: dev(y, d), chunk=s1b, recv=recv_b,
             ssem=ssem, rsem=rsem, base=2 * (nz + ny - 2) + ny - 1),
    ])
    oa[...] = s1a[y] + jnp.sum(recv_a[...], axis=0)
    ob[...] = s1b[z] + jnp.sum(recv_b[...], axis=0)


def reduce_scatter(xa, xb, ny, nz):
    ra, rb = xa.shape[2], xb.shape[2]
    f32 = jnp.float32

    def slots(n, shape):
        return [pltpu.VMEM((n // 2,) + shape, f32), pltpu.VMEM((n - 1 - n // 2,) + shape, f32)] * 2

    ha, hb = ny // 2, nz // 2
    bufs = (
        slots(nz, (ha, ra, LANES)) + slots(nz, (ny - ha, ra, LANES))
        + slots(ny, (hb, rb, LANES)) + slots(ny, (nz - hb, rb, LANES))
        + [pltpu.VMEM((ny - 1, ra, LANES), f32), pltpu.VMEM((nz - 1, rb, LANES), f32)]
    )
    return pl.pallas_call(
        functools.partial(rs_kernel, ny, nz),
        out_shape=(jax.ShapeDtypeStruct((ra, LANES), f32), jax.ShapeDtypeStruct((rb, LANES), f32)),
        in_specs=[pl.BlockSpec(memory_space=pltpu.VMEM)] * 2,
        out_specs=(pl.BlockSpec(memory_space=pltpu.VMEM),) * 2,
        scratch_shapes=[pltpu.VMEM((ny, ra, LANES), f32), pltpu.VMEM((nz, rb, LANES), f32)]
        + bufs
        + [pltpu.SemaphoreType.DMA((3 * (nz + ny - 2),)), pltpu.SemaphoreType.DMA((3 * (nz + ny - 2),))],
        compiler_params=pltpu.CompilerParams(collective_id=0, has_side_effects=True),
    )(xa, xb)


def sums_kernel(perm_ref, proj_ref, tiles_ref, out_ref):
    blocks, pair, samples = tiles_ref.shape
    footprint = proj_ref.shape[2]
    per = pair // footprint
    perm = perm_ref[...]
    total = None
    for b in range(blocks):
        lhs = jnp.concatenate(
            [
                jnp.dot(perm, proj_ref[b * per + h], preferred_element_type=jnp.float32)
                for h in range(per)
            ],
            axis=1,
        ).astype(proj_ref.dtype)
        term = jnp.dot(lhs, tiles_ref[b], preferred_element_type=jnp.float32)
        total = term if total is None else total + term
    out_ref[...] = total


def owner_sums(perm, proj, tiles):
    return pl.pallas_call(
        sums_kernel,
        out_shape=jax.ShapeDtypeStruct((proj.shape[1], tiles.shape[2]), jnp.float32),
        in_specs=[pl.BlockSpec(memory_space=pltpu.VMEM)] * 3,
        out_specs=pl.BlockSpec(memory_space=pltpu.VMEM),
    )(perm, proj, tiles)


def per_device(ny, nz, proj, tiles, owner, lengths):
    view_count, group_rows, footprint = proj.shape
    samples = tiles.shape[2]
    group = lax.axis_index("chord")
    view_place = lax.axis_index("view")
    view_devices = ny * nz
    owned = group_rows // view_devices
    chunks_per_row = samples // LANES
    slots = min(chunks_per_row * owned, (PACK + owned * (LANES - 1)) // LANES)

    my_order = lax.dynamic_index_in_dim(owner, group, 0, keepdims=False)
    my_lengths = lax.dynamic_index_in_dim(lengths, group, 0, keepdims=False)
    order_len = pick(my_lengths[None, :], my_order[None, :])
    order_len = order_len.reshape(view_devices, owned)

    perm = (my_order[:, None] == jnp.arange(group_rows, dtype=jnp.int32)[None, :]).astype(proj.dtype)
    sums = owner_sums(perm, proj, tiles)
    blocks = sums.reshape(ny, nz, owned, chunks_per_row, LANES)

    counts = (order_len + LANES - 1) // LANES
    ends = jnp.cumsum(counts, axis=1)
    starts = ends - counts
    slot = jnp.arange(slots, dtype=jnp.int32)
    member = jnp.sum((ends[:, None, :] <= slot[None, :, None]).astype(jnp.int32), axis=2)
    member = jnp.minimum(member, owned - 1)
    first = pick(starts, member)
    within = jnp.clip(slot[None, :] - first, 0, chunks_per_row - 1)
    member = member.reshape(ny, nz, slots)
    within = within.reshape(ny, nz, slots)
    half = (slots + 1) // 2
    choose = (
        (member[..., None, None] == jnp.arange(owned, dtype=jnp.int32)[:, None])
        & (within[..., None, None] == jnp.arange(chunks_per_row, dtype=jnp.int32)[None, :])
    ).astype(jnp.float32)
    bf16 = jnp.bfloat16
    hi = lax.reduce_precision(blocks, exponent_bits=8, mantissa_bits=7)
    rest = blocks - hi
    mid = lax.reduce_precision(rest, exponent_bits=8, mantissa_bits=7)
    lo = rest - mid
    parts = jnp.stack([hi, mid, lo]).astype(bf16)
    choose = choose.astype(bf16)
    xa = jnp.einsum("yzbmc,pyzmcl->pzybl", choose[:, :, :half], parts,
                    preferred_element_type=jnp.float32).sum(axis=0)
    xb = jnp.einsum("yzbmc,pyzmcl->pyzbl", choose[:, :, half:], parts,
                    preferred_element_type=jnp.float32).sum(axis=0)

    mine = jnp.concatenate(reduce_scatter(xa, xb, ny, nz), axis=0)

    my_starts = lax.dynamic_index_in_dim(starts, view_place, 0, keepdims=False)
    my_len = lax.dynamic_index_in_dim(order_len, view_place, 0, keepdims=False)
    back = my_starts[:, None] + jnp.arange(chunks_per_row, dtype=jnp.int32)[None, :]
    back = jnp.minimum(back, slots - 1)
    rows = jnp.take(mine, back.reshape(-1), axis=0).reshape(owned, samples)

    table = kernel_table(samples, 0.0, samples)
    recon = invert_block(rows, my_len, table, 0.0)
    return recon[None]


def solution(mesh):
    view_devices = mesh.shape["view"]
    ny = int(round(math.sqrt(view_devices)))
    nz = view_devices // ny
    placed = (P("view", "chord", None), P("view", None, None), P(), P())
    return jax.shard_map(
        functools.partial(per_device, ny, nz),
        mesh=mesh,
        in_specs=placed,
        out_specs=P("chord", "view", None),
        check_vma=False,
    )
```

```python
import functools
import math

import jax
import jax.numpy as jnp
from jax import lax
from jax.experimental import pallas as pl
from jax.experimental.pallas import tpu as pltpu
from jax.sharding import PartitionSpec as P

LANES = 128
PACK = 4608
MESH = pl.DeviceIdType.MESH


def kernel_table(rows, start, cols):
    row_pos = start + jnp.arange(rows, dtype=jnp.float32)[:, None]
    col_pos = jnp.arange(cols, dtype=jnp.float32)[None, :]
    return 1.0 / (row_pos - col_pos + 0.5)


def weigh(length, count, start):
    position = start + jnp.arange(count, dtype=jnp.float32)[None, :] + 0.5
    inside = position < length
    return (inside, jnp.sqrt(jnp.where(inside, position * (length - position), 1.0)))


def invert_block(sums, length, table, start):
    length = length.astype(jnp.float32)[:, None]
    col_in, col_w = weigh(length, sums.shape[1], 0.0)
    row_in, row_w = weigh(length, table.shape[0], start)
    scaled = jnp.where(col_in, col_w * sums, 0.0)
    image = jnp.dot(
        scaled, table.T, precision=lax.Precision.HIGH, preferred_element_type=jnp.float32
    )
    return jnp.where(row_in, image / (math.pi * row_w), 0.0)


def pick(table, index):
    hit = index[:, :, None] == jnp.arange(table.shape[1], dtype=jnp.int32)
    return jnp.sum(jnp.where(hit, table[:, None, :], 0), axis=-1)


def run_rings(rings):
    chains = []
    for r in rings:
        n = r["n"]
        nr = n // 2
        nl = n - 1 - nr
        chains.append((r, 1, nr, r["right"], r["rr"], r["sr"], r["base"]))
        chains.append((r, -1, nl, r["left"], r["rl"], r["sl"], r["base"] + nr))
    pending = [None] * len(chains)
    for s in range(max(c[2] for c in chains)):
        for i, (r, go, steps, to, recv, send, base) in enumerate(chains):
            if s >= steps:
                continue
            n = r["n"]
            dest = lax.rem(r["me"] + go * (steps - s) + 2 * n, n)
            if s == 0:
                src = r["src"](dest)
            else:
                pending[i].wait()
                send[s] = recv[s - 1] + r["val"](dest)
                src = send.at[s]
            copy = pltpu.make_async_remote_copy(
                src_ref=src,
                dst_ref=recv.at[s],
                send_sem=r["ssem"].at[base + s],
                recv_sem=r["rsem"].at[base + s],
                device_id=to,
                device_id_type=MESH,
            )
            copy.start()
            pending[i] = copy
    for copy in pending:
        copy.wait()
    return [(r["rr"].at[r["n"] // 2 - 1], r["rl"].at[r["n"] - 2 - r["n"] // 2]) for r in rings]


def run_direct(rings):
    copies = []
    for r in rings:
        n = r["n"]
        for k in range(1, n):
            dest = lax.rem(r["me"] + k, n)
            copy = pltpu.make_async_remote_copy(
                src_ref=r["chunk"].at[dest],
                dst_ref=r["recv"].at[k - 1],
                send_sem=r["ssem"].at[r["base"] + k - 1],
                recv_sem=r["rsem"].at[r["base"] + k - 1],
                device_id=r["dev"](dest),
                device_id_type=MESH,
            )
            copy.start()
            copies.append(copy)
    for copy in copies:
        copy.wait()


def rs_kernel(ny, nz, xa, xb, oa, ob, s1a, s1b, *bufs):
    ssem, rsem = bufs[-2:]
    bufs = bufs[:-2]
    view = lax.axis_index("view")
    group = lax.axis_index("chord")
    y = view // nz
    z = lax.rem(view, nz)

    def dev(yy, zz):
        return (yy * nz + zz, group)

    z_right = dev(y, lax.rem(z + 1, nz))
    z_left = dev(y, lax.rem(z + nz - 1, nz))
    y_right = dev(lax.rem(y + 1, ny), z)
    y_left = dev(lax.rem(y + ny - 1, ny), z)

    barrier = pltpu.get_barrier_semaphore()
    for k in range(1, ny):
        pl.semaphore_signal(barrier, inc=1, device_id=dev(lax.rem(y + k, ny), z), device_id_type=MESH)
    for k in range(1, nz):
        pl.semaphore_signal(barrier, inc=1, device_id=dev(y, lax.rem(z + k, nz)), device_id_type=MESH)
    pl.semaphore_wait(barrier, ny + nz - 2)

    def ring(n, me, right, left, x, part, at, base):
        rr, rl, sr, sl = bufs[4 * at: 4 * at + 4]
        return dict(n=n, me=me, right=right, left=left, rr=rr, rl=rl, sr=sr, sl=sl,
                    src=lambda d: x.at[d, part], val=lambda d: x[d, part],
                    ssem=ssem, rsem=rsem, base=base)

    ha, hb = ny // 2, nz // 2
    lo_a, hi_a = pl.ds(0, ha), pl.ds(ha, ny - ha)
    lo_b, hi_b = pl.ds(0, hb), pl.ds(hb, nz - hb)
    fins = run_rings([
        ring(nz, z, z_right, z_left, xa, lo_a, 0, 0),
        ring(nz, z, z_right, z_left, xa, hi_a, 1, nz - 1),
        ring(ny, y, y_right, y_left, xb, lo_b, 2, 2 * (nz - 1)),
        ring(ny, y, y_right, y_left, xb, hi_b, 3, 2 * (nz - 1) + ny - 1),
    ])
    s1a[lo_a] = xa[z, lo_a] + fins[0][0][...] + fins[0][1][...]
    s1a[hi_a] = xa[z, hi_a] + fins[1][0][...] + fins[1][1][...]
    s1b[lo_b] = xb[y, lo_b] + fins[2][0][...] + fins[2][1][...]
    s1b[hi_b] = xb[y, hi_b] + fins[3][0][...] + fins[3][1][...]
    recv_a, recv_b = bufs[16], bufs[17]
    run_direct([
        dict(n=ny, me=y, dev=lambda d: dev(d, z), chunk=s1a, recv=recv_a,
             ssem=ssem, rsem=rsem, base=2 * (nz + ny - 2)),
        dict(n=nz, me=z, dev=lambda d: dev(y, d), chunk=s1b, recv=recv_b,
             ssem=ssem, rsem=rsem, base=2 * (nz + ny - 2) + ny - 1),
    ])
    oa[...] = s1a[y] + jnp.sum(recv_a[...], axis=0)
    ob[...] = s1b[z] + jnp.sum(recv_b[...], axis=0)


def reduce_scatter(xa, xb, ny, nz):
    ra, rb = xa.shape[2], xb.shape[2]
    f32 = jnp.float32

    def slots(n, shape):
        return [pltpu.VMEM((n // 2,) + shape, f32), pltpu.VMEM((n - 1 - n // 2,) + shape, f32)] * 2

    ha, hb = ny // 2, nz // 2
    bufs = (
        slots(nz, (ha, ra, LANES)) + slots(nz, (ny - ha, ra, LANES))
        + slots(ny, (hb, rb, LANES)) + slots(ny, (nz - hb, rb, LANES))
        + [pltpu.VMEM((ny - 1, ra, LANES), f32), pltpu.VMEM((nz - 1, rb, LANES), f32)]
    )
    return pl.pallas_call(
        functools.partial(rs_kernel, ny, nz),
        out_shape=(jax.ShapeDtypeStruct((ra, LANES), f32), jax.ShapeDtypeStruct((rb, LANES), f32)),
        in_specs=[pl.BlockSpec(memory_space=pltpu.VMEM)] * 2,
        out_specs=(pl.BlockSpec(memory_space=pltpu.VMEM),) * 2,
        scratch_shapes=[pltpu.VMEM((ny, ra, LANES), f32), pltpu.VMEM((nz, rb, LANES), f32)]
        + bufs
        + [pltpu.SemaphoreType.DMA((3 * (nz + ny - 2),)), pltpu.SemaphoreType.DMA((3 * (nz + ny - 2),))],
        compiler_params=pltpu.CompilerParams(collective_id=0, has_side_effects=True),
    )(xa, xb)


def sums_kernel(proj_ref, tiles_ref, out_ref):
    blocks, pair, samples = tiles_ref.shape
    footprint = proj_ref.shape[2]
    per = pair // footprint
    total = None
    for b in range(blocks):
        lhs = jnp.concatenate([proj_ref[b * per + h] for h in range(per)], axis=1)
        term = jnp.dot(lhs, tiles_ref[b], preferred_element_type=jnp.float32)
        total = term if total is None else total + term
    out_ref[...] = total


def owner_sums(proj, tiles):
    return pl.pallas_call(
        sums_kernel,
        out_shape=jax.ShapeDtypeStruct((proj.shape[1], tiles.shape[2]), jnp.float32),
        in_specs=[pl.BlockSpec(memory_space=pltpu.VMEM)] * 2,
        out_specs=pl.BlockSpec(memory_space=pltpu.VMEM),
    )(proj, tiles)


def per_device(ny, nz, proj, tiles, owner, lengths):
    view_count, group_rows, footprint = proj.shape
    samples = tiles.shape[2]
    group = lax.axis_index("chord")
    view_place = lax.axis_index("view")
    view_devices = ny * nz
    owned = group_rows // view_devices
    chunks_per_row = samples // LANES
    slots = min(chunks_per_row * owned, (PACK + owned * (LANES - 1)) // LANES)

    my_order = lax.dynamic_index_in_dim(owner, group, 0, keepdims=False)
    my_lengths = lax.dynamic_index_in_dim(lengths, group, 0, keepdims=False)
    order_len = pick(my_lengths[None, :], my_order[None, :])
    order_len = order_len.reshape(view_devices, owned)

    perm = (my_order[:, None] == jnp.arange(group_rows, dtype=jnp.int32)[None, :]).astype(proj.dtype)
    proj_ord = jnp.einsum("rk,vkd->vrd", perm, proj, preferred_element_type=jnp.float32)
    sums = owner_sums(proj_ord.astype(proj.dtype), tiles)
    blocks = sums.reshape(ny, nz, owned, chunks_per_row, LANES)

    counts = (order_len + LANES - 1) // LANES
    ends = jnp.cumsum(counts, axis=1)
    starts = ends - counts
    slot = jnp.arange(slots, dtype=jnp.int32)
    member = jnp.sum((ends[:, None, :] <= slot[None, :, None]).astype(jnp.int32), axis=2)
    member = jnp.minimum(member, owned - 1)
    first = pick(starts, member)
    within = jnp.clip(slot[None, :] - first, 0, chunks_per_row - 1)
    member = member.reshape(ny, nz, slots)
    within = within.reshape(ny, nz, slots)
    half = (slots + 1) // 2
    choose = (
        (member[..., None, None] == jnp.arange(owned, dtype=jnp.int32)[:, None])
        & (within[..., None, None] == jnp.arange(chunks_per_row, dtype=jnp.int32)[None, :])
    ).astype(jnp.float32)
    bf16 = jnp.bfloat16
    hi = lax.reduce_precision(blocks, exponent_bits=8, mantissa_bits=7)
    rest = blocks - hi
    mid = lax.reduce_precision(rest, exponent_bits=8, mantissa_bits=7)
    lo = rest - mid
    parts = jnp.stack([hi, mid, lo]).astype(bf16)
    choose = choose.astype(bf16)
    xa = jnp.einsum("yzbmc,pyzmcl->pzybl", choose[:, :, :half], parts,
                    preferred_element_type=jnp.float32).sum(axis=0)
    xb = jnp.einsum("yzbmc,pyzmcl->pyzbl", choose[:, :, half:], parts,
                    preferred_element_type=jnp.float32).sum(axis=0)

    mine = jnp.concatenate(reduce_scatter(xa, xb, ny, nz), axis=0)

    my_starts = lax.dynamic_index_in_dim(starts, view_place, 0, keepdims=False)
    my_len = lax.dynamic_index_in_dim(order_len, view_place, 0, keepdims=False)
    back = my_starts[:, None] + jnp.arange(chunks_per_row, dtype=jnp.int32)[None, :]
    back = jnp.minimum(back, slots - 1)
    rows = jnp.take(mine, back.reshape(-1), axis=0).reshape(owned, samples)

    table = kernel_table(samples, 0.0, samples)
    recon = invert_block(rows, my_len, table, 0.0)
    return recon[None]


def solution(mesh):
    view_devices = mesh.shape["view"]
    ny = int(round(math.sqrt(view_devices)))
    nz = view_devices // ny
    placed = (P("view", "chord", None), P("view", None, None), P(), P())
    return jax.shard_map(
        functools.partial(per_device, ny, nz),
        mesh=mesh,
        in_specs=placed,
        out_specs=P("chord", "view", None),
        check_vma=False,
    )
```

```python
import functools
import math

import jax
import jax.numpy as jnp
from jax import lax
from jax.experimental import pallas as pl
from jax.experimental.pallas import tpu as pltpu
from jax.sharding import PartitionSpec as P

LANES = 128
PACK = 4608
MESH = pl.DeviceIdType.MESH


def kernel_table(rows, start, cols):
    row_pos = start + jnp.arange(rows, dtype=jnp.float32)[:, None]
    col_pos = jnp.arange(cols, dtype=jnp.float32)[None, :]
    return 1.0 / (row_pos - col_pos + 0.5)


def weigh(length, count, start):
    position = start + jnp.arange(count, dtype=jnp.float32)[None, :] + 0.5
    inside = position < length
    return (inside, jnp.sqrt(jnp.where(inside, position * (length - position), 1.0)))


def invert_block(sums, length, table, start):
    length = length.astype(jnp.float32)[:, None]
    col_in, col_w = weigh(length, sums.shape[1], 0.0)
    row_in, row_w = weigh(length, table.shape[0], start)
    scaled = jnp.where(col_in, col_w * sums, 0.0)
    image = jnp.dot(
        scaled, table.T, precision=lax.Precision.HIGH, preferred_element_type=jnp.float32
    )
    return jnp.where(row_in, image / (math.pi * row_w), 0.0)


def pick(table, index):
    hit = index[:, :, None] == jnp.arange(table.shape[1], dtype=jnp.int32)
    return jnp.sum(jnp.where(hit, table[:, None, :], 0), axis=-1)


def run_rings(rings):
    chains = []
    for r in rings:
        n = r["n"]
        nr = n // 2
        nl = n - 1 - nr
        chains.append((r, 1, nr, r["right"], r["rr"], r["sr"], r["base"]))
        chains.append((r, -1, nl, r["left"], r["rl"], r["sl"], r["base"] + nr))
    pending = [None] * len(chains)
    for s in range(max(c[2] for c in chains)):
        for i, (r, go, steps, to, recv, send, base) in enumerate(chains):
            if s >= steps:
                continue
            n = r["n"]
            dest = lax.rem(r["me"] + go * (steps - s) + 2 * n, n)
            if s == 0:
                src = r["src"](dest)
            else:
                pending[i].wait()
                send[s] = recv[s - 1] + r["val"](dest)
                src = send.at[s]
            copy = pltpu.make_async_remote_copy(
                src_ref=src,
                dst_ref=recv.at[s],
                send_sem=r["ssem"].at[base + s],
                recv_sem=r["rsem"].at[base + s],
                device_id=to,
                device_id_type=MESH,
            )
            copy.start()
            pending[i] = copy
    for copy in pending:
        copy.wait()
    return [(r["rr"].at[r["n"] // 2 - 1], r["rl"].at[r["n"] - 2 - r["n"] // 2]) for r in rings]


def run_direct(rings):
    copies = []
    for r in rings:
        n = r["n"]
        for k in range(1, n):
            dest = lax.rem(r["me"] + k, n)
            copy = pltpu.make_async_remote_copy(
                src_ref=r["chunk"].at[dest],
                dst_ref=r["recv"].at[k - 1],
                send_sem=r["ssem"].at[r["base"] + k - 1],
                recv_sem=r["rsem"].at[r["base"] + k - 1],
                device_id=r["dev"](dest),
                device_id_type=MESH,
            )
            copy.start()
            copies.append(copy)
    for copy in copies:
        copy.wait()


def rs_kernel(ny, nz, xa, xb, oa, ob, s1a, s1b, *bufs):
    ssem, rsem = bufs[-2:]
    bufs = bufs[:-2]
    view = lax.axis_index("view")
    group = lax.axis_index("chord")
    y = view // nz
    z = lax.rem(view, nz)

    def dev(yy, zz):
        return (yy * nz + zz, group)

    z_right = dev(y, lax.rem(z + 1, nz))
    z_left = dev(y, lax.rem(z + nz - 1, nz))
    y_right = dev(lax.rem(y + 1, ny), z)
    y_left = dev(lax.rem(y + ny - 1, ny), z)

    barrier = pltpu.get_barrier_semaphore()
    for k in range(1, ny):
        pl.semaphore_signal(barrier, inc=1, device_id=dev(lax.rem(y + k, ny), z), device_id_type=MESH)
    for k in range(1, nz):
        pl.semaphore_signal(barrier, inc=1, device_id=dev(y, lax.rem(z + k, nz)), device_id_type=MESH)
    pl.semaphore_wait(barrier, ny + nz - 2)

    def ring(n, me, right, left, x, part, at, base):
        rr, rl, sr, sl = bufs[4 * at: 4 * at + 4]
        return dict(n=n, me=me, right=right, left=left, rr=rr, rl=rl, sr=sr, sl=sl,
                    src=lambda d: x.at[d, part], val=lambda d: x[d, part],
                    ssem=ssem, rsem=rsem, base=base)

    ha, hb = ny // 2, nz // 2
    lo_a, hi_a = pl.ds(0, ha), pl.ds(ha, ny - ha)
    lo_b, hi_b = pl.ds(0, hb), pl.ds(hb, nz - hb)
    fins = run_rings([
        ring(nz, z, z_right, z_left, xa, lo_a, 0, 0),
        ring(nz, z, z_right, z_left, xa, hi_a, 1, nz - 1),
        ring(ny, y, y_right, y_left, xb, lo_b, 2, 2 * (nz - 1)),
        ring(ny, y, y_right, y_left, xb, hi_b, 3, 2 * (nz - 1) + ny - 1),
    ])
    s1a[lo_a] = xa[z, lo_a] + fins[0][0][...] + fins[0][1][...]
    s1a[hi_a] = xa[z, hi_a] + fins[1][0][...] + fins[1][1][...]
    s1b[lo_b] = xb[y, lo_b] + fins[2][0][...] + fins[2][1][...]
    s1b[hi_b] = xb[y, hi_b] + fins[3][0][...] + fins[3][1][...]
    recv_a, recv_b = bufs[16], bufs[17]
    run_direct([
        dict(n=ny, me=y, dev=lambda d: dev(d, z), chunk=s1a, recv=recv_a,
             ssem=ssem, rsem=rsem, base=2 * (nz + ny - 2)),
        dict(n=nz, me=z, dev=lambda d: dev(y, d), chunk=s1b, recv=recv_b,
             ssem=ssem, rsem=rsem, base=2 * (nz + ny - 2) + ny - 1),
    ])
    oa[...] = s1a[y] + jnp.sum(recv_a[...], axis=0)
    ob[...] = s1b[z] + jnp.sum(recv_b[...], axis=0)


def reduce_scatter(xa, xb, ny, nz):
    ra, rb = xa.shape[2], xb.shape[2]
    f32 = jnp.float32

    def slots(n, shape):
        return [pltpu.VMEM((n // 2,) + shape, f32), pltpu.VMEM((n - 1 - n // 2,) + shape, f32)] * 2

    ha, hb = ny // 2, nz // 2
    bufs = (
        slots(nz, (ha, ra, LANES)) + slots(nz, (ny - ha, ra, LANES))
        + slots(ny, (hb, rb, LANES)) + slots(ny, (nz - hb, rb, LANES))
        + [pltpu.VMEM((ny - 1, ra, LANES), f32), pltpu.VMEM((nz - 1, rb, LANES), f32)]
    )
    return pl.pallas_call(
        functools.partial(rs_kernel, ny, nz),
        out_shape=(jax.ShapeDtypeStruct((ra, LANES), f32), jax.ShapeDtypeStruct((rb, LANES), f32)),
        in_specs=[pl.BlockSpec(memory_space=pltpu.VMEM)] * 2,
        out_specs=(pl.BlockSpec(memory_space=pltpu.VMEM),) * 2,
        scratch_shapes=[pltpu.VMEM((ny, ra, LANES), f32), pltpu.VMEM((nz, rb, LANES), f32)]
        + bufs
        + [pltpu.SemaphoreType.DMA((3 * (nz + ny - 2),)), pltpu.SemaphoreType.DMA((3 * (nz + ny - 2),))],
        compiler_params=pltpu.CompilerParams(collective_id=0, has_side_effects=True),
    )(xa, xb)


def sums_kernel(proj_ref, tiles_ref, out_ref):
    blocks, pair, samples = tiles_ref.shape
    footprint = proj_ref.shape[2]
    per = pair // footprint
    total = None
    for b in range(blocks):
        lhs = jnp.concatenate([proj_ref[b * per + h] for h in range(per)], axis=1)
        term = jnp.dot(lhs, tiles_ref[b], preferred_element_type=jnp.float32)
        total = term if total is None else total + term
    hi = total.astype(jnp.bfloat16)
    rest = total - hi.astype(jnp.float32)
    mid = rest.astype(jnp.bfloat16)
    out_ref[0] = hi
    out_ref[1] = mid
    out_ref[2] = (rest - mid.astype(jnp.float32)).astype(jnp.bfloat16)


def owner_sums(proj, tiles):
    return pl.pallas_call(
        sums_kernel,
        out_shape=jax.ShapeDtypeStruct((3, proj.shape[1], tiles.shape[2]), jnp.bfloat16),
        in_specs=[pl.BlockSpec(memory_space=pltpu.VMEM)] * 2,
        out_specs=pl.BlockSpec(memory_space=pltpu.VMEM),
    )(proj, tiles)


def per_device(ny, nz, proj, tiles, owner, lengths):
    view_count, group_rows, footprint = proj.shape
    samples = tiles.shape[2]
    group = lax.axis_index("chord")
    view_place = lax.axis_index("view")
    view_devices = ny * nz
    owned = group_rows // view_devices
    chunks_per_row = samples // LANES
    slots = min(chunks_per_row * owned, (PACK + owned * (LANES - 1)) // LANES)

    my_order = lax.dynamic_index_in_dim(owner, group, 0, keepdims=False)
    my_lengths = lax.dynamic_index_in_dim(lengths, group, 0, keepdims=False)
    order_len = pick(my_lengths[None, :], my_order[None, :])
    order_len = order_len.reshape(view_devices, owned)

    perm = (my_order[:, None] == jnp.arange(group_rows, dtype=jnp.int32)[None, :]).astype(proj.dtype)
    proj_ord = jnp.einsum("rk,vkd->vrd", perm, proj, preferred_element_type=jnp.float32)
    sums = owner_sums(proj_ord.astype(proj.dtype), tiles)
    parts = sums.reshape(3, ny, nz, owned, chunks_per_row, LANES)

    counts = (order_len + LANES - 1) // LANES
    ends = jnp.cumsum(counts, axis=1)
    starts = ends - counts
    slot = jnp.arange(slots, dtype=jnp.int32)
    member = jnp.sum((ends[:, None, :] <= slot[None, :, None]).astype(jnp.int32), axis=2)
    member = jnp.minimum(member, owned - 1)
    first = pick(starts, member)
    within = jnp.clip(slot[None, :] - first, 0, chunks_per_row - 1)
    member = member.reshape(ny, nz, slots)
    within = within.reshape(ny, nz, slots)
    half = (slots + 1) // 2
    choose = (
        (member[..., None, None] == jnp.arange(owned, dtype=jnp.int32)[:, None])
        & (within[..., None, None] == jnp.arange(chunks_per_row, dtype=jnp.int32)[None, :])
    ).astype(jnp.float32)
    choose = choose.astype(jnp.bfloat16)
    xa = jnp.einsum("yzbmc,pyzmcl->pzybl", choose[:, :, :half], parts,
                    preferred_element_type=jnp.float32).sum(axis=0)
    xb = jnp.einsum("yzbmc,pyzmcl->pyzbl", choose[:, :, half:], parts,
                    preferred_element_type=jnp.float32).sum(axis=0)

    mine = jnp.concatenate(reduce_scatter(xa, xb, ny, nz), axis=0)

    my_starts = lax.dynamic_index_in_dim(starts, view_place, 0, keepdims=False)
    my_len = lax.dynamic_index_in_dim(order_len, view_place, 0, keepdims=False)
    back = my_starts[:, None] + jnp.arange(chunks_per_row, dtype=jnp.int32)[None, :]
    back = jnp.minimum(back, slots - 1)
    rows = jnp.take(mine, back.reshape(-1), axis=0).reshape(owned, samples)

    table = kernel_table(samples, 0.0, samples)
    recon = invert_block(rows, my_len, table, 0.0)
    return recon[None]


def solution(mesh):
    view_devices = mesh.shape["view"]
    ny = int(round(math.sqrt(view_devices)))
    nz = view_devices // ny
    placed = (P("view", "chord", None), P("view", None, None), P(), P())
    return jax.shard_map(
        functools.partial(per_device, ny, nz),
        mesh=mesh,
        in_specs=placed,
        out_specs=P("chord", "view", None),
        check_vma=False,
    )
```

```python
import functools
import math

import jax
import jax.numpy as jnp
from jax import lax
from jax.experimental import pallas as pl
from jax.experimental.pallas import tpu as pltpu
from jax.sharding import PartitionSpec as P

LANES = 128
PACK = 4608
MESH = pl.DeviceIdType.MESH


def kernel_table(rows, start, cols):
    row_pos = start + jnp.arange(rows, dtype=jnp.float32)[:, None]
    col_pos = jnp.arange(cols, dtype=jnp.float32)[None, :]
    return 1.0 / (row_pos - col_pos + 0.5)


def weigh(length, count, start):
    position = start + jnp.arange(count, dtype=jnp.float32)[None, :] + 0.5
    inside = position < length
    return (inside, jnp.sqrt(jnp.where(inside, position * (length - position), 1.0)))


def invert_block(sums, length, table, start):
    length = length.astype(jnp.float32)[:, None]
    col_in, col_w = weigh(length, sums.shape[1], 0.0)
    row_in, row_w = weigh(length, table.shape[0], start)
    scaled = jnp.where(col_in, col_w * sums, 0.0)
    image = jnp.dot(
        scaled, table.T, precision=lax.Precision.HIGH, preferred_element_type=jnp.float32
    )
    return jnp.where(row_in, image / (math.pi * row_w), 0.0)


def pick(table, index):
    hit = index[:, :, None] == jnp.arange(table.shape[1], dtype=jnp.int32)
    return jnp.sum(jnp.where(hit, table[:, None, :], 0), axis=-1)


def run_rings(rings):
    chains = []
    for r in rings:
        n = r["n"]
        nr = n // 2
        nl = n - 1 - nr
        chains.append((r, 1, nr, r["right"], r["rr"], r["sr"], r["base"]))
        chains.append((r, -1, nl, r["left"], r["rl"], r["sl"], r["base"] + nr))
    pending = [None] * len(chains)
    for s in range(max(c[2] for c in chains)):
        for i, (r, go, steps, to, recv, send, base) in enumerate(chains):
            if s >= steps:
                continue
            n = r["n"]
            dest = lax.rem(r["me"] + go * (steps - s) + 2 * n, n)
            if s == 0:
                src = r["src"](dest)
            else:
                pending[i].wait()
                send[s] = recv[s - 1] + r["val"](dest)
                src = send.at[s]
            copy = pltpu.make_async_remote_copy(
                src_ref=src,
                dst_ref=recv.at[s],
                send_sem=r["ssem"].at[base + s],
                recv_sem=r["rsem"].at[base + s],
                device_id=to,
                device_id_type=MESH,
            )
            copy.start()
            pending[i] = copy
    for copy in pending:
        copy.wait()
    return [(r["rr"].at[r["n"] // 2 - 1], r["rl"].at[r["n"] - 2 - r["n"] // 2]) for r in rings]


def run_direct(rings):
    copies = []
    for r in rings:
        n = r["n"]
        for k in range(1, n):
            dest = lax.rem(r["me"] + k, n)
            copy = pltpu.make_async_remote_copy(
                src_ref=r["chunk"].at[dest],
                dst_ref=r["recv"].at[k - 1],
                send_sem=r["ssem"].at[r["base"] + k - 1],
                recv_sem=r["rsem"].at[r["base"] + k - 1],
                device_id=r["dev"](dest),
                device_id_type=MESH,
            )
            copy.start()
            copies.append(copy)
    for copy in copies:
        copy.wait()


def rs_kernel(ny, nz, xa, xb, oa, ob, s1a, s1b, *bufs):
    ssem, rsem = bufs[-2:]
    bufs = bufs[:-2]
    view = lax.axis_index("view")
    group = lax.axis_index("chord")
    y = view // nz
    z = lax.rem(view, nz)

    def dev(yy, zz):
        return (yy * nz + zz, group)

    z_right = dev(y, lax.rem(z + 1, nz))
    z_left = dev(y, lax.rem(z + nz - 1, nz))
    y_right = dev(lax.rem(y + 1, ny), z)
    y_left = dev(lax.rem(y + ny - 1, ny), z)

    barrier = pltpu.get_barrier_semaphore()
    for k in range(1, ny):
        pl.semaphore_signal(barrier, inc=1, device_id=dev(lax.rem(y + k, ny), z), device_id_type=MESH)
    for k in range(1, nz):
        pl.semaphore_signal(barrier, inc=1, device_id=dev(y, lax.rem(z + k, nz)), device_id_type=MESH)
    pl.semaphore_wait(barrier, ny + nz - 2)

    def ring(n, me, right, left, x, part, at, base, swap=False):
        rr, rl, sr, sl = bufs[4 * at: 4 * at + 4]
        if swap:
            src, val = (lambda d: x.at[part, d]), (lambda d: x[part, d])
        else:
            src, val = (lambda d: x.at[d, part]), (lambda d: x[d, part])
        return dict(n=n, me=me, right=right, left=left, rr=rr, rl=rl, sr=sr, sl=sl,
                    src=src, val=val, ssem=ssem, rsem=rsem, base=base)

    ha, hb = ny // 2, nz // 2
    lo_a, hi_a = pl.ds(0, ha), pl.ds(ha, ny - ha)
    lo_b, hi_b = pl.ds(0, hb), pl.ds(hb, nz - hb)
    fins = run_rings([
        ring(nz, z, z_right, z_left, xa, lo_a, 0, 0, swap=True),
        ring(nz, z, z_right, z_left, xa, hi_a, 1, nz - 1, swap=True),
        ring(ny, y, y_right, y_left, xb, lo_b, 2, 2 * (nz - 1)),
        ring(ny, y, y_right, y_left, xb, hi_b, 3, 2 * (nz - 1) + ny - 1),
    ])
    s1a[lo_a] = xa[lo_a, z] + fins[0][0][...] + fins[0][1][...]
    s1a[hi_a] = xa[hi_a, z] + fins[1][0][...] + fins[1][1][...]
    s1b[lo_b] = xb[y, lo_b] + fins[2][0][...] + fins[2][1][...]
    s1b[hi_b] = xb[y, hi_b] + fins[3][0][...] + fins[3][1][...]
    recv_a, recv_b = bufs[16], bufs[17]
    run_direct([
        dict(n=ny, me=y, dev=lambda d: dev(d, z), chunk=s1a, recv=recv_a,
             ssem=ssem, rsem=rsem, base=2 * (nz + ny - 2)),
        dict(n=nz, me=z, dev=lambda d: dev(y, d), chunk=s1b, recv=recv_b,
             ssem=ssem, rsem=rsem, base=2 * (nz + ny - 2) + ny - 1),
    ])
    oa[...] = s1a[y] + jnp.sum(recv_a[...], axis=0)
    ob[...] = s1b[z] + jnp.sum(recv_b[...], axis=0)


def reduce_scatter(xa, xb, ny, nz):
    ra, rb = xa.shape[2], xb.shape[2]
    f32 = jnp.float32

    def slots(n, shape):
        return [pltpu.VMEM((n // 2,) + shape, f32), pltpu.VMEM((n - 1 - n // 2,) + shape, f32)] * 2

    ha, hb = ny // 2, nz // 2
    bufs = (
        slots(nz, (ha, ra, LANES)) + slots(nz, (ny - ha, ra, LANES))
        + slots(ny, (hb, rb, LANES)) + slots(ny, (nz - hb, rb, LANES))
        + [pltpu.VMEM((ny - 1, ra, LANES), f32), pltpu.VMEM((nz - 1, rb, LANES), f32)]
    )
    return pl.pallas_call(
        functools.partial(rs_kernel, ny, nz),
        out_shape=(jax.ShapeDtypeStruct((ra, LANES), f32), jax.ShapeDtypeStruct((rb, LANES), f32)),
        in_specs=[pl.BlockSpec(memory_space=pltpu.VMEM)] * 2,
        out_specs=(pl.BlockSpec(memory_space=pltpu.VMEM),) * 2,
        scratch_shapes=[pltpu.VMEM((ny, ra, LANES), f32), pltpu.VMEM((nz, rb, LANES), f32)]
        + bufs
        + [pltpu.SemaphoreType.DMA((3 * (nz + ny - 2),)), pltpu.SemaphoreType.DMA((3 * (nz + ny - 2),))],
        compiler_params=pltpu.CompilerParams(collective_id=0, has_side_effects=True),
    )(xa, xb)


def sums_kernel(proj_ref, tiles_ref, out_ref):
    blocks, pair, samples = tiles_ref.shape
    footprint = proj_ref.shape[2]
    per = pair // footprint
    total = None
    for b in range(blocks):
        lhs = jnp.concatenate([proj_ref[b * per + h] for h in range(per)], axis=1)
        term = jnp.dot(lhs, tiles_ref[b], preferred_element_type=jnp.float32)
        total = term if total is None else total + term
    hi = total.astype(jnp.bfloat16)
    rest = total - hi.astype(jnp.float32)
    mid = rest.astype(jnp.bfloat16)
    out_ref[0] = hi
    out_ref[1] = mid
    out_ref[2] = (rest - mid.astype(jnp.float32)).astype(jnp.bfloat16)


def owner_sums(proj, tiles):
    return pl.pallas_call(
        sums_kernel,
        out_shape=jax.ShapeDtypeStruct((3, proj.shape[1], tiles.shape[2]), jnp.bfloat16),
        in_specs=[pl.BlockSpec(memory_space=pltpu.VMEM)] * 2,
        out_specs=pl.BlockSpec(memory_space=pltpu.VMEM),
    )(proj, tiles)


def per_device(ny, nz, proj, tiles, owner, lengths):
    view_count, group_rows, footprint = proj.shape
    samples = tiles.shape[2]
    group = lax.axis_index("chord")
    view_place = lax.axis_index("view")
    view_devices = ny * nz
    owned = group_rows // view_devices
    chunks_per_row = samples // LANES
    slots = min(chunks_per_row * owned, (PACK + owned * (LANES - 1)) // LANES)

    my_order = lax.dynamic_index_in_dim(owner, group, 0, keepdims=False)
    my_lengths = lax.dynamic_index_in_dim(lengths, group, 0, keepdims=False)
    order_len = pick(my_lengths[None, :], my_order[None, :])
    order_len = order_len.reshape(view_devices, owned)

    perm = (my_order[:, None] == jnp.arange(group_rows, dtype=jnp.int32)[None, :]).astype(proj.dtype)
    proj_ord = jnp.einsum("rk,vkd->vrd", perm, proj, preferred_element_type=jnp.float32)
    sums = owner_sums(proj_ord.astype(proj.dtype), tiles)
    parts = sums.reshape(3, ny, nz, owned, chunks_per_row, LANES)

    counts = (order_len + LANES - 1) // LANES
    ends = jnp.cumsum(counts, axis=1)
    starts = ends - counts
    slot = jnp.arange(slots, dtype=jnp.int32)
    member = jnp.sum((ends[:, None, :] <= slot[None, :, None]).astype(jnp.int32), axis=2)
    member = jnp.minimum(member, owned - 1)
    first = pick(starts, member)
    within = jnp.clip(slot[None, :] - first, 0, chunks_per_row - 1)
    member = member.reshape(ny, nz, slots)
    within = within.reshape(ny, nz, slots)
    half = (slots + 1) // 2
    choose = (
        (member[..., None, None] == jnp.arange(owned, dtype=jnp.int32)[:, None])
        & (within[..., None, None] == jnp.arange(chunks_per_row, dtype=jnp.int32)[None, :])
    ).astype(jnp.float32)
    choose = choose.astype(jnp.bfloat16)
    xa = jnp.einsum("yzbmc,pyzmcl->pyzbl", choose[:, :, :half], parts,
                    preferred_element_type=jnp.float32).sum(axis=0)
    xb = jnp.einsum("yzbmc,pyzmcl->pyzbl", choose[:, :, half:], parts,
                    preferred_element_type=jnp.float32).sum(axis=0)

    mine = jnp.concatenate(reduce_scatter(xa, xb, ny, nz), axis=0)

    my_starts = lax.dynamic_index_in_dim(starts, view_place, 0, keepdims=False)
    my_len = lax.dynamic_index_in_dim(order_len, view_place, 0, keepdims=False)
    back = my_starts[:, None] + jnp.arange(chunks_per_row, dtype=jnp.int32)[None, :]
    back = jnp.minimum(back, slots - 1)
    rows = jnp.take(mine, back.reshape(-1), axis=0).reshape(owned, samples)

    table = kernel_table(samples, 0.0, samples)
    recon = invert_block(rows, my_len, table, 0.0)
    return recon[None]


def solution(mesh):
    view_devices = mesh.shape["view"]
    ny = int(round(math.sqrt(view_devices)))
    nz = view_devices // ny
    placed = (P("view", "chord", None), P("view", None, None), P(), P())
    return jax.shard_map(
        functools.partial(per_device, ny, nz),
        mesh=mesh,
        in_specs=placed,
        out_specs=P("chord", "view", None),
        check_vma=False,
    )
```

```python
import functools
import math

import jax
import jax.numpy as jnp
from jax import lax
from jax.experimental import pallas as pl
from jax.experimental.pallas import tpu as pltpu
from jax.sharding import PartitionSpec as P

LANES = 128
PACK = 4608
MESH = pl.DeviceIdType.MESH


def kernel_table(rows, start, cols):
    row_pos = start + jnp.arange(rows, dtype=jnp.float32)[:, None]
    col_pos = jnp.arange(cols, dtype=jnp.float32)[None, :]
    return 1.0 / (row_pos - col_pos + 0.5)


def weigh(length, count, start):
    position = start + jnp.arange(count, dtype=jnp.float32)[None, :] + 0.5
    inside = position < length
    return (inside, jnp.sqrt(jnp.where(inside, position * (length - position), 1.0)))


def invert_block(sums, length, table, start):
    length = length.astype(jnp.float32)[:, None]
    col_in, col_w = weigh(length, sums.shape[1], 0.0)
    row_in, row_w = weigh(length, table.shape[0], start)
    scaled = jnp.where(col_in, col_w * sums, 0.0)
    image = jnp.dot(
        scaled, table.T, precision=lax.Precision.HIGH, preferred_element_type=jnp.float32
    )
    return jnp.where(row_in, image / (math.pi * row_w), 0.0)


def pick(table, index):
    hit = index[:, :, None] == jnp.arange(table.shape[1], dtype=jnp.int32)
    return jnp.sum(jnp.where(hit, table[:, None, :], 0), axis=-1)


def run_rings(rings):
    chains = []
    for r in rings:
        n = r["n"]
        nr = n // 2
        nl = n - 1 - nr
        chains.append((r, 1, nr, r["right"], r["rr"], r["sr"], r["base"]))
        chains.append((r, -1, nl, r["left"], r["rl"], r["sl"], r["base"] + nr))
    pending = [None] * len(chains)
    for s in range(max(c[2] for c in chains)):
        for i, (r, go, steps, to, recv, send, base) in enumerate(chains):
            if s >= steps:
                continue
            n = r["n"]
            dest = lax.rem(r["me"] + go * (steps - s) + 2 * n, n)
            if s == 0:
                src = r["src"](dest)
            else:
                pending[i].wait()
                send[s] = recv[s - 1] + r["val"](dest)
                src = send.at[s]
            copy = pltpu.make_async_remote_copy(
                src_ref=src,
                dst_ref=recv.at[s],
                send_sem=r["ssem"].at[base + s],
                recv_sem=r["rsem"].at[base + s],
                device_id=to,
                device_id_type=MESH,
            )
            copy.start()
            pending[i] = copy
    for copy in pending:
        copy.wait()
    return [(r["rr"].at[r["n"] // 2 - 1], r["rl"].at[r["n"] - 2 - r["n"] // 2]) for r in rings]


def run_direct(rings):
    copies = []
    for r in rings:
        n = r["n"]
        for k in range(1, n):
            dest = lax.rem(r["me"] + k, n)
            copy = pltpu.make_async_remote_copy(
                src_ref=r["chunk"].at[dest],
                dst_ref=r["recv"].at[k - 1],
                send_sem=r["ssem"].at[r["base"] + k - 1],
                recv_sem=r["rsem"].at[r["base"] + k - 1],
                device_id=r["dev"](dest),
                device_id_type=MESH,
            )
            copy.start()
            copies.append(copy)
    for copy in copies:
        copy.wait()


def rs_kernel(ny, nz, xa, xb, oa, ob, s1a, s1b, *bufs):
    ssem, rsem = bufs[-2:]
    bufs = bufs[:-2]
    view = lax.axis_index("view")
    group = lax.axis_index("chord")
    y = view // nz
    z = lax.rem(view, nz)

    def dev(yy, zz):
        return (yy * nz + zz, group)

    z_right = dev(y, lax.rem(z + 1, nz))
    z_left = dev(y, lax.rem(z + nz - 1, nz))
    y_right = dev(lax.rem(y + 1, ny), z)
    y_left = dev(lax.rem(y + ny - 1, ny), z)

    barrier = pltpu.get_barrier_semaphore()
    for k in range(1, ny):
        pl.semaphore_signal(barrier, inc=1, device_id=dev(lax.rem(y + k, ny), z), device_id_type=MESH)
    for k in range(1, nz):
        pl.semaphore_signal(barrier, inc=1, device_id=dev(y, lax.rem(z + k, nz)), device_id_type=MESH)
    pl.semaphore_wait(barrier, ny + nz - 2)

    def ring(n, me, right, left, x, part, at, base, swap=False):
        rr, rl, sr, sl = bufs[4 * at: 4 * at + 4]
        if swap:
            src, val = (lambda d: x.at[part, d]), (lambda d: x[part, d])
        else:
            src, val = (lambda d: x.at[d, part]), (lambda d: x[d, part])
        return dict(n=n, me=me, right=right, left=left, rr=rr, rl=rl, sr=sr, sl=sl,
                    src=src, val=val, ssem=ssem, rsem=rsem, base=base)

    ha, hb = ny // 2, nz // 2
    lo_a, hi_a = pl.ds(0, ha), pl.ds(ha, ny - ha)
    lo_b, hi_b = pl.ds(0, hb), pl.ds(hb, nz - hb)
    fins = run_rings([
        ring(nz, z, z_right, z_left, xa, lo_a, 0, 0, swap=True),
        ring(nz, z, z_right, z_left, xa, hi_a, 1, nz - 1, swap=True),
        ring(ny, y, y_right, y_left, xb, lo_b, 2, 2 * (nz - 1)),
        ring(ny, y, y_right, y_left, xb, hi_b, 3, 2 * (nz - 1) + ny - 1),
    ])
    s1a[lo_a] = xa[lo_a, z] + fins[0][0][...] + fins[0][1][...]
    s1a[hi_a] = xa[hi_a, z] + fins[1][0][...] + fins[1][1][...]
    s1b[lo_b] = xb[y, lo_b] + fins[2][0][...] + fins[2][1][...]
    s1b[hi_b] = xb[y, hi_b] + fins[3][0][...] + fins[3][1][...]
    recv_a, recv_b = bufs[16], bufs[17]
    run_direct([
        dict(n=ny, me=y, dev=lambda d: dev(d, z), chunk=s1a, recv=recv_a,
             ssem=ssem, rsem=rsem, base=2 * (nz + ny - 2)),
        dict(n=nz, me=z, dev=lambda d: dev(y, d), chunk=s1b, recv=recv_b,
             ssem=ssem, rsem=rsem, base=2 * (nz + ny - 2) + ny - 1),
    ])
    oa[...] = s1a[y] + jnp.sum(recv_a[...], axis=0)
    ob[...] = s1b[z] + jnp.sum(recv_b[...], axis=0)


def reduce_scatter(xa, xb, ny, nz):
    ra, rb = xa.shape[2], xb.shape[2]
    f32 = jnp.float32

    def slots(n, shape):
        return [pltpu.VMEM((n // 2,) + shape, f32), pltpu.VMEM((n - 1 - n // 2,) + shape, f32)] * 2

    ha, hb = ny // 2, nz // 2
    bufs = (
        slots(nz, (ha, ra, LANES)) + slots(nz, (ny - ha, ra, LANES))
        + slots(ny, (hb, rb, LANES)) + slots(ny, (nz - hb, rb, LANES))
        + [pltpu.VMEM((ny - 1, ra, LANES), f32), pltpu.VMEM((nz - 1, rb, LANES), f32)]
    )
    return pl.pallas_call(
        functools.partial(rs_kernel, ny, nz),
        out_shape=(jax.ShapeDtypeStruct((ra, LANES), f32), jax.ShapeDtypeStruct((rb, LANES), f32)),
        in_specs=[pl.BlockSpec(memory_space=pltpu.VMEM)] * 2,
        out_specs=(pl.BlockSpec(memory_space=pltpu.VMEM),) * 2,
        scratch_shapes=[pltpu.VMEM((ny, ra, LANES), f32), pltpu.VMEM((nz, rb, LANES), f32)]
        + bufs
        + [pltpu.SemaphoreType.DMA((3 * (nz + ny - 2),)), pltpu.SemaphoreType.DMA((3 * (nz + ny - 2),))],
        compiler_params=pltpu.CompilerParams(collective_id=0, has_side_effects=True),
    )(xa, xb)


def sums_kernel(proj_ref, tiles_ref, out_ref):
    views = proj_ref.shape[0]
    samples = tiles_ref.shape[1]
    lhs = jnp.concatenate([proj_ref[v] for v in range(views)], axis=1)
    width = min(samples, 256)
    for cb in range(samples // width):
        cols = pl.ds(cb * width, width)
        total = jnp.dot(lhs, tiles_ref[:, cols], preferred_element_type=jnp.float32)
        hi = total.astype(jnp.bfloat16)
        rest = total - hi.astype(jnp.float32)
        mid = rest.astype(jnp.bfloat16)
        out_ref[0, :, cols] = hi
        out_ref[1, :, cols] = mid
        out_ref[2, :, cols] = (rest - mid.astype(jnp.float32)).astype(jnp.bfloat16)


def owner_sums(proj, tiles):
    tiles = tiles.reshape(-1, tiles.shape[2])
    return pl.pallas_call(
        sums_kernel,
        out_shape=jax.ShapeDtypeStruct((3, proj.shape[1], tiles.shape[1]), jnp.bfloat16),
        in_specs=[pl.BlockSpec(memory_space=pltpu.VMEM)] * 2,
        out_specs=pl.BlockSpec(memory_space=pltpu.VMEM),
    )(proj, tiles)


def per_device(ny, nz, proj, tiles, owner, lengths):
    view_count, group_rows, footprint = proj.shape
    samples = tiles.shape[2]
    group = lax.axis_index("chord")
    view_place = lax.axis_index("view")
    view_devices = ny * nz
    owned = group_rows // view_devices
    chunks_per_row = samples // LANES
    slots = min(chunks_per_row * owned, (PACK + owned * (LANES - 1)) // LANES)

    my_order = lax.dynamic_index_in_dim(owner, group, 0, keepdims=False)
    my_lengths = lax.dynamic_index_in_dim(lengths, group, 0, keepdims=False)
    order_len = pick(my_lengths[None, :], my_order[None, :])
    order_len = order_len.reshape(view_devices, owned)

    perm = (my_order[:, None] == jnp.arange(group_rows, dtype=jnp.int32)[None, :]).astype(proj.dtype)
    proj_ord = jnp.einsum("rk,vkd->vrd", perm, proj, preferred_element_type=jnp.float32)
    sums = owner_sums(proj_ord.astype(proj.dtype), tiles)
    parts = sums.reshape(3, ny, nz, owned, chunks_per_row, LANES)

    counts = (order_len + LANES - 1) // LANES
    ends = jnp.cumsum(counts, axis=1)
    starts = ends - counts
    slot = jnp.arange(slots, dtype=jnp.int32)
    member = jnp.sum((ends[:, None, :] <= slot[None, :, None]).astype(jnp.int32), axis=2)
    member = jnp.minimum(member, owned - 1)
    first = pick(starts, member)
    within = jnp.clip(slot[None, :] - first, 0, chunks_per_row - 1)
    member = member.reshape(ny, nz, slots)
    within = within.reshape(ny, nz, slots)
    half = (slots + 1) // 2
    choose = (
        (member[..., None, None] == jnp.arange(owned, dtype=jnp.int32)[:, None])
        & (within[..., None, None] == jnp.arange(chunks_per_row, dtype=jnp.int32)[None, :])
    ).astype(jnp.float32)
    choose = choose.astype(jnp.bfloat16)
    xa = jnp.einsum("yzbmc,pyzmcl->pyzbl", choose[:, :, :half], parts,
                    preferred_element_type=jnp.float32).sum(axis=0)
    xb = jnp.einsum("yzbmc,pyzmcl->pyzbl", choose[:, :, half:], parts,
                    preferred_element_type=jnp.float32).sum(axis=0)

    mine = jnp.concatenate(reduce_scatter(xa, xb, ny, nz), axis=0)

    my_starts = lax.dynamic_index_in_dim(starts, view_place, 0, keepdims=False)
    my_len = lax.dynamic_index_in_dim(order_len, view_place, 0, keepdims=False)
    back = my_starts[:, None] + jnp.arange(chunks_per_row, dtype=jnp.int32)[None, :]
    back = jnp.minimum(back, slots - 1)
    rows = jnp.take(mine, back.reshape(-1), axis=0).reshape(owned, samples)

    table = kernel_table(samples, 0.0, samples)
    recon = invert_block(rows, my_len, table, 0.0)
    return recon[None]


def solution(mesh):
    view_devices = mesh.shape["view"]
    ny = int(round(math.sqrt(view_devices)))
    nz = view_devices // ny
    placed = (P("view", "chord", None), P("view", None, None), P(), P())
    return jax.shard_map(
        functools.partial(per_device, ny, nz),
        mesh=mesh,
        in_specs=placed,
        out_specs=P("chord", "view", None),
        check_vma=False,
    )
```

```python
import functools
import math

import jax
import jax.numpy as jnp
from jax import lax
from jax.experimental import pallas as pl
from jax.experimental.pallas import tpu as pltpu
from jax.sharding import PartitionSpec as P

LANES = 128
PACK = 4608
MESH = pl.DeviceIdType.MESH


def kernel_table(rows, start, cols):
    row_pos = start + jnp.arange(rows, dtype=jnp.float32)[:, None]
    col_pos = jnp.arange(cols, dtype=jnp.float32)[None, :]
    return 1.0 / (row_pos - col_pos + 0.5)


def weigh(length, count, start):
    position = start + jnp.arange(count, dtype=jnp.float32)[None, :] + 0.5
    inside = position < length
    return (inside, jnp.sqrt(jnp.where(inside, position * (length - position), 1.0)))


def invert_block(sums, length, table, start):
    length = length.astype(jnp.float32)[:, None]
    col_in, col_w = weigh(length, sums.shape[1], 0.0)
    row_in, row_w = weigh(length, table.shape[0], start)
    scaled = jnp.where(col_in, col_w * sums, 0.0)
    image = jnp.dot(
        scaled, table.T, precision=lax.Precision.HIGH, preferred_element_type=jnp.float32
    )
    return jnp.where(row_in, image / (math.pi * row_w), 0.0)


def pick(table, index):
    hit = index[:, :, None] == jnp.arange(table.shape[1], dtype=jnp.int32)
    return jnp.sum(jnp.where(hit, table[:, None, :], 0), axis=-1)


def run_rings(rings):
    chains = []
    for r in rings:
        n = r["n"]
        nr = n // 2
        nl = n - 1 - nr
        chains.append((r, 1, nr, r["right"], r["rr"], r["sr"], r["base"]))
        chains.append((r, -1, nl, r["left"], r["rl"], r["sl"], r["base"] + nr))
    pending = [None] * len(chains)
    for s in range(max(c[2] for c in chains)):
        for i, (r, go, steps, to, recv, send, base) in enumerate(chains):
            if s >= steps:
                continue
            n = r["n"]
            dest = lax.rem(r["me"] + go * (steps - s) + 2 * n, n)
            if s == 0:
                src = r["src"](dest)
            else:
                pending[i].wait()
                send[s] = recv[s - 1] + r["val"](dest)
                src = send.at[s]
            copy = pltpu.make_async_remote_copy(
                src_ref=src,
                dst_ref=recv.at[s],
                send_sem=r["ssem"].at[base + s],
                recv_sem=r["rsem"].at[base + s],
                device_id=to,
                device_id_type=MESH,
            )
            copy.start()
            pending[i] = copy
    for copy in pending:
        copy.wait()
    return [(r["rr"].at[r["n"] // 2 - 1], r["rl"].at[r["n"] - 2 - r["n"] // 2]) for r in rings]


def run_direct(rings):
    copies = []
    for r in rings:
        n = r["n"]
        for k in range(1, n):
            dest = lax.rem(r["me"] + k, n)
            copy = pltpu.make_async_remote_copy(
                src_ref=r["chunk"].at[dest],
                dst_ref=r["recv"].at[k - 1],
                send_sem=r["ssem"].at[r["base"] + k - 1],
                recv_sem=r["rsem"].at[r["base"] + k - 1],
                device_id=r["dev"](dest),
                device_id_type=MESH,
            )
            copy.start()
            copies.append(copy)
    for copy in copies:
        copy.wait()


def rs_kernel(ny, nz, xa, xb, out, s1a, s1b, *bufs):
    ssem, rsem = bufs[-2:]
    bufs = bufs[:-2]
    view = lax.axis_index("view")
    group = lax.axis_index("chord")
    y = view // nz
    z = lax.rem(view, nz)

    def dev(yy, zz):
        return (yy * nz + zz, group)

    z_right = dev(y, lax.rem(z + 1, nz))
    z_left = dev(y, lax.rem(z + nz - 1, nz))
    y_right = dev(lax.rem(y + 1, ny), z)
    y_left = dev(lax.rem(y + ny - 1, ny), z)

    barrier = pltpu.get_barrier_semaphore()
    for k in range(1, ny):
        pl.semaphore_signal(barrier, inc=1, device_id=dev(lax.rem(y + k, ny), z), device_id_type=MESH)
    for k in range(1, nz):
        pl.semaphore_signal(barrier, inc=1, device_id=dev(y, lax.rem(z + k, nz)), device_id_type=MESH)
    pl.semaphore_wait(barrier, ny + nz - 2)

    def ring(n, me, right, left, x, part, at, base, swap=False):
        rr, rl, sr, sl = bufs[4 * at: 4 * at + 4]
        if swap:
            src, val = (lambda d: x.at[part, d]), (lambda d: x[part, d])
        else:
            src, val = (lambda d: x.at[d, part]), (lambda d: x[d, part])
        return dict(n=n, me=me, right=right, left=left, rr=rr, rl=rl, sr=sr, sl=sl,
                    src=src, val=val, ssem=ssem, rsem=rsem, base=base)

    ha, hb = ny // 2, nz // 2
    lo_a, hi_a = pl.ds(0, ha), pl.ds(ha, ny - ha)
    lo_b, hi_b = pl.ds(0, hb), pl.ds(hb, nz - hb)
    fins = run_rings([
        ring(nz, z, z_right, z_left, xa, lo_a, 0, 0, swap=True),
        ring(nz, z, z_right, z_left, xa, hi_a, 1, nz - 1, swap=True),
        ring(ny, y, y_right, y_left, xb, lo_b, 2, 2 * (nz - 1)),
        ring(ny, y, y_right, y_left, xb, hi_b, 3, 2 * (nz - 1) + ny - 1),
    ])
    s1a[lo_a] = xa[lo_a, z] + fins[0][0][...] + fins[0][1][...]
    s1a[hi_a] = xa[hi_a, z] + fins[1][0][...] + fins[1][1][...]
    s1b[lo_b] = xb[y, lo_b] + fins[2][0][...] + fins[2][1][...]
    s1b[hi_b] = xb[y, hi_b] + fins[3][0][...] + fins[3][1][...]
    recv_a, recv_b = bufs[16], bufs[17]
    run_direct([
        dict(n=ny, me=y, dev=lambda d: dev(d, z), chunk=s1a, recv=recv_a,
             ssem=ssem, rsem=rsem, base=2 * (nz + ny - 2)),
        dict(n=nz, me=z, dev=lambda d: dev(y, d), chunk=s1b, recv=recv_b,
             ssem=ssem, rsem=rsem, base=2 * (nz + ny - 2) + ny - 1),
    ])
    ra = xa.shape[2]
    out[pl.ds(0, ra), :] = s1a[y] + jnp.sum(recv_a[...], axis=0)
    out[pl.ds(ra, xb.shape[2]), :] = s1b[z] + jnp.sum(recv_b[...], axis=0)


def reduce_scatter(xa, xb, ny, nz):
    ra, rb = xa.shape[2], xb.shape[2]
    f32 = jnp.float32

    def slots(n, shape):
        return [pltpu.VMEM((n // 2,) + shape, f32), pltpu.VMEM((n - 1 - n // 2,) + shape, f32)] * 2

    ha, hb = ny // 2, nz // 2
    bufs = (
        slots(nz, (ha, ra, LANES)) + slots(nz, (ny - ha, ra, LANES))
        + slots(ny, (hb, rb, LANES)) + slots(ny, (nz - hb, rb, LANES))
        + [pltpu.VMEM((ny - 1, ra, LANES), f32), pltpu.VMEM((nz - 1, rb, LANES), f32)]
    )
    return pl.pallas_call(
        functools.partial(rs_kernel, ny, nz),
        out_shape=jax.ShapeDtypeStruct((ra + rb, LANES), f32),
        in_specs=[pl.BlockSpec(memory_space=pltpu.VMEM)] * 2,
        out_specs=pl.BlockSpec(memory_space=pltpu.VMEM),
        scratch_shapes=[pltpu.VMEM((ny, ra, LANES), f32), pltpu.VMEM((nz, rb, LANES), f32)]
        + bufs
        + [pltpu.SemaphoreType.DMA((3 * (nz + ny - 2),)), pltpu.SemaphoreType.DMA((3 * (nz + ny - 2),))],
        compiler_params=pltpu.CompilerParams(collective_id=0, has_side_effects=True),
    )(xa, xb)


def sums_kernel(proj_ref, tiles_ref, out_ref):
    views = proj_ref.shape[0]
    samples = tiles_ref.shape[1]
    lhs = jnp.concatenate([proj_ref[v] for v in range(views)], axis=1)
    width = min(samples, 256)
    for cb in range(samples // width):
        cols = pl.ds(cb * width, width)
        total = jnp.dot(lhs, tiles_ref[:, cols], preferred_element_type=jnp.float32)
        hi = total.astype(jnp.bfloat16)
        rest = total - hi.astype(jnp.float32)
        mid = rest.astype(jnp.bfloat16)
        out_ref[0, :, cols] = hi
        out_ref[1, :, cols] = mid
        out_ref[2, :, cols] = (rest - mid.astype(jnp.float32)).astype(jnp.bfloat16)


def owner_sums(proj, tiles):
    tiles = tiles.reshape(-1, tiles.shape[2])
    return pl.pallas_call(
        sums_kernel,
        out_shape=jax.ShapeDtypeStruct((3, proj.shape[1], tiles.shape[1]), jnp.bfloat16),
        in_specs=[pl.BlockSpec(memory_space=pltpu.VMEM)] * 2,
        out_specs=pl.BlockSpec(memory_space=pltpu.VMEM),
    )(proj, tiles)


def per_device(ny, nz, proj, tiles, owner, lengths):
    view_count, group_rows, footprint = proj.shape
    samples = tiles.shape[2]
    group = lax.axis_index("chord")
    view_place = lax.axis_index("view")
    view_devices = ny * nz
    owned = group_rows // view_devices
    chunks_per_row = samples // LANES
    slots = min(chunks_per_row * owned, (PACK + owned * (LANES - 1)) // LANES)

    my_order = lax.dynamic_index_in_dim(owner, group, 0, keepdims=False)
    my_lengths = lax.dynamic_index_in_dim(lengths, group, 0, keepdims=False)
    order_len = pick(my_lengths[None, :], my_order[None, :])
    order_len = order_len.reshape(view_devices, owned)

    perm = (my_order[:, None] == jnp.arange(group_rows, dtype=jnp.int32)[None, :]).astype(proj.dtype)
    proj_ord = jnp.einsum("rk,vkd->vrd", perm, proj, preferred_element_type=jnp.float32)
    sums = owner_sums(proj_ord.astype(proj.dtype), tiles)
    parts = sums.reshape(3, ny, nz, owned, chunks_per_row, LANES)

    counts = (order_len + LANES - 1) // LANES
    ends = jnp.cumsum(counts, axis=1)
    starts = ends - counts
    slot = jnp.arange(slots, dtype=jnp.int32)
    member = jnp.sum((ends[:, None, :] <= slot[None, :, None]).astype(jnp.int32), axis=2)
    member = jnp.minimum(member, owned - 1)
    first = pick(starts, member)
    within = jnp.clip(slot[None, :] - first, 0, chunks_per_row - 1)
    member = member.reshape(ny, nz, slots)
    within = within.reshape(ny, nz, slots)
    half = (slots + 1) // 2
    choose = (
        (member[..., None, None] == jnp.arange(owned, dtype=jnp.int32)[:, None])
        & (within[..., None, None] == jnp.arange(chunks_per_row, dtype=jnp.int32)[None, :])
    ).astype(jnp.float32)
    choose = choose.astype(jnp.bfloat16)
    xa = jnp.einsum("yzbmc,pyzmcl->pyzbl", choose[:, :, :half], parts,
                    preferred_element_type=jnp.float32).sum(axis=0)
    xb = jnp.einsum("yzbmc,pyzmcl->pyzbl", choose[:, :, half:], parts,
                    preferred_element_type=jnp.float32).sum(axis=0)

    mine = reduce_scatter(xa, xb, ny, nz)

    my_starts = lax.dynamic_index_in_dim(starts, view_place, 0, keepdims=False)
    my_len = lax.dynamic_index_in_dim(order_len, view_place, 0, keepdims=False)
    back = my_starts[:, None] + jnp.arange(chunks_per_row, dtype=jnp.int32)[None, :]
    back = jnp.minimum(back, slots - 1)
    rows = jnp.take(mine, back.reshape(-1), axis=0).reshape(owned, samples)

    table = kernel_table(samples, 0.0, samples)
    recon = invert_block(rows, my_len, table, 0.0)
    return recon[None]


def solution(mesh):
    view_devices = mesh.shape["view"]
    ny = int(round(math.sqrt(view_devices)))
    nz = view_devices // ny
    placed = (P("view", "chord", None), P("view", None, None), P(), P())
    return jax.shard_map(
        functools.partial(per_device, ny, nz),
        mesh=mesh,
        in_specs=placed,
        out_specs=P("chord", "view", None),
        check_vma=False,
    )
```

```python
import functools
import math

import jax
import jax.numpy as jnp
from jax import lax
from jax.experimental import pallas as pl
from jax.experimental.pallas import tpu as pltpu
from jax.sharding import PartitionSpec as P

LANES = 128
PACK = 4608
MESH = pl.DeviceIdType.MESH


def kernel_table(rows, start, cols):
    row_pos = start + jnp.arange(rows, dtype=jnp.float32)[:, None]
    col_pos = jnp.arange(cols, dtype=jnp.float32)[None, :]
    return 1.0 / (row_pos - col_pos + 0.5)


def weigh(length, count, start):
    position = start + jnp.arange(count, dtype=jnp.float32)[None, :] + 0.5
    inside = position < length
    return (inside, jnp.sqrt(jnp.where(inside, position * (length - position), 1.0)))


def invert_block(sums, length, table, start):
    length = length.astype(jnp.float32)[:, None]
    col_in, col_w = weigh(length, sums.shape[1], 0.0)
    row_in, row_w = weigh(length, table.shape[0], start)
    scaled = jnp.where(col_in, col_w * sums, 0.0)
    image = jnp.dot(
        scaled, table.T, precision=lax.Precision.HIGH, preferred_element_type=jnp.float32
    )
    return jnp.where(row_in, image / (math.pi * row_w), 0.0)


def pick(table, index):
    hit = index[:, :, None] == jnp.arange(table.shape[1], dtype=jnp.int32)
    return jnp.sum(jnp.where(hit, table[:, None, :], 0), axis=-1)


def run_rings(rings):
    chains = []
    for r in rings:
        n = r["n"]
        nr = n // 2
        nl = n - 1 - nr
        chains.append((r, 1, nr, r["right"], r["rr"], r["sr"], r["base"]))
        chains.append((r, -1, nl, r["left"], r["rl"], r["sl"], r["base"] + nr))
    pending = [None] * len(chains)
    for s in range(max(c[2] for c in chains)):
        for i, (r, go, steps, to, recv, send, base) in enumerate(chains):
            if s >= steps:
                continue
            n = r["n"]
            dest = lax.rem(r["me"] + go * (steps - s) + 2 * n, n)
            if s == 0:
                src = r["src"](dest)
            else:
                pending[i].wait()
                send[s] = recv[s - 1] + r["val"](dest)
                src = send.at[s]
            copy = pltpu.make_async_remote_copy(
                src_ref=src,
                dst_ref=recv.at[s],
                send_sem=r["ssem"].at[base + s],
                recv_sem=r["rsem"].at[base + s],
                device_id=to,
                device_id_type=MESH,
            )
            copy.start()
            pending[i] = copy
    for copy in pending:
        copy.wait()
    return [(r["rr"].at[r["n"] // 2 - 1], r["rl"].at[r["n"] - 2 - r["n"] // 2]) for r in rings]


def run_direct(rings):
    copies = []
    for r in rings:
        n = r["n"]
        for k in range(1, n):
            dest = lax.rem(r["me"] + k, n)
            copy = pltpu.make_async_remote_copy(
                src_ref=r["chunk"].at[dest],
                dst_ref=r["recv"].at[k - 1],
                send_sem=r["ssem"].at[r["base"] + k - 1],
                recv_sem=r["rsem"].at[r["base"] + k - 1],
                device_id=r["dev"](dest),
                device_id_type=MESH,
            )
            copy.start()
            copies.append(copy)
    for copy in copies:
        copy.wait()


def rs_kernel(ny, nz, ra, x, out, s1a, s1b, *bufs):
    ssem, rsem = bufs[-2:]
    bufs = bufs[:-2]
    view = lax.axis_index("view")
    group = lax.axis_index("chord")
    y = view // nz
    z = lax.rem(view, nz)

    def dev(yy, zz):
        return (yy * nz + zz, group)

    z_right = dev(y, lax.rem(z + 1, nz))
    z_left = dev(y, lax.rem(z + nz - 1, nz))
    y_right = dev(lax.rem(y + 1, ny), z)
    y_left = dev(lax.rem(y + ny - 1, ny), z)

    barrier = pltpu.get_barrier_semaphore()
    for k in range(1, ny):
        pl.semaphore_signal(barrier, inc=1, device_id=dev(lax.rem(y + k, ny), z), device_id_type=MESH)
    for k in range(1, nz):
        pl.semaphore_signal(barrier, inc=1, device_id=dev(y, lax.rem(z + k, nz)), device_id_type=MESH)
    pl.semaphore_wait(barrier, ny + nz - 2)

    rows_a = pl.ds(0, ra)
    rows_b = pl.ds(ra, x.shape[2] - ra)

    def ring(n, me, right, left, x, part, at, base, swap=False):
        rr, rl, sr, sl = bufs[4 * at: 4 * at + 4]
        if swap:
            src, val = (lambda d: x.at[part, d, rows_a]), (lambda d: x[part, d, rows_a])
        else:
            src, val = (lambda d: x.at[d, part, rows_b]), (lambda d: x[d, part, rows_b])
        return dict(n=n, me=me, right=right, left=left, rr=rr, rl=rl, sr=sr, sl=sl,
                    src=src, val=val, ssem=ssem, rsem=rsem, base=base)

    ha, hb = ny // 2, nz // 2
    lo_a, hi_a = pl.ds(0, ha), pl.ds(ha, ny - ha)
    lo_b, hi_b = pl.ds(0, hb), pl.ds(hb, nz - hb)
    fins = run_rings([
        ring(nz, z, z_right, z_left, x, lo_a, 0, 0, swap=True),
        ring(nz, z, z_right, z_left, x, hi_a, 1, nz - 1, swap=True),
        ring(ny, y, y_right, y_left, x, lo_b, 2, 2 * (nz - 1)),
        ring(ny, y, y_right, y_left, x, hi_b, 3, 2 * (nz - 1) + ny - 1),
    ])
    s1a[lo_a] = x[lo_a, z, rows_a] + fins[0][0][...] + fins[0][1][...]
    s1a[hi_a] = x[hi_a, z, rows_a] + fins[1][0][...] + fins[1][1][...]
    s1b[lo_b] = x[y, lo_b, rows_b] + fins[2][0][...] + fins[2][1][...]
    s1b[hi_b] = x[y, hi_b, rows_b] + fins[3][0][...] + fins[3][1][...]
    recv_a, recv_b = bufs[16], bufs[17]
    run_direct([
        dict(n=ny, me=y, dev=lambda d: dev(d, z), chunk=s1a, recv=recv_a,
             ssem=ssem, rsem=rsem, base=2 * (nz + ny - 2)),
        dict(n=nz, me=z, dev=lambda d: dev(y, d), chunk=s1b, recv=recv_b,
             ssem=ssem, rsem=rsem, base=2 * (nz + ny - 2) + ny - 1),
    ])
    out[rows_a, :] = s1a[y] + jnp.sum(recv_a[...], axis=0)
    out[rows_b, :] = s1b[z] + jnp.sum(recv_b[...], axis=0)


def reduce_scatter(x, ra, ny, nz):
    rb = x.shape[2] - ra
    f32 = jnp.float32

    def slots(n, shape):
        return [pltpu.VMEM((n // 2,) + shape, f32), pltpu.VMEM((n - 1 - n // 2,) + shape, f32)] * 2

    ha, hb = ny // 2, nz // 2
    bufs = (
        slots(nz, (ha, ra, LANES)) + slots(nz, (ny - ha, ra, LANES))
        + slots(ny, (hb, rb, LANES)) + slots(ny, (nz - hb, rb, LANES))
        + [pltpu.VMEM((ny - 1, ra, LANES), f32), pltpu.VMEM((nz - 1, rb, LANES), f32)]
    )
    return pl.pallas_call(
        functools.partial(rs_kernel, ny, nz, ra),
        out_shape=jax.ShapeDtypeStruct((ra + rb, LANES), f32),
        in_specs=[pl.BlockSpec(memory_space=pltpu.VMEM)],
        out_specs=pl.BlockSpec(memory_space=pltpu.VMEM),
        scratch_shapes=[pltpu.VMEM((ny, ra, LANES), f32), pltpu.VMEM((nz, rb, LANES), f32)]
        + bufs
        + [pltpu.SemaphoreType.DMA((3 * (nz + ny - 2),)), pltpu.SemaphoreType.DMA((3 * (nz + ny - 2),))],
        compiler_params=pltpu.CompilerParams(collective_id=0, has_side_effects=True),
    )(x)


def sums_kernel(proj_ref, tiles_ref, out_ref):
    views = proj_ref.shape[0]
    samples = tiles_ref.shape[1]
    lhs = jnp.concatenate([proj_ref[v] for v in range(views)], axis=1)
    width = min(samples, 256)
    for cb in range(samples // width):
        cols = pl.ds(cb * width, width)
        total = jnp.dot(lhs, tiles_ref[:, cols], preferred_element_type=jnp.float32)
        hi = total.astype(jnp.bfloat16)
        rest = total - hi.astype(jnp.float32)
        mid = rest.astype(jnp.bfloat16)
        out_ref[0, :, cols] = hi
        out_ref[1, :, cols] = mid
        out_ref[2, :, cols] = (rest - mid.astype(jnp.float32)).astype(jnp.bfloat16)


def owner_sums(proj, tiles):
    tiles = tiles.reshape(-1, tiles.shape[2])
    return pl.pallas_call(
        sums_kernel,
        out_shape=jax.ShapeDtypeStruct((3, proj.shape[1], tiles.shape[1]), jnp.bfloat16),
        in_specs=[pl.BlockSpec(memory_space=pltpu.VMEM)] * 2,
        out_specs=pl.BlockSpec(memory_space=pltpu.VMEM),
    )(proj, tiles)


def per_device(ny, nz, proj, tiles, owner, lengths):
    view_count, group_rows, footprint = proj.shape
    samples = tiles.shape[2]
    group = lax.axis_index("chord")
    view_place = lax.axis_index("view")
    view_devices = ny * nz
    owned = group_rows // view_devices
    chunks_per_row = samples // LANES
    slots = min(chunks_per_row * owned, (PACK + owned * (LANES - 1)) // LANES)

    my_order = lax.dynamic_index_in_dim(owner, group, 0, keepdims=False)
    my_lengths = lax.dynamic_index_in_dim(lengths, group, 0, keepdims=False)
    order_len = pick(my_lengths[None, :], my_order[None, :])
    order_len = order_len.reshape(view_devices, owned)

    perm = (my_order[:, None] == jnp.arange(group_rows, dtype=jnp.int32)[None, :]).astype(proj.dtype)
    proj_ord = jnp.einsum("rk,vkd->vrd", perm, proj, preferred_element_type=jnp.float32)
    sums = owner_sums(proj_ord.astype(proj.dtype), tiles)
    parts = sums.reshape(3, ny, nz, owned, chunks_per_row, LANES)

    counts = (order_len + LANES - 1) // LANES
    ends = jnp.cumsum(counts, axis=1)
    starts = ends - counts
    slot = jnp.arange(slots, dtype=jnp.int32)
    member = jnp.sum((ends[:, None, :] <= slot[None, :, None]).astype(jnp.int32), axis=2)
    member = jnp.minimum(member, owned - 1)
    first = pick(starts, member)
    within = jnp.clip(slot[None, :] - first, 0, chunks_per_row - 1)
    member = member.reshape(ny, nz, slots)
    within = within.reshape(ny, nz, slots)
    half = (slots + 1) // 2
    choose = (
        (member[..., None, None] == jnp.arange(owned, dtype=jnp.int32)[:, None])
        & (within[..., None, None] == jnp.arange(chunks_per_row, dtype=jnp.int32)[None, :])
    ).astype(jnp.float32)
    choose = choose.astype(jnp.bfloat16)
    x = jnp.einsum("yzbmc,pyzmcl->pyzbl", choose, parts,
                   preferred_element_type=jnp.float32).sum(axis=0)

    mine = reduce_scatter(x, half, ny, nz)

    my_starts = lax.dynamic_index_in_dim(starts, view_place, 0, keepdims=False)
    my_len = lax.dynamic_index_in_dim(order_len, view_place, 0, keepdims=False)
    back = my_starts[:, None] + jnp.arange(chunks_per_row, dtype=jnp.int32)[None, :]
    back = jnp.minimum(back, slots - 1)
    rows = jnp.take(mine, back.reshape(-1), axis=0).reshape(owned, samples)

    table = kernel_table(samples, 0.0, samples)
    recon = invert_block(rows, my_len, table, 0.0)
    return recon[None]


def solution(mesh):
    view_devices = mesh.shape["view"]
    ny = int(round(math.sqrt(view_devices)))
    nz = view_devices // ny
    placed = (P("view", "chord", None), P("view", None, None), P(), P())
    return jax.shard_map(
        functools.partial(per_device, ny, nz),
        mesh=mesh,
        in_specs=placed,
        out_specs=P("chord", "view", None),
        check_vma=False,
    )
```

```python
import functools
import math

import jax
import jax.numpy as jnp
from jax import lax
from jax.experimental import pallas as pl
from jax.experimental.pallas import tpu as pltpu
from jax.sharding import PartitionSpec as P

LANES = 128
PACK = 4608
MESH = pl.DeviceIdType.MESH


def kernel_table(rows, start, cols):
    row_pos = start + jnp.arange(rows, dtype=jnp.float32)[:, None]
    col_pos = jnp.arange(cols, dtype=jnp.float32)[None, :]
    return 1.0 / (row_pos - col_pos + 0.5)


def weigh(length, count, start):
    position = start + jnp.arange(count, dtype=jnp.float32)[None, :] + 0.5
    inside = position < length
    return (inside, jnp.sqrt(jnp.where(inside, position * (length - position), 1.0)))


def invert_block(sums, length, table, start):
    length = length.astype(jnp.float32)[:, None]
    col_in, col_w = weigh(length, sums.shape[1], 0.0)
    row_in, row_w = weigh(length, table.shape[0], start)
    scaled = jnp.where(col_in, col_w * sums, 0.0)
    image = jnp.dot(
        scaled, table.T, precision=lax.Precision.HIGH, preferred_element_type=jnp.float32
    )
    return jnp.where(row_in, image / (math.pi * row_w), 0.0)


def pick(table, index):
    hit = index[:, :, None] == jnp.arange(table.shape[1], dtype=jnp.int32)
    return jnp.sum(jnp.where(hit, table[:, None, :], 0), axis=-1)


def run_rings(rings):
    chains = []
    for r in rings:
        n = r["n"]
        nr = n // 2
        nl = n - 1 - nr
        chains.append((r, 1, nr, r["right"], r["rr"], r["sr"], r["base"]))
        chains.append((r, -1, nl, r["left"], r["rl"], r["sl"], r["base"] + nr))
    pending = [None] * len(chains)
    for s in range(max(c[2] for c in chains)):
        for i, (r, go, steps, to, recv, send, base) in enumerate(chains):
            if s >= steps:
                continue
            n = r["n"]
            dest = lax.rem(r["me"] + go * (steps - s) + 2 * n, n)
            if s == 0:
                src = r["src"](dest)
            else:
                pending[i].wait()
                send[s] = recv[s - 1] + r["val"](dest)
                src = send.at[s]
            copy = pltpu.make_async_remote_copy(
                src_ref=src,
                dst_ref=recv.at[s],
                send_sem=r["ssem"].at[base + s],
                recv_sem=r["rsem"].at[base + s],
                device_id=to,
                device_id_type=MESH,
            )
            copy.start()
            pending[i] = copy
    for copy in pending:
        copy.wait()
    return [(r["rr"].at[r["n"] // 2 - 1], r["rl"].at[r["n"] - 2 - r["n"] // 2]) for r in rings]


def run_direct(rings):
    copies = []
    for r in rings:
        n = r["n"]
        for k in range(1, n):
            dest = lax.rem(r["me"] + k, n)
            copy = pltpu.make_async_remote_copy(
                src_ref=r["chunk"].at[dest],
                dst_ref=r["recv"].at[k - 1],
                send_sem=r["ssem"].at[r["base"] + k - 1],
                recv_sem=r["rsem"].at[r["base"] + k - 1],
                device_id=r["dev"](dest),
                device_id_type=MESH,
            )
            copy.start()
            copies.append(copy)
    for copy in copies:
        copy.wait()


def rs_kernel(ny, nz, ra, x, out, s1a, s1b, *bufs):
    ssem, rsem = bufs[-2:]
    bufs = bufs[:-2]
    view = lax.axis_index("view")
    group = lax.axis_index("chord")
    y = view // nz
    z = lax.rem(view, nz)

    def dev(yy, zz):
        return (yy * nz + zz, group)

    z_right = dev(y, lax.rem(z + 1, nz))
    z_left = dev(y, lax.rem(z + nz - 1, nz))
    y_right = dev(lax.rem(y + 1, ny), z)
    y_left = dev(lax.rem(y + ny - 1, ny), z)

    barrier = pltpu.get_barrier_semaphore()
    for k in range(1, ny):
        pl.semaphore_signal(barrier, inc=1, device_id=dev(lax.rem(y + k, ny), z), device_id_type=MESH)
    for k in range(1, nz):
        pl.semaphore_signal(barrier, inc=1, device_id=dev(y, lax.rem(z + k, nz)), device_id_type=MESH)
    pl.semaphore_wait(barrier, ny + nz - 2)

    rows_a = pl.ds(0, ra)
    rows_b = pl.ds(ra, x.shape[2] - ra)

    def ring(n, me, right, left, x, part, at, base, swap=False):
        rr, rl, sr, sl = bufs[4 * at: 4 * at + 4]
        if swap:
            src, val = (lambda d: x.at[part, d, rows_a]), (lambda d: x[part, d, rows_a])
        else:
            src, val = (lambda d: x.at[d, part, rows_b]), (lambda d: x[d, part, rows_b])
        return dict(n=n, me=me, right=right, left=left, rr=rr, rl=rl, sr=sr, sl=sl,
                    src=src, val=val, ssem=ssem, rsem=rsem, base=base)

    ha, hb = ny // 2, nz // 2
    lo_a, hi_a = pl.ds(0, ha), pl.ds(ha, ny - ha)
    lo_b, hi_b = pl.ds(0, hb), pl.ds(hb, nz - hb)
    fins = run_rings([
        ring(nz, z, z_right, z_left, x, lo_a, 0, 0, swap=True),
        ring(nz, z, z_right, z_left, x, hi_a, 1, nz - 1, swap=True),
        ring(ny, y, y_right, y_left, x, lo_b, 2, 2 * (nz - 1)),
        ring(ny, y, y_right, y_left, x, hi_b, 3, 2 * (nz - 1) + ny - 1),
    ])
    s1a[lo_a] = x[lo_a, z, rows_a] + fins[0][0][...] + fins[0][1][...]
    s1a[hi_a] = x[hi_a, z, rows_a] + fins[1][0][...] + fins[1][1][...]
    s1b[lo_b] = x[y, lo_b, rows_b] + fins[2][0][...] + fins[2][1][...]
    s1b[hi_b] = x[y, hi_b, rows_b] + fins[3][0][...] + fins[3][1][...]
    recv_a, recv_b = bufs[16], bufs[17]
    run_direct([
        dict(n=ny, me=y, dev=lambda d: dev(d, z), chunk=s1a, recv=recv_a,
             ssem=ssem, rsem=rsem, base=2 * (nz + ny - 2)),
        dict(n=nz, me=z, dev=lambda d: dev(y, d), chunk=s1b, recv=recv_b,
             ssem=ssem, rsem=rsem, base=2 * (nz + ny - 2) + ny - 1),
    ])
    out[rows_a, :] = s1a[y] + jnp.sum(recv_a[...], axis=0)
    out[rows_b, :] = s1b[z] + jnp.sum(recv_b[...], axis=0)


def reduce_scatter(x, ra, ny, nz):
    rb = x.shape[2] - ra
    f32 = jnp.float32

    def slots(n, shape):
        return [pltpu.VMEM((n // 2,) + shape, f32), pltpu.VMEM((n - 1 - n // 2,) + shape, f32)] * 2

    ha, hb = ny // 2, nz // 2
    bufs = (
        slots(nz, (ha, ra, LANES)) + slots(nz, (ny - ha, ra, LANES))
        + slots(ny, (hb, rb, LANES)) + slots(ny, (nz - hb, rb, LANES))
        + [pltpu.VMEM((ny - 1, ra, LANES), f32), pltpu.VMEM((nz - 1, rb, LANES), f32)]
    )
    return pl.pallas_call(
        functools.partial(rs_kernel, ny, nz, ra),
        out_shape=jax.ShapeDtypeStruct((ra + rb, LANES), f32),
        in_specs=[pl.BlockSpec(memory_space=pltpu.VMEM)],
        out_specs=pl.BlockSpec(memory_space=pltpu.VMEM),
        scratch_shapes=[pltpu.VMEM((ny, ra, LANES), f32), pltpu.VMEM((nz, rb, LANES), f32)]
        + bufs
        + [pltpu.SemaphoreType.DMA((3 * (nz + ny - 2),)), pltpu.SemaphoreType.DMA((3 * (nz + ny - 2),))],
        compiler_params=pltpu.CompilerParams(collective_id=0, has_side_effects=True),
    )(x)


def sums_kernel(proj_ref, tiles_ref, out_ref):
    views = proj_ref.shape[0]
    samples = tiles_ref.shape[1]
    lhs = jnp.concatenate([proj_ref[v] for v in range(views)], axis=1)
    width = min(samples, 256)
    for cb in range(samples // width):
        cols = pl.ds(cb * width, width)
        total = jnp.dot(lhs, tiles_ref[:, cols], preferred_element_type=jnp.float32)
        hi = total.astype(jnp.bfloat16)
        rest = total - hi.astype(jnp.float32)
        mid = rest.astype(jnp.bfloat16)
        out_ref[0, :, cols] = hi
        out_ref[1, :, cols] = mid
        out_ref[2, :, cols] = (rest - mid.astype(jnp.float32)).astype(jnp.bfloat16)


def owner_sums(proj, tiles):
    tiles = tiles.reshape(-1, tiles.shape[2])
    return pl.pallas_call(
        sums_kernel,
        out_shape=jax.ShapeDtypeStruct((3, proj.shape[1], tiles.shape[1]), jnp.bfloat16),
        in_specs=[pl.BlockSpec(memory_space=pltpu.VMEM)] * 2,
        out_specs=pl.BlockSpec(memory_space=pltpu.VMEM),
    )(proj, tiles)


def per_device(ny, nz, proj, tiles, owner, lengths):
    view_count, group_rows, footprint = proj.shape
    samples = tiles.shape[2]
    group = lax.axis_index("chord")
    view_place = lax.axis_index("view")
    view_devices = ny * nz
    owned = group_rows // view_devices
    chunks_per_row = samples // LANES
    slots = min(chunks_per_row * owned, (PACK + owned * (LANES - 1)) // LANES)

    my_order = lax.dynamic_index_in_dim(owner, group, 0, keepdims=False)
    my_lengths = lax.dynamic_index_in_dim(lengths, group, 0, keepdims=False)
    order_len = pick(my_lengths[None, :], my_order[None, :])
    order_len = order_len.reshape(view_devices, owned)

    perm = (my_order[:, None] == jnp.arange(group_rows, dtype=jnp.int32)[None, :]).astype(proj.dtype)
    proj_ord = jnp.einsum("rk,vkd->vrd", perm, proj, preferred_element_type=jnp.float32)
    sums = owner_sums(proj_ord.astype(proj.dtype), tiles)
    parts = sums.reshape(3, ny, nz, owned, chunks_per_row, LANES)

    counts = (order_len + LANES - 1) // LANES
    ends = jnp.cumsum(counts, axis=1)
    starts = ends - counts
    slot = jnp.arange(slots, dtype=jnp.int32)
    member = jnp.sum((ends[:, None, :] <= slot[None, :, None]).astype(jnp.int32), axis=2)
    member = jnp.minimum(member, owned - 1)
    first = pick(starts, member)
    within = jnp.clip(slot[None, :] - first, 0, chunks_per_row - 1)
    member = member.reshape(ny, nz, slots)
    within = within.reshape(ny, nz, slots)
    half = (slots + 1) // 2
    choose = (
        (member[..., None, None] == jnp.arange(owned, dtype=jnp.int32)[:, None])
        & (within[..., None, None] == jnp.arange(chunks_per_row, dtype=jnp.int32)[None, :])
    ).astype(jnp.float32)
    choose = choose.astype(jnp.bfloat16)
    choose = jnp.broadcast_to(choose[:, :, :, None], choose.shape[:3] + (3,) + choose.shape[3:])
    x = jnp.einsum("yzbpmc,pyzmcl->yzbl", choose, parts, preferred_element_type=jnp.float32)

    mine = reduce_scatter(x, half, ny, nz)

    my_starts = lax.dynamic_index_in_dim(starts, view_place, 0, keepdims=False)
    my_len = lax.dynamic_index_in_dim(order_len, view_place, 0, keepdims=False)
    back = my_starts[:, None] + jnp.arange(chunks_per_row, dtype=jnp.int32)[None, :]
    back = jnp.minimum(back, slots - 1)
    rows = jnp.take(mine, back.reshape(-1), axis=0).reshape(owned, samples)

    table = kernel_table(samples, 0.0, samples)
    recon = invert_block(rows, my_len, table, 0.0)
    return recon[None]


def solution(mesh):
    view_devices = mesh.shape["view"]
    ny = int(round(math.sqrt(view_devices)))
    nz = view_devices // ny
    placed = (P("view", "chord", None), P("view", None, None), P(), P())
    return jax.shard_map(
        functools.partial(per_device, ny, nz),
        mesh=mesh,
        in_specs=placed,
        out_specs=P("chord", "view", None),
        check_vma=False,
    )
```

```python
import functools
import math

import jax
import jax.numpy as jnp
from jax import lax
from jax.experimental import pallas as pl
from jax.experimental.pallas import tpu as pltpu
from jax.sharding import PartitionSpec as P

LANES = 128
PACK = 4608
MESH = pl.DeviceIdType.MESH


def kernel_table(rows, start, cols):
    row_pos = start + jnp.arange(rows, dtype=jnp.float32)[:, None]
    col_pos = jnp.arange(cols, dtype=jnp.float32)[None, :]
    return 1.0 / (row_pos - col_pos + 0.5)


def weigh(length, count, start):
    position = start + jnp.arange(count, dtype=jnp.float32)[None, :] + 0.5
    inside = position < length
    return (inside, jnp.sqrt(jnp.where(inside, position * (length - position), 1.0)))


def invert_block(sums, length, table, start):
    length = length.astype(jnp.float32)[:, None]
    col_in, col_w = weigh(length, sums.shape[1], 0.0)
    row_in, row_w = weigh(length, table.shape[0], start)
    scaled = jnp.where(col_in, col_w * sums, 0.0)
    image = jnp.dot(
        scaled, table.T, precision=lax.Precision.HIGH, preferred_element_type=jnp.float32
    )
    return jnp.where(row_in, image / (math.pi * row_w), 0.0)


def pick(table, index):
    hit = index[:, :, None] == jnp.arange(table.shape[1], dtype=jnp.int32)
    return jnp.sum(jnp.where(hit, table[:, None, :], 0), axis=-1)


def run_rings(rings):
    chains = []
    for r in rings:
        n = r["n"]
        nr = n // 2
        nl = n - 1 - nr
        chains.append((r, 1, nr, r["right"], r["rr"], r["sr"], r["base"]))
        chains.append((r, -1, nl, r["left"], r["rl"], r["sl"], r["base"] + nr))
    pending = [None] * len(chains)
    for s in range(max(c[2] for c in chains)):
        for i, (r, go, steps, to, recv, send, base) in enumerate(chains):
            if s >= steps:
                continue
            n = r["n"]
            dest = lax.rem(r["me"] + go * (steps - s) + 2 * n, n)
            if s == 0:
                src = r["src"](dest)
            else:
                pending[i].wait()
                send[s] = recv[s - 1] + r["val"](dest)
                src = send.at[s]
            copy = pltpu.make_async_remote_copy(
                src_ref=src,
                dst_ref=recv.at[s],
                send_sem=r["ssem"].at[base + s],
                recv_sem=r["rsem"].at[base + s],
                device_id=to,
                device_id_type=MESH,
            )
            copy.start()
            pending[i] = copy
    for copy in pending:
        copy.wait()
    return [(r["rr"].at[r["n"] // 2 - 1], r["rl"].at[r["n"] - 2 - r["n"] // 2]) for r in rings]


def run_direct(rings):
    copies = []
    for r in rings:
        n = r["n"]
        for k in range(1, n):
            dest = lax.rem(r["me"] + k, n)
            copy = pltpu.make_async_remote_copy(
                src_ref=r["chunk"].at[dest],
                dst_ref=r["recv"].at[k - 1],
                send_sem=r["ssem"].at[r["base"] + k - 1],
                recv_sem=r["rsem"].at[r["base"] + k - 1],
                device_id=r["dev"](dest),
                device_id_type=MESH,
            )
            copy.start()
            copies.append(copy)
    for copy in copies:
        copy.wait()


def rs_kernel(ny, nz, ra, x, out, s1a, s1b, *bufs):
    ssem, rsem = bufs[-2:]
    bufs = bufs[:-2]
    view = lax.axis_index("view")
    group = lax.axis_index("chord")
    y = view // nz
    z = lax.rem(view, nz)

    def dev(yy, zz):
        return (yy * nz + zz, group)

    z_right = dev(y, lax.rem(z + 1, nz))
    z_left = dev(y, lax.rem(z + nz - 1, nz))
    y_right = dev(lax.rem(y + 1, ny), z)
    y_left = dev(lax.rem(y + ny - 1, ny), z)

    barrier = pltpu.get_barrier_semaphore()
    for k in range(1, ny):
        pl.semaphore_signal(barrier, inc=1, device_id=dev(lax.rem(y + k, ny), z), device_id_type=MESH)
    for k in range(1, nz):
        pl.semaphore_signal(barrier, inc=1, device_id=dev(y, lax.rem(z + k, nz)), device_id_type=MESH)
    pl.semaphore_wait(barrier, ny + nz - 2)

    rows_a = pl.ds(0, ra)
    rows_b = pl.ds(ra, x.shape[2] - ra)

    def ring(n, me, right, left, x, part, at, base, swap=False):
        rr, rl, sr, sl = bufs[4 * at: 4 * at + 4]
        if swap:
            src, val = (lambda d: x.at[part, d, rows_a]), (lambda d: x[part, d, rows_a])
        else:
            src, val = (lambda d: x.at[d, part, rows_b]), (lambda d: x[d, part, rows_b])
        return dict(n=n, me=me, right=right, left=left, rr=rr, rl=rl, sr=sr, sl=sl,
                    src=src, val=val, ssem=ssem, rsem=rsem, base=base)

    ha, hb = ny // 2, nz // 2
    lo_a, hi_a = pl.ds(0, ha), pl.ds(ha, ny - ha)
    lo_b, hi_b = pl.ds(0, hb), pl.ds(hb, nz - hb)
    fins = run_rings([
        ring(nz, z, z_right, z_left, x, lo_a, 0, 0, swap=True),
        ring(nz, z, z_right, z_left, x, hi_a, 1, nz - 1, swap=True),
        ring(ny, y, y_right, y_left, x, lo_b, 2, 2 * (nz - 1)),
        ring(ny, y, y_right, y_left, x, hi_b, 3, 2 * (nz - 1) + ny - 1),
    ])
    s1a[lo_a] = x[lo_a, z, rows_a] + fins[0][0][...] + fins[0][1][...]
    s1a[hi_a] = x[hi_a, z, rows_a] + fins[1][0][...] + fins[1][1][...]
    s1b[lo_b] = x[y, lo_b, rows_b] + fins[2][0][...] + fins[2][1][...]
    s1b[hi_b] = x[y, hi_b, rows_b] + fins[3][0][...] + fins[3][1][...]
    recv_a, recv_b = bufs[16], bufs[17]
    run_direct([
        dict(n=ny, me=y, dev=lambda d: dev(d, z), chunk=s1a, recv=recv_a,
             ssem=ssem, rsem=rsem, base=2 * (nz + ny - 2)),
        dict(n=nz, me=z, dev=lambda d: dev(y, d), chunk=s1b, recv=recv_b,
             ssem=ssem, rsem=rsem, base=2 * (nz + ny - 2) + ny - 1),
    ])
    out[rows_a, :] = s1a[y] + jnp.sum(recv_a[...], axis=0)
    out[rows_b, :] = s1b[z] + jnp.sum(recv_b[...], axis=0)


def reduce_scatter(x, ra, ny, nz):
    rb = x.shape[2] - ra
    f32 = jnp.float32

    def slots(n, shape):
        return [pltpu.VMEM((n // 2,) + shape, f32), pltpu.VMEM((n - 1 - n // 2,) + shape, f32)] * 2

    ha, hb = ny // 2, nz // 2
    bufs = (
        slots(nz, (ha, ra, LANES)) + slots(nz, (ny - ha, ra, LANES))
        + slots(ny, (hb, rb, LANES)) + slots(ny, (nz - hb, rb, LANES))
        + [pltpu.VMEM((ny - 1, ra, LANES), f32), pltpu.VMEM((nz - 1, rb, LANES), f32)]
    )
    return pl.pallas_call(
        functools.partial(rs_kernel, ny, nz, ra),
        out_shape=jax.ShapeDtypeStruct((ra + rb, LANES), f32),
        in_specs=[pl.BlockSpec(memory_space=pltpu.VMEM)],
        out_specs=pl.BlockSpec(memory_space=pltpu.VMEM),
        scratch_shapes=[pltpu.VMEM((ny, ra, LANES), f32), pltpu.VMEM((nz, rb, LANES), f32)]
        + bufs
        + [pltpu.SemaphoreType.DMA((3 * (nz + ny - 2),)), pltpu.SemaphoreType.DMA((3 * (nz + ny - 2),))],
        compiler_params=pltpu.CompilerParams(collective_id=0, has_side_effects=True),
    )(x)


def sums_kernel(proj_ref, tiles_ref, out_ref):
    views = proj_ref.shape[0]
    samples = tiles_ref.shape[1]
    lhs = jnp.concatenate([proj_ref[v] for v in range(views)], axis=1)
    width = min(samples, 256)
    for cb in range(samples // width):
        cols = pl.ds(cb * width, width)
        total = jnp.dot(lhs, tiles_ref[:, cols], preferred_element_type=jnp.float32)
        hi = total.astype(jnp.bfloat16)
        rest = total - hi.astype(jnp.float32)
        mid = rest.astype(jnp.bfloat16)
        out_ref[0, :, cols] = hi
        out_ref[1, :, cols] = mid
        out_ref[2, :, cols] = (rest - mid.astype(jnp.float32)).astype(jnp.bfloat16)


def owner_sums(proj, tiles):
    tiles = tiles.reshape(-1, tiles.shape[2])
    return pl.pallas_call(
        sums_kernel,
        out_shape=jax.ShapeDtypeStruct((3, proj.shape[1], tiles.shape[1]), jnp.bfloat16),
        in_specs=[pl.BlockSpec(memory_space=pltpu.VMEM)] * 2,
        out_specs=pl.BlockSpec(memory_space=pltpu.VMEM),
    )(proj, tiles)


def per_device(ny, nz, proj, tiles, owner, lengths):
    view_count, group_rows, footprint = proj.shape
    samples = tiles.shape[2]
    group = lax.axis_index("chord")
    view_place = lax.axis_index("view")
    view_devices = ny * nz
    owned = group_rows // view_devices
    chunks_per_row = samples // LANES
    slots = min(chunks_per_row * owned, (PACK + owned * (LANES - 1)) // LANES)

    my_order = lax.dynamic_index_in_dim(owner, group, 0, keepdims=False)
    my_lengths = lax.dynamic_index_in_dim(lengths, group, 0, keepdims=False)
    order_len = pick(my_lengths[None, :], my_order[None, :])
    order_len = order_len.reshape(view_devices, owned)

    perm = (my_order[:, None] == jnp.arange(group_rows, dtype=jnp.int32)[None, :]).astype(proj.dtype)
    proj_ord = jnp.einsum("rk,vkd->vrd", perm, proj, preferred_element_type=jnp.float32)
    sums = owner_sums(proj_ord.astype(proj.dtype), tiles)
    parts = sums.reshape(3, ny, nz, owned, chunks_per_row, LANES)

    counts = (order_len + LANES - 1) // LANES
    ends = jnp.cumsum(counts, axis=1)
    starts = ends - counts
    slot = jnp.arange(slots, dtype=jnp.int32)
    member = jnp.sum((ends[:, None, :] <= slot[None, :, None]).astype(jnp.int32), axis=2)
    member = jnp.minimum(member, owned - 1)
    first = pick(starts, member)
    within = jnp.clip(slot[None, :] - first, 0, chunks_per_row - 1)
    member = member.reshape(ny, nz, slots)
    within = within.reshape(ny, nz, slots)
    half = (slots + 1) // 2
    choose = (
        (member[..., None, None] == jnp.arange(owned, dtype=jnp.int32)[:, None])
        & (within[..., None, None] == jnp.arange(chunks_per_row, dtype=jnp.int32)[None, :])
    ).astype(jnp.float32)
    choose = choose.astype(jnp.bfloat16)
    x = jnp.einsum("yzbmc,pyzmcl->pyzbl", choose, parts,
                   preferred_element_type=jnp.float32).sum(axis=0)

    mine = reduce_scatter(x, half, ny, nz)

    my_starts = lax.dynamic_index_in_dim(starts, view_place, 0, keepdims=False)
    my_len = lax.dynamic_index_in_dim(order_len, view_place, 0, keepdims=False)
    back = my_starts[:, None] + jnp.arange(chunks_per_row, dtype=jnp.int32)[None, :]
    back = jnp.minimum(back, slots - 1)
    rows = jnp.take(mine, back, axis=0, mode="clip")

    length = my_len.astype(jnp.float32)[:, None, None]
    position = (
        jnp.arange(chunks_per_row, dtype=jnp.float32)[:, None] * LANES
        + jnp.arange(LANES, dtype=jnp.float32)[None, :]
    )[None] + 0.5
    col_in = position < length
    col_w = jnp.sqrt(jnp.where(col_in, position * (length - position), 1.0))
    scaled = jnp.where(col_in, col_w * rows, 0.0)
    row_pos = jnp.arange(samples, dtype=jnp.float32)[:, None, None]
    table = 1.0 / (row_pos - (position - 0.5) + 0.5)
    image = jnp.einsum("mcl,pcl->mp", scaled, table, precision=lax.Precision.HIGH,
                       preferred_element_type=jnp.float32)
    row_in, row_w = weigh(my_len.astype(jnp.float32)[:, None], samples, 0.0)
    recon = jnp.where(row_in, image / (math.pi * row_w), 0.0)
    return recon[None]


def solution(mesh):
    view_devices = mesh.shape["view"]
    ny = int(round(math.sqrt(view_devices)))
    nz = view_devices // ny
    placed = (P("view", "chord", None), P("view", None, None), P(), P())
    return jax.shard_map(
        functools.partial(per_device, ny, nz),
        mesh=mesh,
        in_specs=placed,
        out_specs=P("chord", "view", None),
        check_vma=False,
    )
```

```python
import functools
import math

import jax
import jax.numpy as jnp
from jax import lax
from jax.experimental import pallas as pl
from jax.experimental.pallas import tpu as pltpu
from jax.sharding import PartitionSpec as P

LANES = 128
PACK = 4608
MESH = pl.DeviceIdType.MESH


def kernel_table(rows, start, cols):
    row_pos = start + jnp.arange(rows, dtype=jnp.float32)[:, None]
    col_pos = jnp.arange(cols, dtype=jnp.float32)[None, :]
    return 1.0 / (row_pos - col_pos + 0.5)


def weigh(length, count, start):
    position = start + jnp.arange(count, dtype=jnp.float32)[None, :] + 0.5
    inside = position < length
    return (inside, jnp.sqrt(jnp.where(inside, position * (length - position), 1.0)))


def invert_block(sums, length, table, start):
    length = length.astype(jnp.float32)[:, None]
    col_in, col_w = weigh(length, sums.shape[1], 0.0)
    row_in, row_w = weigh(length, table.shape[0], start)
    scaled = jnp.where(col_in, col_w * sums, 0.0)
    image = jnp.dot(
        scaled, table.T, precision=lax.Precision.HIGH, preferred_element_type=jnp.float32
    )
    return jnp.where(row_in, image / (math.pi * row_w), 0.0)


def pick(table, index):
    hit = index[:, :, None] == jnp.arange(table.shape[1], dtype=jnp.int32)
    return jnp.sum(jnp.where(hit, table[:, None, :], 0), axis=-1)


def run_rings(rings):
    chains = []
    for r in rings:
        n = r["n"]
        nr = n // 2
        nl = n - 1 - nr
        chains.append((r, 1, nr, r["right"], r["rr"], r["sr"], r["base"]))
        chains.append((r, -1, nl, r["left"], r["rl"], r["sl"], r["base"] + nr))
    pending = [None] * len(chains)
    for s in range(max(c[2] for c in chains)):
        for i, (r, go, steps, to, recv, send, base) in enumerate(chains):
            if s >= steps:
                continue
            n = r["n"]
            dest = lax.rem(r["me"] + go * (steps - s) + 2 * n, n)
            if s == 0:
                src = r["src"](dest)
            else:
                pending[i].wait()
                send[s] = recv[s - 1] + r["val"](dest)
                src = send.at[s]
            copy = pltpu.make_async_remote_copy(
                src_ref=src,
                dst_ref=recv.at[s],
                send_sem=r["ssem"].at[base + s],
                recv_sem=r["rsem"].at[base + s],
                device_id=to,
                device_id_type=MESH,
            )
            copy.start()
            pending[i] = copy
    for copy in pending:
        copy.wait()
    return [(r["rr"].at[r["n"] // 2 - 1], r["rl"].at[r["n"] - 2 - r["n"] // 2]) for r in rings]


def run_direct(rings):
    copies = []
    for r in rings:
        n = r["n"]
        for k in range(1, n):
            dest = lax.rem(r["me"] + k, n)
            copy = pltpu.make_async_remote_copy(
                src_ref=r["chunk"].at[dest],
                dst_ref=r["recv"].at[k - 1],
                send_sem=r["ssem"].at[r["base"] + k - 1],
                recv_sem=r["rsem"].at[r["base"] + k - 1],
                device_id=r["dev"](dest),
                device_id_type=MESH,
            )
            copy.start()
            copies.append(copy)
    for copy in copies:
        copy.wait()


def rs_kernel(ny, nz, ra, x, out, s1a, s1b, *bufs):
    ssem, rsem = bufs[-2:]
    bufs = bufs[:-2]
    view = lax.axis_index("view")
    group = lax.axis_index("chord")
    y = view // nz
    z = lax.rem(view, nz)

    def dev(yy, zz):
        return (yy * nz + zz, group)

    z_right = dev(y, lax.rem(z + 1, nz))
    z_left = dev(y, lax.rem(z + nz - 1, nz))
    y_right = dev(lax.rem(y + 1, ny), z)
    y_left = dev(lax.rem(y + ny - 1, ny), z)

    barrier = pltpu.get_barrier_semaphore()
    for k in range(1, ny):
        pl.semaphore_signal(barrier, inc=1, device_id=dev(lax.rem(y + k, ny), z), device_id_type=MESH)
    for k in range(1, nz):
        pl.semaphore_signal(barrier, inc=1, device_id=dev(y, lax.rem(z + k, nz)), device_id_type=MESH)
    pl.semaphore_wait(barrier, ny + nz - 2)

    rows_a = pl.ds(0, ra)
    rows_b = pl.ds(ra, x.shape[2] - ra)

    def ring(n, me, right, left, x, part, at, base, swap=False):
        rr, rl, sr, sl = bufs[4 * at: 4 * at + 4]
        if swap:
            src, val = (lambda d: x.at[part, d, rows_a]), (lambda d: x[part, d, rows_a])
        else:
            src, val = (lambda d: x.at[d, part, rows_b]), (lambda d: x[d, part, rows_b])
        return dict(n=n, me=me, right=right, left=left, rr=rr, rl=rl, sr=sr, sl=sl,
                    src=src, val=val, ssem=ssem, rsem=rsem, base=base)

    ha, hb = ny // 2, nz // 2
    lo_a, hi_a = pl.ds(0, ha), pl.ds(ha, ny - ha)
    lo_b, hi_b = pl.ds(0, hb), pl.ds(hb, nz - hb)
    fins = run_rings([
        ring(nz, z, z_right, z_left, x, lo_a, 0, 0, swap=True),
        ring(nz, z, z_right, z_left, x, hi_a, 1, nz - 1, swap=True),
        ring(ny, y, y_right, y_left, x, lo_b, 2, 2 * (nz - 1)),
        ring(ny, y, y_right, y_left, x, hi_b, 3, 2 * (nz - 1) + ny - 1),
    ])
    s1a[lo_a] = x[lo_a, z, rows_a] + fins[0][0][...] + fins[0][1][...]
    s1a[hi_a] = x[hi_a, z, rows_a] + fins[1][0][...] + fins[1][1][...]
    s1b[lo_b] = x[y, lo_b, rows_b] + fins[2][0][...] + fins[2][1][...]
    s1b[hi_b] = x[y, hi_b, rows_b] + fins[3][0][...] + fins[3][1][...]
    recv_a, recv_b = bufs[16], bufs[17]
    run_direct([
        dict(n=ny, me=y, dev=lambda d: dev(d, z), chunk=s1a, recv=recv_a,
             ssem=ssem, rsem=rsem, base=2 * (nz + ny - 2)),
        dict(n=nz, me=z, dev=lambda d: dev(y, d), chunk=s1b, recv=recv_b,
             ssem=ssem, rsem=rsem, base=2 * (nz + ny - 2) + ny - 1),
    ])
    out[rows_a, :] = s1a[y] + jnp.sum(recv_a[...], axis=0)
    out[rows_b, :] = s1b[z] + jnp.sum(recv_b[...], axis=0)


def reduce_scatter(x, ra, ny, nz):
    rb = x.shape[2] - ra
    f32 = jnp.float32

    def slots(n, shape):
        return [pltpu.VMEM((n // 2,) + shape, f32), pltpu.VMEM((n - 1 - n // 2,) + shape, f32)] * 2

    ha, hb = ny // 2, nz // 2
    bufs = (
        slots(nz, (ha, ra, LANES)) + slots(nz, (ny - ha, ra, LANES))
        + slots(ny, (hb, rb, LANES)) + slots(ny, (nz - hb, rb, LANES))
        + [pltpu.VMEM((ny - 1, ra, LANES), f32), pltpu.VMEM((nz - 1, rb, LANES), f32)]
    )
    return pl.pallas_call(
        functools.partial(rs_kernel, ny, nz, ra),
        out_shape=jax.ShapeDtypeStruct((ra + rb, LANES), f32),
        in_specs=[pl.BlockSpec(memory_space=pltpu.VMEM)],
        out_specs=pl.BlockSpec(memory_space=pltpu.VMEM),
        scratch_shapes=[pltpu.VMEM((ny, ra, LANES), f32), pltpu.VMEM((nz, rb, LANES), f32)]
        + bufs
        + [pltpu.SemaphoreType.DMA((3 * (nz + ny - 2),)), pltpu.SemaphoreType.DMA((3 * (nz + ny - 2),))],
        compiler_params=pltpu.CompilerParams(collective_id=0, has_side_effects=True),
    )(x)


def sums_kernel(proj_ref, tiles_ref, out_ref):
    views = proj_ref.shape[0]
    samples = tiles_ref.shape[1]
    lhs = jnp.concatenate([proj_ref[v] for v in range(views)], axis=1)
    width = min(samples, 256)
    for cb in range(samples // width):
        cols = pl.ds(cb * width, width)
        total = jnp.dot(lhs, tiles_ref[:, cols], preferred_element_type=jnp.float32)
        hi = total.astype(jnp.bfloat16)
        rest = total - hi.astype(jnp.float32)
        mid = rest.astype(jnp.bfloat16)
        out_ref[0, :, cols] = hi
        out_ref[1, :, cols] = mid
        out_ref[2, :, cols] = (rest - mid.astype(jnp.float32)).astype(jnp.bfloat16)


def owner_sums(proj, tiles):
    tiles = tiles.reshape(-1, tiles.shape[2])
    return pl.pallas_call(
        sums_kernel,
        out_shape=jax.ShapeDtypeStruct((3, proj.shape[1], tiles.shape[1]), jnp.bfloat16),
        in_specs=[pl.BlockSpec(memory_space=pltpu.VMEM)] * 2,
        out_specs=pl.BlockSpec(memory_space=pltpu.VMEM),
    )(proj, tiles)


def per_device(ny, nz, proj, tiles, owner, lengths):
    view_count, group_rows, footprint = proj.shape
    samples = tiles.shape[2]
    group = lax.axis_index("chord")
    view_place = lax.axis_index("view")
    view_devices = ny * nz
    owned = group_rows // view_devices
    chunks_per_row = samples // LANES
    slots = min(chunks_per_row * owned, (PACK + owned * (LANES - 1)) // LANES)

    my_order = lax.dynamic_index_in_dim(owner, group, 0, keepdims=False)
    my_lengths = lax.dynamic_index_in_dim(lengths, group, 0, keepdims=False)
    order_len = pick(my_lengths[None, :], my_order[None, :])
    order_len = order_len.reshape(view_devices, owned)

    perm = (my_order[:, None] == jnp.arange(group_rows, dtype=jnp.int32)[None, :]).astype(proj.dtype)
    proj_ord = jnp.einsum("rk,vkd->vrd", perm, proj, preferred_element_type=jnp.float32)
    sums = owner_sums(proj_ord.astype(proj.dtype), tiles)
    parts = sums.reshape(3, ny, nz, owned, chunks_per_row, LANES)

    counts = (order_len + LANES - 1) // LANES
    ends = jnp.cumsum(counts, axis=1)
    starts = ends - counts
    slot = jnp.arange(slots, dtype=jnp.int32)
    member = jnp.sum((ends[:, None, :] <= slot[None, :, None]).astype(jnp.int32), axis=2)
    member = jnp.minimum(member, owned - 1)
    first = pick(starts, member)
    within = jnp.clip(slot[None, :] - first, 0, chunks_per_row - 1)
    member = member.reshape(ny, nz, slots)
    within = within.reshape(ny, nz, slots)
    half = (slots + 1) // 2
    choose = (
        (member[..., None, None] == jnp.arange(owned, dtype=jnp.int32)[:, None])
        & (within[..., None, None] == jnp.arange(chunks_per_row, dtype=jnp.int32)[None, :])
    ).astype(jnp.float32)
    choose = choose.astype(jnp.bfloat16)
    x = jnp.einsum("yzbmc,pyzmcl->pyzbl", choose, parts,
                   preferred_element_type=jnp.float32).sum(axis=0)

    mine = reduce_scatter(x, half, ny, nz)

    my_starts = lax.dynamic_index_in_dim(starts, view_place, 0, keepdims=False)
    my_len = lax.dynamic_index_in_dim(order_len, view_place, 0, keepdims=False)
    back = my_starts[:, None] + jnp.arange(chunks_per_row, dtype=jnp.int32)[None, :]
    back = jnp.minimum(back, slots - 1)
    hit = (back[:, :, None] == jnp.arange(slots, dtype=jnp.int32)).astype(jnp.float32)
    rows = jnp.einsum("mcj,jl->mcl", hit, mine, precision=lax.Precision.HIGHEST,
                      preferred_element_type=jnp.float32)

    length = my_len.astype(jnp.float32)[:, None, None]
    position = (
        jnp.arange(chunks_per_row, dtype=jnp.float32)[:, None] * LANES
        + jnp.arange(LANES, dtype=jnp.float32)[None, :]
    )[None] + 0.5
    col_in = position < length
    col_w = jnp.sqrt(jnp.where(col_in, position * (length - position), 1.0))
    scaled = jnp.where(col_in, col_w * rows, 0.0)
    row_pos = jnp.arange(samples, dtype=jnp.float32)[:, None, None]
    table = 1.0 / (row_pos - (position - 0.5) + 0.5)
    image = jnp.einsum("mcl,pcl->mp", scaled, table, precision=lax.Precision.HIGH,
                       preferred_element_type=jnp.float32)
    row_in, row_w = weigh(my_len.astype(jnp.float32)[:, None], samples, 0.0)
    recon = jnp.where(row_in, image / (math.pi * row_w), 0.0)
    return recon[None]


def solution(mesh):
    view_devices = mesh.shape["view"]
    ny = int(round(math.sqrt(view_devices)))
    nz = view_devices // ny
    placed = (P("view", "chord", None), P("view", None, None), P(), P())
    return jax.shard_map(
        functools.partial(per_device, ny, nz),
        mesh=mesh,
        in_specs=placed,
        out_specs=P("chord", "view", None),
        check_vma=False,
    )
```
